128 devices in a mesh: pages: 4 (over y), blk: 32 (over z, x, core).
Axes of the slice: x: 4, y: 4, z: 4, core: 2. Of those that a mesh axis runs over, the one named last changes fastest.
Arguments:
- new_hidden: bfloat16 [128, 6144], P('pages', 'blk'), may hold values from -6 to 6
- attn_gain: float32 [6144], replicated, may hold values from 0.1 to 1.9
- mlp_gain: float32 [6144], replicated, may hold values from 0.1 to 1.9
- qkv_weight: bfloat16 [6144, 18432], P(None, 'blk'), may hold values from -0.078125 to 0.078125
- dense_weight: bfloat16 [6144, 6144], P('blk'), may hold values from -0.078125 to 0.078125
- in_weight: bfloat16 [6144, 24576], P(None, ('pages', 'blk')), may hold values from -0.078125 to 0.078125
- out_weight: bfloat16 [24576, 6144], P(('pages', 'blk')), may hold values from -0.15625 to 0.15625
- page_store: bfloat16 [1536, 16, 12288], P(('pages', 'blk')), may hold values from -420 to 420
- held_states: bfloat16 [128, 8, 6144], P(('pages', 'blk')), may hold values from -6 to 6
- fold_weights: float32 [8, 16], replicated, may hold values from 0.02 to 0.14
- page_table: int32 [128, 12], replicated, may hold values from 0 to 1535, as said below
- lengths: int32 [128], P('pages'), may hold values from 81 to 192, as said below
- keep_slots: int32 [128, 5], P('pages'), may hold values from 0 to 11, as said below
- fold_index: int32 [128, 12], P('pages'), may hold values from 0 to 7
- recompute_list: int32 [128, 8], P('pages'), may hold values from 0 to 79, as said below
Outputs:
- update: bfloat16 [128, 6144], P('pages', 'blk')
- folded: bfloat16 [128, 12, 12288], P('pages', None, 'blk')
The draws below stay inside these ranges and needn't reach their ends.
Inputs may be any that keep to these rules, and one draw needn't show every extreme that they name: `page_table`: every page id appears exactly once; the device of index s along pages+blk holds pages s*12 to s*12 + 11, and exactly 3 of them belong to requests of each group of 32 consecutive requests. `lengths`: one request in every draw holds 192 tokens. `keep_slots`: A request's kept slots are distinct, ascending, and all below lengths // 16. `recompute_list`: A request's entries are distinct and ascending.
All inputs are finite; a program needn't handle non-finite values.
Results may differ from the reference program's by a relative error of at most 0.024.
Values may be sent and summed in bfloat16 or wider, within the bound.
A program may use at most 128 MiB of HBM per device.

```python
import math
import jax
import jax.numpy as jnp
from jax import lax

D = 6144
H = 64
HD = 96
FF = 24576
ROT = 24
PAGE = 16
PPR = 12
KP = 5
NREC = 8
NF = 8
RG = 32
R = 128
PD = 12
PGD = 3
NPAGES = 1536


def draw_page_store(key, part):
    first_key = jax.random.fold_in(jax.random.fold_in(key, 5), 0)
    shape = (NPAGES, PAGE, 2 * D)
    values = jnp.clip(jax.random.normal(first_key, shape, jnp.float32), -6.0, 6.0)
    return values.astype(jnp.bfloat16)


def draw_page_table(key, part):
    first_key, second_key = jax.random.split(jax.random.fold_in(key, 11))
    owners = NPAGES // PD
    groups = R // RG
    local_slots = jnp.tile(jnp.arange(PD, dtype=jnp.int32)[None, :], (owners, 1))
    local_slots = jax.random.permutation(first_key, local_slots, axis=1, independent=True)
    page_ids = jnp.arange(owners, dtype=jnp.int32)[:, None] * PD + local_slots
    page_ids = page_ids.reshape(owners, groups, PGD).transpose(1, 0, 2).reshape(groups, owners * PGD)
    page_ids = jax.random.permutation(second_key, page_ids, axis=1, independent=True)
    return page_ids.reshape(R, PPR).astype(jnp.int32)


def length_helper(key):
    first_key, second_key, third_key = jax.random.split(jax.random.fold_in(key, 31), 3)
    counts = jax.random.randint(first_key, (R,), KP * PAGE + 1, PPR * PAGE + 1)
    longest = jax.random.randint(second_key, (), 0, R)
    shortest = (longest + 1 + jax.random.randint(third_key, (), 0, R - 1)) % R
    row_ids = jnp.arange(R)
    counts = jnp.where(row_ids == longest, PPR * PAGE, counts)
    counts = jnp.where(row_ids == shortest, KP * PAGE + 1, counts)
    return counts.astype(jnp.int32)


def draw_lengths(key, part):
    return length_helper(key)


def draw_keep_slots(key, part):
    counts = length_helper(key)
    full_pages = counts // PAGE
    slot_ids = jnp.arange(PPR, dtype=jnp.int32)
    scores = jax.random.randint(jax.random.fold_in(key, 41), (R, PPR), 0, 1 << 20) * PPR + slot_ids[None, :]
    scores = jnp.where(slot_ids[None, :] < full_pages[:, None], scores, (1 << 20) * PPR + slot_ids[None, :])
    chosen = jnp.argsort(scores, axis=1)[:, :KP]
    return jnp.sort(chosen, axis=1).astype(jnp.int32)


def draw_recompute_list(key, part):
    kept_count = KP * PAGE
    scores = jax.random.randint(jax.random.fold_in(key, 53), (R, kept_count), 0, 1 << 20) * kept_count + jnp.arange(kept_count, dtype=jnp.int32)[None, :]
    chosen = jnp.argsort(scores, axis=1)[:, :NREC]
    return jnp.sort(chosen, axis=1).astype(jnp.int32)


def with_ends(result, key, smallest, largest):
    dims = result.shape
    spot = [jax.random.randint(jax.random.fold_in(key, axis), (), 0, dims[axis]) for axis in range(len(dims))]
    result = result.at[tuple(spot)].set(smallest)
    longest = dims.index(max(dims))
    spot[longest] = (spot[longest] + 1) % dims[longest]
    return result.at[tuple(spot)].set(largest)


def strengthened(array, stream_key, source, target, blocks, factor):
    def block_of(axis_at):
        return (jnp.arange(array.shape[axis_at]) // (array.shape[axis_at] // blocks)).reshape((-1,) + (1,) * (array.ndim - 1 - axis_at))

    first = jax.random.permutation(stream_key, blocks)[block_of(target)]
    other_side = (block_of(target) + blocks // 2) % blocks
    return jnp.where((block_of(source) == first) | (block_of(source) == other_side), factor * array, array)


def block_scale(stream_key, dims, shards, smallest, top_value):
    def one(axis_at, shards_of):
        steps = jax.random.uniform(jax.random.fold_in(jax.random.fold_in(stream_key, 6), axis_at), (shards_of,), jnp.float32, smallest / len(shards), top_value / len(shards))
        return jnp.repeat(jnp.exp(steps), dims[axis_at] // shards_of).reshape((-1,) + (1,) * (len(dims) - axis_at - 1))

    loudness = one(*shards[0])
    for cut in shards[1:]:
        loudness = loudness * one(*cut)
    return loudness


def normal_values(stream_key, extent, deviation, most, pieces=(), held_as=jnp.bfloat16):
    result = deviation * jax.random.normal(stream_key, extent, jnp.float32)
    if pieces:
        result = result * block_scale(stream_key, extent, pieces, -0.22, 0.18)
    return jnp.clip(result, -most, most).astype(held_as)


def gaussian_with(key, extent, scale, most, cuts, heavy, kind=jnp.bfloat16):
    values = scale * jax.random.normal(key, extent, jnp.float32)
    if cuts:
        values = values * block_scale(key, extent, cuts, -0.22, 0.18)
    return jnp.clip(strengthened(values, jax.random.fold_in(key, 3), *heavy), -most, most).astype(kind)


def setup_inputs(seed: int = 0) -> dict:
    key_list = jax.random.split(jax.random.key(seed), 16)
    return {
        "new_hidden": normal_values(key_list[0], (R, D), 1.0, 6.0, ((0, 4), (1, 32))),
        "attn_gain": jnp.clip(1.0 + 0.18 * jax.random.normal(key_list[1], (D,), jnp.float32), 0.1, 1.9),
        "mlp_gain": jnp.clip(1.0 + 0.18 * jax.random.normal(key_list[2], (D,), jnp.float32), 0.1, 1.9),
        "qkv_weight": normal_values(key_list[3], (D, 3 * D), D ** -0.5, 0.078125, ((1, 32),)),
        "dense_weight": normal_values(key_list[4], (D, D), D ** -0.5, 0.078125, ((0, 32),)),
        "in_weight": normal_values(key_list[5], (D, FF), D ** -0.5, 0.078125, ((1, 128),)),
        "out_weight": gaussian_with(key_list[6], (FF, D), FF ** -0.5, 0.15625, ((0, 128),), (0, 1, 128, 5.5)),
        "page_store": draw_page_store(jax.random.fold_in(key_list[15], 71), 0),
        "held_states": normal_values(key_list[8], (R, NREC, D), 1.0, 6.0, ((0, 128),)),
        "fold_weights": jnp.clip(jax.random.uniform(key_list[9], (NF, PAGE), jnp.float32, 0.02, 0.14), 0.02, 0.14),
        "page_table": draw_page_table(jax.random.fold_in(key_list[15], 71), 0),
        "lengths": draw_lengths(jax.random.fold_in(key_list[15], 71), 0),
        "keep_slots": draw_keep_slots(jax.random.fold_in(key_list[15], 71), 0),
        "fold_index": with_ends(jax.random.randint(key_list[13], (R, PPR), 0, NF), jax.random.fold_in(key_list[13], 1), 0, NF - 1).astype(jnp.int32),
        "recompute_list": draw_recompute_list(jax.random.fold_in(key_list[15], 71), 0),
    }


EPSILON = 1e-05
ROT_BASE = 10000.0

def layer_norm(values, scale_gain):
    values = values.astype(jnp.float32)
    centered = values - lax.optimization_barrier(jnp.mean(values, axis=-1, keepdims=True))
    spread = lax.optimization_barrier(jnp.mean(centered * centered, axis=-1, keepdims=True))
    return centered * lax.rsqrt(spread + EPSILON) * scale_gain

def rotate(values, positions):
    half_rot = ROT // 2
    frequency = ROT_BASE ** (-2.0 * jnp.arange(half_rot, dtype=jnp.float32) / ROT)
    angles = positions.astype(jnp.float32)[..., None] * frequency
    cos_part = jnp.cos(angles)
    sin_part = jnp.sin(angles)
    lower_part = values[..., :half_rot]
    upper_part = values[..., half_rot:ROT]
    return jnp.concatenate([lower_part * cos_part - upper_part * sin_part, upper_part * cos_part + lower_part * sin_part, values[..., ROT:]], axis=-1)

def reference(new_hidden, attn_gain, mlp_gain, qkv_weight, dense_weight, in_weight, out_weight, page_store, held_states, fold_weights, page_table, lengths, keep_slots, fold_index, recompute_list):
    scale = 1.0 / math.sqrt(HD)
    normed_attn = layer_norm(new_hidden, attn_gain).astype(jnp.bfloat16)
    normed_mlp = layer_norm(new_hidden, mlp_gain).astype(jnp.bfloat16)
    projected = jnp.dot(normed_attn, qkv_weight, preferred_element_type=jnp.float32).reshape(R, H, 3, HD)
    new_pos = lengths[:, None]
    query = rotate(projected[:, :, 0], new_pos).astype(jnp.bfloat16)
    new_key = rotate(projected[:, :, 1], new_pos).astype(jnp.bfloat16)
    new_value = projected[:, :, 2].astype(jnp.bfloat16)
    key_weight = qkv_weight.reshape(D, H, 3, HD)[:, :, 1, :].reshape(D, D)
    normed_held = layer_norm(held_states.reshape(R * NREC, D), attn_gain).astype(jnp.bfloat16)
    fresh = jnp.dot(normed_held, key_weight, preferred_element_type=jnp.float32).reshape(R, NREC, H, HD)
    rec_slot = jnp.take_along_axis(keep_slots, recompute_list // PAGE, axis=1)
    rec_pos = rec_slot * PAGE + recompute_list % PAGE
    fresh = rotate(fresh, rec_pos[:, :, None]).astype(jnp.bfloat16)
    slot_ids = jnp.arange(PPR, dtype=jnp.int32)
    token_ids = jnp.arange(PAGE, dtype=jnp.int32)
    kept_ids = jnp.arange(KP * PAGE, dtype=jnp.int32)

    def one_request(request_items):
        table_row, length, keep_row, fold_row, rec_row, query_row, key_row, value_row, fresh_row = request_items
        page_rows = page_store[table_row]
        split_rows = page_rows.reshape(PPR, PAGE, H, 2, HD)
        kept = split_rows[keep_row].reshape(KP * PAGE, H, 2, HD)
        hits = (rec_row[:, None] == kept_ids[None, :]).astype(jnp.float32)
        touched = lax.optimization_barrier(jnp.sum(hits, axis=0)) > 0.5
        placed = jnp.einsum('nk,nhd->khd', hits, fresh_row.astype(jnp.float32))
        keys = jnp.where(touched[:, None, None], placed, kept[:, :, 0].astype(jnp.float32))
        values = kept[:, :, 1].astype(jnp.float32)
        is_kept = jnp.any(keep_row[:, None] == slot_ids[None, :], axis=0)
        dropped = jnp.logical_and(jnp.logical_not(is_kept), slot_ids * PAGE < length)
        live = slot_ids[:, None] * PAGE + token_ids[None, :] < length
        weight_rows = jnp.where(jnp.logical_and(live, dropped[:, None]), fold_weights[fold_row], 0.0)
        folded_row = jnp.einsum('jt,jtc->jc', weight_rows, page_rows.astype(jnp.float32), precision=lax.Precision.HIGHEST).astype(jnp.bfloat16)
        fold_pairs = folded_row.reshape(PPR, H, 2, HD).astype(jnp.float32)
        query_f = query_row.astype(jnp.float32)
        kept_scores = jnp.einsum('hd,khd->hk', query_f, keys) * scale
        fold_scores = jnp.einsum('hd,jhd->hj', query_f, fold_pairs[:, :, 0]) * scale
        fold_scores = jnp.where(dropped[None, :], fold_scores, -1e+30)
        own_score = lax.optimization_barrier(jnp.sum(query_f * key_row.astype(jnp.float32), axis=-1)) * scale
        top = jnp.maximum(jnp.maximum(lax.optimization_barrier(jnp.max(kept_scores, axis=-1)), lax.optimization_barrier(jnp.max(fold_scores, axis=-1))), own_score)
        kept_exp = jnp.exp(kept_scores - top[:, None])
        fold_exp = jnp.exp(fold_scores - top[:, None])
        own_exp = jnp.exp(own_score - top)
        total = lax.optimization_barrier(jnp.sum(kept_exp, axis=-1)) + lax.optimization_barrier(jnp.sum(fold_exp, axis=-1)) + own_exp
        kept_prob = (kept_exp / total[:, None]).astype(jnp.bfloat16).astype(jnp.float32)
        fold_prob = (fold_exp / total[:, None]).astype(jnp.bfloat16).astype(jnp.float32)
        own_prob = (own_exp / total).astype(jnp.bfloat16).astype(jnp.float32)
        mixed = jnp.einsum('hk,khd->hd', kept_prob, values) + jnp.einsum('hj,jhd->hd', fold_prob, fold_pairs[:, :, 1]) + own_prob[:, None] * value_row.astype(jnp.float32)
        return (mixed.reshape(D).astype(jnp.bfloat16), folded_row)
    attended, folded = lax.map(one_request, (page_table, lengths, keep_slots, fold_index, recompute_list, query, new_key, new_value, fresh))
    attn_part = jnp.dot(attended, dense_weight, preferred_element_type=jnp.float32)
    activated = jax.nn.gelu(jnp.dot(normed_mlp, in_weight, preferred_element_type=jnp.float32), approximate=False).astype(jnp.bfloat16)
    mlp_part = jnp.dot(activated, out_weight, preferred_element_type=jnp.float32)
    return ((attn_part + mlp_part).astype(jnp.bfloat16), folded)
```

```python
import functools
import math

import jax
import jax.numpy as jnp
from jax import lax
from jax.experimental import pallas as pl
from jax.experimental.pallas import tpu as pltpu
from jax.sharding import PartitionSpec as P

D = 6144
H = 64
HD = 96
ROT = 24
PAGE = 16
PPR = 12
KP = 5
NREC = 8
NF = 8
PAIR = 2 * HD
EPSILON = 1e-05
ROT_BASE = 10000.0
MESH = pl.DeviceIdType.MESH
VMEM_SPEC = pl.BlockSpec(memory_space=pltpu.VMEM)


def layer_norm(values, scale_gain):
    values = values.astype(jnp.float32)
    centered = values - jnp.mean(values, axis=-1, keepdims=True)
    spread = jnp.mean(centered * centered, axis=-1, keepdims=True)
    return centered * lax.rsqrt(spread + EPSILON) * scale_gain


def rotate(values, positions):
    half_rot = ROT // 2
    frequency = ROT_BASE ** (-2.0 * jnp.arange(half_rot, dtype=jnp.float32) / ROT)
    angles = positions.astype(jnp.float32)[..., None] * frequency
    cos_part = jnp.cos(angles)
    sin_part = jnp.sin(angles)
    lower_part = values[..., :half_rot]
    upper_part = values[..., half_rot:ROT]
    return jnp.concatenate(
        [
            lower_part * cos_part - upper_part * sin_part,
            upper_part * cos_part + lower_part * sin_part,
            values[..., ROT:],
        ],
        axis=-1,
    )


def device_of(index, n_blk):
    return {"pages": lax.div(index, n_blk), "blk": lax.rem(index, n_blk)}


def greet(count, peer):
    barrier = pltpu.get_barrier_semaphore()

    def signal(step, carry):
        pl.semaphore_signal(barrier, inc=1, device_id=peer(step), device_id_type=MESH)
        return carry

    lax.fori_loop(0, count, signal, 0)
    pl.semaphore_wait(barrier, count)


def exchange_kernel(n_pages, n_blk, src, dst, send_sem, recv_sem, own_sem):
    total = n_pages * n_blk
    me = lax.axis_index("pages") * n_blk + lax.axis_index("blk")

    def peer(step):
        return device_of(lax.rem(me + 1 + step, total), n_blk)

    own = pltpu.make_async_copy(src.at[me], dst.at[me], own_sem)
    own.start()
    greet(total - 1, peer)

    def send(step, carry):
        other = lax.rem(me + 1 + step, total)
        pltpu.make_async_remote_copy(
            src_ref=src.at[other],
            dst_ref=dst.at[me],
            send_sem=send_sem,
            recv_sem=recv_sem,
            device_id=device_of(other, n_blk),
            device_id_type=MESH,
        ).start()
        return carry

    lax.fori_loop(0, total - 1, send, 0)
    own.wait()
    rest = pl.ds(0, total - 1)
    pltpu.make_async_copy(src.at[rest], src.at[rest], send_sem).wait()
    pltpu.make_async_copy(dst.at[rest], dst.at[rest], recv_sem).wait()


def exchange(values, n_pages, n_blk, number):
    return pl.pallas_call(
        functools.partial(exchange_kernel, n_pages, n_blk),
        out_shape=jax.ShapeDtypeStruct(values.shape, values.dtype),
        in_specs=[VMEM_SPEC],
        out_specs=VMEM_SPEC,
        scratch_shapes=[pltpu.SemaphoreType.DMA] * 3,
        compiler_params=pltpu.CompilerParams(collective_id=number, has_side_effects=True, vmem_limit_bytes=48 << 20),
        name="exchange%d" % number,
    )(values)


def gather_kernel(x_ref, held_ref, w_ref, xall, hbuf, wall, own_sem, xs, xr, x2s, x2r, x3s, x3r,
                  as1, ar1, bs1, br1, as2, ar2, bs2, br2, cs, cr, ds, dr, ws, wr):
    y = lax.axis_index("pages")
    b = lax.axis_index("blk")
    z = lax.div(b, 8)
    x = lax.rem(lax.div(b, 2), 4)
    c = lax.rem(b, 2)
    half = held_ref.shape[1] // 2
    lanes_a = pl.ds(0, half)
    lanes_b = pl.ds(half, half)

    def plane_peer(step):
        return {"pages": y, "blk": lax.rem(b + 1 + step, 32)}

    def y_peer(step):
        return {"pages": lax.rem(y + 1 + step, 4), "blk": b}

    def x_peer(step):
        return {"pages": y, "blk": z * 8 + lax.rem(x + 1 + step, 4) * 2 + c}

    def z_peer(step):
        return {"pages": y, "blk": lax.rem(z + 1 + step, 4) * 8 + x * 2 + c}

    partner = {"pages": y, "blk": b + 1 - 2 * c}

    own_x = pltpu.make_async_copy(x_ref, xall.at[y, b], own_sem.at[0])
    own_h = pltpu.make_async_copy(held_ref, hbuf.at[z, x, c], own_sem.at[1])
    own_w = pltpu.make_async_copy(w_ref.at[y], wall.at[y], own_sem.at[2])
    own_x.start()
    own_h.start()
    own_w.start()

    barrier = pltpu.get_barrier_semaphore()

    def hello_plane(step, carry):
        pl.semaphore_signal(barrier, inc=1, device_id=plane_peer(step), device_id_type=MESH)
        return carry

    def hello_y(step, carry):
        pl.semaphore_signal(barrier, inc=1, device_id=y_peer(step), device_id_type=MESH)
        return carry

    lax.fori_loop(0, 31, hello_plane, 0)
    lax.fori_loop(0, 3, hello_y, 0)
    pl.semaphore_wait(barrier, 34)

    def remote(src, dst, s, r, dev):
        return pltpu.make_async_remote_copy(
            src_ref=src, dst_ref=dst, send_sem=s, recv_sem=r, device_id=dev, device_id_type=MESH
        )

    def send_x(step, carry):
        remote(x_ref, xall.at[y, b], xs, xr, plane_peer(step)).start()
        return carry

    lax.fori_loop(0, 31, send_x, 0)
    w_sends = []
    for step in range(3):
        other = lax.rem(y + 1 + step, 4)
        cp = remote(w_ref.at[other], wall.at[y], ws.at[step], wr.at[step], y_peer(step))
        cp.start()
        w_sends.append(cp)
    a1 = [remote(held_ref.at[:, lanes_a], hbuf.at[z, x, c, :, lanes_a], as1.at[s], ar1.at[s], x_peer(s)) for s in range(3)]
    b1 = [remote(held_ref.at[:, lanes_b], hbuf.at[z, x, c, :, lanes_b], bs1.at[s], br1.at[s], z_peer(s)) for s in range(3)]
    for s in range(3):
        a1[s].start()
        b1[s].start()

    rest = pl.ds(0, 31)
    own_x.wait()
    pltpu.make_async_copy(xall.at[0, rest], xall.at[0, rest], xr).wait()
    mine = pl.ds(c * 16, 16)
    x2 = [remote(xall.at[y, mine], xall.at[y, mine], x2s.at[s], x2r.at[s], y_peer(s)) for s in range(3)]
    for cp in x2:
        cp.start()
    own_h.wait()
    for s in range(3):
        a1[s].wait_recv()
    a2 = [remote(hbuf.at[z, :, c, :, lanes_a], hbuf.at[z, :, c, :, lanes_a], as2.at[s], ar2.at[s], z_peer(s)) for s in range(3)]
    for cp in a2:
        cp.start()
    for s in range(3):
        b1[s].wait_recv()
    b2 = [remote(hbuf.at[:, x, c, :, lanes_b], hbuf.at[:, x, c, :, lanes_b], bs2.at[s], br2.at[s], x_peer(s)) for s in range(3)]
    for cp in b2:
        cp.start()
    swaps = [
        remote(hbuf.at[z, :, c, :, lanes_a], hbuf.at[z, :, c, :, lanes_a], cs.at[3], cr.at[3], partner),
        remote(hbuf.at[:, x, c, :, lanes_b], hbuf.at[:, x, c, :, lanes_b], ds.at[3], dr.at[3], partner),
    ]
    for cp in swaps:
        cp.start()
    x3 = []
    for s in range(3):
        x2[s].wait_recv()
        back = lax.rem(y + 3 - s, 4)
        cp = remote(xall.at[back, mine], xall.at[back, mine], x3s.at[s], x3r.at[s], partner)
        cp.start()
        x3.append(cp)
    for s in range(3):
        a2[s].wait_recv()
        back = lax.rem(z + 3 - s, 4)
        cp = remote(hbuf.at[back, :, c, :, lanes_a], hbuf.at[back, :, c, :, lanes_a], cs.at[s], cr.at[s], partner)
        cp.start()
        swaps.append(cp)
        b2[s].wait_recv()
        back = lax.rem(x + 3 - s, 4)
        cp = remote(hbuf.at[:, back, c, :, lanes_b], hbuf.at[:, back, c, :, lanes_b], ds.at[s], dr.at[s], partner)
        cp.start()
        swaps.append(cp)
    own_w.wait()
    pltpu.make_async_copy(xall.at[0, rest], xall.at[0, rest], xs).wait()
    for cp in w_sends + x3 + swaps:
        cp.wait()
    for cp in a1 + b1 + x2 + a2 + b2:
        cp.wait_send()


def gather_inputs(x, held, w):
    three = pltpu.SemaphoreType.DMA((3,))
    four = pltpu.SemaphoreType.DMA((4,))
    one = pltpu.SemaphoreType.DMA
    return pl.pallas_call(
        gather_kernel,
        out_shape=[
            jax.ShapeDtypeStruct((4, 32) + x.shape, x.dtype),
            jax.ShapeDtypeStruct((4, 4, 2) + held.shape, held.dtype),
            jax.ShapeDtypeStruct(w.shape, w.dtype),
        ],
        in_specs=[VMEM_SPEC] * 3,
        out_specs=[VMEM_SPEC] * 3,
        scratch_shapes=[three, one, one] + [three] * 4 + [three] * 8 + [four] * 4 + [three] * 2,
        compiler_params=pltpu.CompilerParams(collective_id=0, has_side_effects=True, vmem_limit_bytes=48 << 20),
        name="gather_inputs",
    )(x, held, w)


def page_kernel(scale, t_ref, tt_ref, m_ref, e_ref, f_ref, page_ref, out_ref):
    m = jnp.dot(t_ref[...], m_ref[0], preferred_element_type=jnp.float32).astype(jnp.bfloat16)
    page = page_ref[...]
    rows, lanes = m.shape
    tokens = page.shape[0]
    lane = lax.broadcasted_iota(jnp.int32, (rows, lanes), 1)
    token = lax.broadcasted_iota(jnp.int32, (rows, tokens), 1)
    row = lax.broadcasted_iota(jnp.int32, (rows, tokens), 0)
    own = jnp.logical_and(token >= row * PAGE, token < row * PAGE + PAGE)
    result = jnp.zeros((rows, lanes), jnp.float32)
    for i in range(2):
        base = i * PAIR
        is_key = jnp.logical_and(lane >= base, lane < base + HD)
        is_value = jnp.logical_and(lane >= base + HD, lane < base + PAIR)
        query = jnp.where(is_key, m, jnp.zeros_like(m))
        scores = scale * lax.dot_general(query, page, (((1,), (1,)), ((), ())), preferred_element_type=jnp.float32)
        fresh = jnp.dot(m, e_ref[i], preferred_element_type=jnp.float32)
        flag = jnp.dot(m, f_ref[i], preferred_element_type=jnp.float32)
        scores = jnp.where(flag > 0.5, fresh, scores)
        scores = jnp.where(own, scores, -1e30)
        top = jnp.max(scores, axis=1, keepdims=True)
        top_hi = top.astype(jnp.bfloat16).astype(jnp.float32)
        top_lo = (top - top_hi).astype(jnp.bfloat16).astype(jnp.float32)
        part = jnp.where(own, jnp.exp(scores - (top_hi + top_lo)), 0.0)
        total = jnp.sum(part, axis=1, keepdims=True)
        total_hi = total.astype(jnp.bfloat16).astype(jnp.float32)
        mixed = jnp.dot(part.astype(jnp.bfloat16), page, preferred_element_type=jnp.float32)
        result = jnp.where(is_value, mixed, result)
        result = jnp.where(lane == base, top_hi, result)
        result = jnp.where(lane == base + 1, top_lo, result)
        result = jnp.where(lane == base + 2, total_hi, result)
        result = jnp.where(lane == base + 3, total - total_hi, result)
    out_ref[0] = jnp.dot(tt_ref[...], result.astype(jnp.bfloat16), preferred_element_type=jnp.float32).astype(jnp.bfloat16)


def page_attention(to_local, to_place, rows, spread, flags, pages, scale):
    chunks, count, width = rows.shape
    tokens = pages.shape[0]
    whole = lambda *shape: pl.BlockSpec(shape, lambda i: (0,) * len(shape))
    return pl.pallas_call(
        functools.partial(page_kernel, scale),
        grid=(chunks,),
        out_shape=jax.ShapeDtypeStruct(rows.shape, jnp.bfloat16),
        in_specs=[
            whole(count, count),
            whole(count, count),
            pl.BlockSpec((1, count, width), lambda i: (i, 0, 0)),
            whole(2, width, tokens),
            whole(2, width, tokens),
            pl.BlockSpec((tokens, width), lambda i: (0, i)),
        ],
        out_specs=pl.BlockSpec((1, count, width), lambda i: (i, 0, 0)),
        name="page_attention",
    )(to_local, to_place, rows, spread, flags, pages)


def on_device(
    new_hidden,
    attn_gain,
    mlp_gain,
    qkv_weight,
    dense_weight,
    in_weight,
    out_weight,
    page_store,
    held_states,
    fold_weights,
    page_table,
    lengths,
    keep_slots,
    fold_index,
    recompute_list,
):
    n_pages = lax.axis_size("pages")
    n_blk = lax.axis_size("blk")
    group = lax.axis_index("pages")
    blk = lax.axis_index("blk")
    device = group * n_blk + blk
    n_devices = n_pages * n_blk
    rows = lengths.shape[0]
    heads = H // n_blk
    width = heads * 2 * HD
    pages_dev = page_store.shape[0]
    per_group = pages_dev // n_pages
    slots = rows * PPR
    scale = 1.0 / math.sqrt(HD)
    f32, bf16 = jnp.float32, jnp.bfloat16
    iota = lambda n: jnp.arange(n, dtype=jnp.int32)

    my_table = lax.dynamic_slice_in_dim(page_table, group * rows, rows, 0)
    ids = my_table.T.reshape(slots)
    rank = jnp.sum((ids[None, :] < ids[:, None]).astype(jnp.int32), axis=1)
    place = rank // per_group * 4 + rank % per_group
    route = (place[:, None] == iota(n_devices * 4)[None, :]).astype(bf16)
    owner = jnp.sum(
        jnp.where(page_table.reshape(1, -1) == (device * pages_dev + iota(16))[:, None], iota(n_devices * pages_dev)[None, :] // slots, 0),
        axis=1,
    )
    owner = jnp.where(iota(16) < pages_dev, owner, -1)
    earlier = jnp.sum(jnp.logical_and(owner[None, :] == owner[:, None], iota(16)[None, :] < iota(16)[:, None]).astype(jnp.int32), axis=1)
    local_place = jnp.where(owner >= 0, owner * 4 + earlier, -1)
    to_local = (local_place[:, None] == iota(16)[None, :]).astype(bf16)

    slot_ids = iota(PPR)[:, None]
    is_kept = jnp.any(keep_slots[None, :, :] == slot_ids[:, :, None], axis=2)
    dropped = jnp.logical_and(jnp.logical_not(is_kept), slot_ids * PAGE < lengths[None, :])
    live = slot_ids[:, :, None] * PAGE + iota(PAGE)[None, None, :] < lengths[None, :, None]
    choose = (fold_index.T[:, :, None] == iota(NF)[None, None, :]).astype(f32)
    weight_rows = jnp.sum(choose[:, :, :, None] * fold_weights[None, None], axis=2)
    weight_rows = jnp.where(jnp.logical_and(live, dropped[:, :, None]), weight_rows, 0.0).reshape(slots, PAGE)
    column = (iota(n_pages)[:, None] * n_blk + blk) * 4 + iota(4)[None, :]
    mine = (column.reshape(-1)[:, None] == place[None, :]).astype(f32)
    weight_out = jnp.einsum("cs,st->ct", mine, weight_rows, precision=lax.Precision.HIGHEST)
    weight_out = jnp.pad(weight_out.reshape(n_pages, 4, PAGE), ((0, 0), (0, 4), (0, 128 - PAGE)))

    held_normed = layer_norm(held_states.reshape(NREC, D), attn_gain).astype(bf16)
    everyone, held_all, weight_in = gather_inputs(new_hidden, held_normed, weight_out)

    weight_local = jnp.einsum(
        "lp,pt->lt", to_local.astype(f32), weight_in[:, :4, :PAGE].reshape(16, PAGE), precision=lax.Precision.HIGHEST
    )[:pages_dev]
    folded_local = jnp.einsum("pt,ptc->pc", weight_local, page_store.astype(f32), precision=lax.Precision.HIGHEST).astype(bf16)
    folded_out = jnp.einsum("lp,lc->pc", to_local[:pages_dev], folded_local, preferred_element_type=f32).astype(bf16)
    folded_out = folded_out.reshape(n_pages, 4, n_blk, width).transpose(0, 2, 1, 3).reshape(n_devices, 4, width)

    raw_rows = everyone.transpose(0, 2, 1, 3).reshape(n_pages * rows, D)
    own_rows = lax.dynamic_slice_in_dim(raw_rows, group * rows, rows, 0)
    normed_attn = layer_norm(own_rows, attn_gain).astype(bf16)
    normed_mlp = layer_norm(raw_rows, mlp_gain).astype(bf16)
    key_weight = qkv_weight.reshape(D, heads, 3, HD)[:, :, 1, :].reshape(D, heads * HD)
    fresh_keys = jnp.dot(held_all.reshape(rows * NREC, D), key_weight, preferred_element_type=f32)
    rec_slot = jnp.take_along_axis(keep_slots, recompute_list // PAGE, axis=1)
    rec_pos = rec_slot * PAGE + recompute_list % PAGE
    fresh_keys = rotate(fresh_keys.reshape(rows, NREC, heads, HD), rec_pos[:, :, None]).astype(bf16)
    projected = jnp.dot(normed_attn, qkv_weight, preferred_element_type=f32).reshape(rows, heads, 3, HD)
    new_pos = lengths[:, None]
    query = rotate(projected[:, :, 0], new_pos).astype(bf16)
    new_key = rotate(projected[:, :, 1], new_pos).astype(bf16)
    new_value = projected[:, :, 2].astype(bf16)
    own_score = jnp.sum(query.astype(f32) * new_key.astype(f32), axis=-1) * scale

    fresh_scores = jnp.sum(query.astype(f32)[:, None] * fresh_keys.astype(f32), axis=-1) * scale
    at_token = jnp.logical_and(
        rec_slot[None, :, :, None] == iota(PPR)[:, None, None, None],
        (recompute_list % PAGE)[None, :, :, None] == iota(PAGE)[None, None, None, :],
    )
    flag = jnp.any(at_token, axis=2)
    fresh_at = jnp.sum(
        jnp.where(at_token[:, :, :, None, :], fresh_scores[None, :, :, :, None], 0.0), axis=2
    )
    fresh_hi = lax.reduce_precision(fresh_at, 8, 7)
    fresh_lo = fresh_at - fresh_hi
    flag = jnp.broadcast_to(flag[:, :, None, :], fresh_at.shape).astype(bf16)
    side = jnp.concatenate([fresh_hi.astype(bf16), fresh_lo.astype(bf16), flag, jnp.zeros(flag.shape[:-1] + (HD - 3 * PAGE,), bf16)], axis=-1)
    query_side = jnp.stack([jnp.broadcast_to(query[None], side.shape), side], axis=3).reshape(slots, width)
    query_out = jnp.einsum("sp,sc->pc", route, query_side, preferred_element_type=f32).astype(bf16)
    query_in = exchange(query_out.reshape(n_devices, 4, width), n_pages, n_blk, 1)

    lane = iota(width)
    spread = []
    flags = []
    for i in range(heads):
        t = lane - (i * PAIR + HD)
        tok = iota(pages_dev * PAGE)[None, :] % PAGE
        spread.append(jnp.logical_or(t[:, None] == tok, t[:, None] == tok + PAGE))
        flags.append(t[:, None] == tok + 2 * PAGE)
    spread = jnp.stack(spread).astype(bf16)
    flags = jnp.stack(flags).astype(bf16)
    query_rows = query_in.reshape(n_pages, n_blk, 4, width).transpose(1, 0, 2, 3).reshape(n_blk, 16, width)
    parts = page_attention(to_local, to_local.T, query_rows, spread, flags, page_store.reshape(pages_dev * PAGE, 2 * D), scale)
    parts_out = parts.reshape(n_blk, n_pages, 4, width).transpose(1, 0, 2, 3).reshape(n_devices, 4, width)
    back = exchange(jnp.concatenate([parts_out, folded_out], axis=2), n_pages, n_blk, 2)
    slot_rows = jnp.dot(route, back.reshape(n_devices * 4, 2 * width), preferred_element_type=f32)
    folded = slot_rows[:, width:].astype(bf16).reshape(PPR, rows, width)
    parts = slot_rows[:, :width].reshape(PPR, rows, heads, 2, HD)
    folded_out = folded.transpose(1, 0, 2)

    fold_pairs = folded.reshape(PPR, rows, heads, 2, HD).astype(f32)
    fold_scores = jnp.sum(query.astype(f32)[None] * fold_pairs[:, :, :, 0], axis=-1) * scale
    fold_scores = jnp.where(dropped[:, :, None], fold_scores, -1e30)
    part_top = jnp.where(is_kept[:, :, None], parts[:, :, :, 0, 0] + parts[:, :, :, 0, 1], -1e30)
    part_total = parts[:, :, :, 0, 2] + parts[:, :, :, 0, 3]
    top = jnp.maximum(jnp.maximum(jnp.max(part_top, axis=0), jnp.max(fold_scores, axis=0)), own_score)
    part_scale = jnp.where(is_kept[:, :, None], jnp.exp(part_top - top[None]), 0.0)
    fold_exp = jnp.exp(fold_scores - top[None])
    own_exp = jnp.exp(own_score - top)
    total = jnp.sum(part_scale * part_total, axis=0) + jnp.sum(fold_exp, axis=0) + own_exp
    mixed = jnp.sum(part_scale[..., None] * parts[:, :, :, 1], axis=0)
    mixed = mixed + jnp.sum(fold_exp[..., None] * fold_pairs[:, :, :, 1], axis=0)
    mixed = mixed + own_exp[..., None] * new_value.astype(f32)
    attended = (mixed / total[..., None]).reshape(rows, heads * HD).astype(bf16)
    attn_part = jnp.dot(attended, dense_weight, preferred_element_type=f32)

    activated = jax.nn.gelu(jnp.dot(normed_mlp, in_weight, preferred_element_type=f32), approximate=False).astype(bf16)
    mlp_part = jnp.dot(activated, out_weight, preferred_element_type=f32).reshape(n_pages, rows, D)
    is_mine = (iota(n_pages) == group)[:, None, None]
    part = (mlp_part + jnp.where(is_mine, attn_part[None], 0.0)).astype(bf16)
    part = part.reshape(n_pages, rows, n_blk, D // n_blk).transpose(0, 2, 1, 3).reshape(n_devices, rows, D // n_blk)
    arrived = exchange(part, n_pages, n_blk, 3)
    summed = jnp.sum(arrived.astype(f32), axis=0).astype(bf16)
    return (summed, folded_out)


def solution(mesh):
    in_specs = (
        P("pages", "blk"),
        P(),
        P(),
        P(None, "blk"),
        P("blk", None),
        P(None, ("pages", "blk")),
        P(("pages", "blk"), None),
        P(("pages", "blk"), None, None),
        P(("pages", "blk"), None, None),
        P(),
        P(),
        P("pages"),
        P("pages", None),
        P("pages", None),
        P("pages", None),
    )
    out_specs = (P("pages", "blk"), P("pages", None, "blk"))
    return jax.shard_map(
        on_device, mesh=mesh, in_specs=in_specs, out_specs=out_specs, check_vma=False
    )
```

```python
import functools
import math

import jax
import jax.numpy as jnp
import numpy as np
from jax import lax
from jax.experimental import pallas as pl
from jax.experimental.pallas import tpu as pltpu
from jax.sharding import PartitionSpec as P

D = 6144
H = 64
HD = 96
ROT = 24
PAGE = 16
PPR = 12
KP = 5
NREC = 8
NF = 8
PAIR = 2 * HD
EPSILON = 1e-05
ROT_BASE = 10000.0
MESH = pl.DeviceIdType.MESH
VMEM_SPEC = pl.BlockSpec(memory_space=pltpu.VMEM)


CHUNK = 2 * PAIR


def rotary_rows(lanes, starts):
    out = np.zeros((8, lanes), np.float32)
    half = ROT // 2
    freq = (np.float32(ROT_BASE) ** (np.float32(-2.0) * np.arange(half, dtype=np.float32) / np.float32(ROT))).astype(np.float32)
    for start in starts:
        out[0, start : start + half] = freq
        out[0, start + half : start + ROT] = freq
        out[1, start + half : start + ROT] = 1.0
        out[2, start : start + half] = 1.0
    return out


def rotated(values, position, rows):
    lanes = values.shape[1]
    angle = position * rows[0:1]
    sine = jnp.sin(angle)
    return (
        values * jnp.cos(angle)
        + pltpu.roll(values, ROT // 2, 1) * (sine * rows[1:2])
        - pltpu.roll(values, lanes - ROT // 2, 1) * (sine * rows[2:3])
    )


def normed(values):
    centered = values - jnp.mean(values, axis=-1, keepdims=True)
    spread = jnp.mean(centered * centered, axis=-1, keepdims=True)
    return centered * lax.rsqrt(spread + EPSILON)


def times(left, right):
    return lax.dot_general(left, right, (((1,), (1,)), ((), ())), preferred_element_type=jnp.float32)


def high(values):
    return values.astype(jnp.bfloat16).astype(jnp.float32)


def step_kernel(
    scale,
    x_ref, held_ref, again_ref, mgain_ref, w_ref, own_ref, route_ref, place_ref, repeat_ref, spread_ref, tile_ref,
    turn_ref, fturn_ref, length_ref, rpos_ref, rtok_ref, kept_ref, drop_ref,
    qkv_hbm, dense_hbm, in_hbm, out_hbm, page_hbm,
    sum_ref, fold_ref,
    wq, wkv, wk, dense, inw, outw, page, xb, xg, nattn, mall, hbuf, wall, wexp, qb, ks,
    qsend, qin, fsend, fin, rsend, rin, mp, mrecv, ysend, yrecv, apart, asend, arecv, tsend, trecv, oall,
    load, xs, xr, x2s, x2r, x3s, x3r, as1, ar1, bs1, br1, as2, ar2, bs2, br2, cs, cr, ds, dr, ws, wr,
    qs, qr, fs, fr, rs, rr, ms, mr, ys, yr, ats, atr, ts, tr, os, orr, owns,
):
    f32, bf16 = jnp.float32, jnp.bfloat16
    y = lax.axis_index("pages")
    b = lax.axis_index("blk")
    me = y * 32 + b
    z = lax.div(b, 8)
    x = lax.rem(lax.div(b, 2), 4)
    c = lax.rem(b, 2)
    chip = lax.div(b, 2)

    loads = [
        pltpu.make_async_copy(page_hbm, page, load.at[0]),
        pltpu.make_async_copy(qkv_hbm.at[pl.ds(0, PAIR)], wq.at[pl.ds(0, PAIR)], load.at[1]),
        pltpu.make_async_copy(qkv_hbm.at[pl.ds(288, PAIR)], wq.at[pl.ds(PAIR, PAIR)], load.at[5]),
        pltpu.make_async_copy(qkv_hbm.at[pl.ds(HD, PAIR)], wkv.at[pl.ds(0, PAIR)], load.at[6]),
        pltpu.make_async_copy(qkv_hbm.at[pl.ds(288 + HD, PAIR)], wkv.at[pl.ds(PAIR, PAIR)], load.at[7]),
        pltpu.make_async_copy(qkv_hbm.at[pl.ds(HD, HD)], wk.at[pl.ds(0, HD)], load.at[8]),
        pltpu.make_async_copy(qkv_hbm.at[pl.ds(288 + HD, HD)], wk.at[pl.ds(HD, HD)], load.at[9]),
        pltpu.make_async_copy(in_hbm, inw, load.at[2]),
        pltpu.make_async_copy(out_hbm, outw, load.at[3]),
        pltpu.make_async_copy(dense_hbm, dense, load.at[4]),
    ]
    for cp in loads:
        cp.start()

    barrier = pltpu.get_barrier_semaphore()

    def hello(step, carry):
        other = lax.rem(me + 1 + step, 128)
        pl.semaphore_signal(barrier, inc=1, device_id={"pages": lax.div(other, 32), "blk": lax.rem(other, 32)}, device_id_type=MESH)
        return carry

    lax.fori_loop(0, 127, hello, 0)
    hbuf[c, z, x] = (normed(held_ref[...].astype(f32)) * again_ref[...]).astype(bf16)
    xb[b] = x_ref[...]
    wall[y] = w_ref[y]
    pl.semaphore_wait(barrier, 127)

    def remote(src, dst, s, r, pages_id, blk_id):
        return pltpu.make_async_remote_copy(
            src_ref=src, dst_ref=dst, send_sem=s, recv_sem=r, device_id={"pages": pages_id, "blk": blk_id}, device_id_type=MESH
        )

    def y_at(step):
        return lax.rem(y + 1 + step, 4)

    def x_blk(step):
        return z * 8 + lax.rem(x + 1 + step, 4) * 2 + c

    def z_blk(step):
        return lax.rem(z + 1 + step, 4) * 8 + x * 2 + c

    partner = b + 1 - 2 * c
    half = held_ref.shape[1] // 2
    la = pl.ds(0, half)
    lb = pl.ds(half, half)
    waits = []

    a1 = [remote(hbuf.at[c, z, x, :, la], hbuf.at[c, z, x, :, la], as1.at[s], ar1.at[s], y, x_blk(s)) for s in range(3)]
    b1 = [remote(hbuf.at[c, z, x, :, lb], hbuf.at[c, z, x, :, lb], bs1.at[s], br1.at[s], y, z_blk(s)) for s in range(3)]
    for s in range(3):
        a1[s].start()
        b1[s].start()

    def send_x(step, carry):
        remote(x_ref, xb.at[b], xs, xr, y, lax.rem(b + 1 + step, 32)).start()
        return carry

    lax.fori_loop(0, 31, send_x, 0)
    w_sends = [remote(w_ref.at[y_at(s)], wall.at[y], ws.at[s], wr.at[s], y_at(s), b) for s in range(3)]
    for cp in w_sends:
        cp.start()

    for cp in a1:
        cp.wait_recv()
    a2 = [remote(hbuf.at[c, z, :, :, la], hbuf.at[c, z, :, :, la], as2.at[s], ar2.at[s], y, z_blk(s)) for s in range(3)]
    for cp in a2:
        cp.start()
    for cp in b1:
        cp.wait_recv()
    b2 = [remote(hbuf.at[c, :, x, :, lb], hbuf.at[c, :, x, :, lb], bs2.at[s], br2.at[s], y, x_blk(s)) for s in range(3)]
    for cp in b2:
        cp.start()
    swaps = [
        remote(hbuf.at[c, z, :, :, la], hbuf.at[c, z, :, :, la], cs.at[3], cr.at[3], y, partner),
        remote(hbuf.at[c, :, x, :, lb], hbuf.at[c, :, x, :, lb], ds.at[3], dr.at[3], y, partner),
    ]
    for cp in swaps:
        cp.start()

    pltpu.make_async_copy(xb.at[pl.ds(0, 31)], xb.at[pl.ds(0, 31)], xr).wait()
    for m in range(16):
        both = jnp.concatenate([xb[2 * m].astype(f32), xb[2 * m + 1].astype(f32)], axis=1)
        xg[:, m * CHUNK : (m + 1) * CHUNK] = both
    unit = normed(xg[...])
    nattn[...] = (unit * again_ref[...]).astype(bf16)
    mall[y] = (unit * mgain_ref[...]).astype(bf16)
    lc = pl.ds(pl.multiple_of(c * half, 128), half)
    x2 = [remote(mall.at[y, :, lc], mall.at[y, :, lc], x2s.at[s], x2r.at[s], y_at(s), b) for s in range(3)]
    for cp in x2:
        cp.start()

    for cp in w_sends:
        cp.wait_recv()
    loads[0].wait()
    own = own_ref[...] > 0.5
    weights = wall[:, 0:4, :].reshape(16, 128)
    w1 = high(weights)
    w2 = high(weights - w1)
    w3 = weights - w1 - w2
    for i, w in enumerate((w1, w2, w3)):
        wide = jnp.dot(w.astype(bf16), tile_ref[...], preferred_element_type=f32)
        wexp[i * 16 : (i + 1) * 16, :] = jnp.where(own, wide, 0.0).astype(bf16)

    def scatter(src, dst, s, r, chunk):
        for g in range(4):
            to_me = jnp.logical_and(y == g, chunk == b)

            @pl.when(jnp.logical_not(to_me))
            def _():
                remote(src.at[g * 32 + chunk], dst.at[me], s, r, g, chunk).start()

    def fold_step(step, carry):
        chunk = lax.rem(b + 1 + step, 32)
        part = page[:, pl.ds(pl.multiple_of(chunk * CHUNK, 128), CHUNK)]
        out = jnp.dot(wexp[...], part, preferred_element_type=f32)
        out = out[0:16] + out[16:32] + out[32:48]
        for g in range(4):
            fsend[g * 32 + chunk] = out[g * 4 : (g + 1) * 4].astype(bf16)
        scatter(fsend, fin, fs, fr, chunk)
        return carry

    lax.fori_loop(0, 32, fold_step, 0)
    fin[me] = fsend[me]

    for cp in loads[1:5]:
        cp.wait()
    lane = lax.broadcasted_iota(jnp.int32, (32, CHUNK), 1)
    zero = jnp.zeros((32, CHUNK), f32)
    k_0, k_1 = lane < HD, jnp.logical_and(lane >= PAIR, lane < PAIR + HD)
    is_key = jnp.logical_or(k_0, k_1)
    normal = nattn[...]
    query = jnp.where(is_key, high(rotated(times(normal, wq[...]), length_ref[...], turn_ref[...])), zero)
    pairs = high(rotated(times(normal, wkv[...]), length_ref[...], turn_ref[...]))
    new_key = jnp.where(is_key, pairs, zero)
    new_value = jnp.where(is_key, zero, pairs)
    q_fresh = jnp.where(lane < HD, query, pltpu.roll(query, CHUNK - HD, 1))[:, 0:PAIR].astype(bf16)
    qb[0:32, :] = query.astype(bf16)
    own_prod = query * new_key
    own_score = [jnp.sum(jnp.where(keep, own_prod, zero), axis=1, keepdims=True) * scale for keep in (k_0, k_1)]

    x3 = []
    for s in range(3):
        x2[s].wait_recv()
        back = lax.rem(y + 3 - s, 4)
        x3.append(remote(mall.at[back, :, lc], mall.at[back, :, lc], x3s.at[s], x3r.at[s], y, partner))
        x3[-1].start()
    for s in range(3):
        a2[s].wait_recv()
        back = lax.rem(z + 3 - s, 4)
        swaps.append(remote(hbuf.at[c, back, :, :, la], hbuf.at[c, back, :, :, la], cs.at[s], cr.at[s], y, partner))
        swaps[-1].start()
        b2[s].wait_recv()
        back = lax.rem(x + 3 - s, 4)
        swaps.append(remote(hbuf.at[c, :, back, :, lb], hbuf.at[c, :, back, :, lb], ds.at[s], dr.at[s], y, partner))
        swaps[-1].start()

    loads[5].wait()
    loads[6].wait()

    def keys_of(core):
        ks[pl.ds(pl.multiple_of(core * 128, 128), 128), 0:PAIR] = times(hbuf[core].reshape(128, D), wk[...])

    ks[:, PAIR:] = jnp.zeros((256, 256 - PAIR), f32)
    keys_of(c)
    for cp in swaps:
        cp.wait_recv()
    keys_of(1 - c)
    fresh = high(rotated(ks[...], rpos_ref[...], fturn_ref[...]))[:, 0:PAIR]
    prod = fresh * jnp.dot(repeat_ref[...], q_fresh, preferred_element_type=f32)
    flane = lax.broadcasted_iota(jnp.int32, (256, PAIR), 1)
    score0 = jnp.sum(jnp.where(flane < HD, prod, 0.0), axis=1, keepdims=True) * scale
    score1 = jnp.sum(jnp.where(flane < HD, 0.0, prod), axis=1, keepdims=True) * scale
    wlane = lax.broadcasted_iota(jnp.int32, (256, CHUNK), 1)
    first = wlane < PAIR
    rel = jnp.where(first, wlane, wlane - PAIR) - HD
    score = jnp.where(first, score0, score1)
    shigh = high(score)
    kind = jnp.where(rel < PAGE, shigh, jnp.where(rel < 2 * PAGE, score - shigh, 1.0))
    token = jnp.where(rel < PAGE, rel, jnp.where(rel < 2 * PAGE, rel - PAGE, rel - 2 * PAGE))
    hit = jnp.logical_and(jnp.logical_and(rel >= 0, rel < 3 * PAGE), token == rtok_ref[...])
    qb[32:288, :] = jnp.where(hit, kind, 0.0).astype(bf16)
    message = jnp.dot(place_ref[...], qb[...], preferred_element_type=f32)
    qsend[...] = message.reshape(128, 4, CHUNK).astype(bf16)

    def send_q(step, carry):
        other = lax.rem(me + 1 + step, 128)
        g, h = lax.div(other, 32), lax.rem(other, 32)
        remote(qsend.at[other], qin.at[me], qs, qr, g, h).start()
        return carry

    lax.fori_loop(0, 127, send_q, 0)
    qin[me] = qsend[me]

    loads[7].wait()
    loads[8].wait()
    for cp in x3:
        cp.wait_recv()
    hidden = times(mall[...].reshape(128, D), inw[...])
    active = (0.5 * hidden * (1.0 + lax.erf(hidden * np.float32(math.sqrt(0.5))))).astype(bf16)

    def mlp_step(step, carry):
        lanes = pl.ds(pl.multiple_of(step * 768, 128), 768)
        out = jnp.dot(active, outw[:, lanes], preferred_element_type=f32).astype(bf16).reshape(4, 2, 16, 768)
        mp[0, :, :, lanes] = out[:, 0]
        mp[1, :, :, lanes] = out[:, 1]
        return carry

    lax.fori_loop(0, 8, mlp_step, 0)
    m_swap = remote(mp.at[1 - c], mrecv, ms, mr, y, partner)
    m_swap.start()

    rest = pl.ds(0, 31)
    others = pl.ds(0, 127)
    pltpu.make_async_copy(qin.at[others], qin.at[others], qr).wait()
    own2 = jnp.concatenate([own, own], axis=0)
    lane16 = lax.broadcasted_iota(jnp.int32, (16, CHUNK), 1)
    key0 = lane16 < HD
    key1 = jnp.logical_and(lane16 >= PAIR, lane16 < PAIR + HD)

    def page_step(step, carry):
        for u in range(2):
            chunk = lax.rem(b + 1 + step * 2 + u, 32)
            part = page[:, pl.ds(pl.multiple_of(chunk * CHUNK, 128), CHUNK)]
            wide = jnp.concatenate([qin[g * 32 + chunk].astype(f32) for g in range(4)], axis=0)
            m = wide.astype(bf16)
            q2 = jnp.concatenate([jnp.where(key0, wide, 0.0), jnp.where(key1, wide, 0.0)], axis=0).astype(bf16)
            s = lax.dot_general(q2, part, (((1,), (1,)), ((), ())), preferred_element_type=f32) * scale
            ex = jnp.dot(m, spread_ref[...], preferred_element_type=f32)
            re = jnp.concatenate([ex[:, 0:192], ex[:, 256:448]], axis=0)
            fl = jnp.concatenate([ex[:, 512:704], ex[:, 768:960]], axis=0)
            s = jnp.where(own2, jnp.where(fl > 0.5, re, s), -1e30)
            top = jnp.max(s, axis=1, keepdims=True)
            thigh = high(top)
            tlow = high(top - thigh)
            p = jnp.where(own2, jnp.exp(s - (thigh + tlow)), 0.0)
            total = jnp.sum(p, axis=1, keepdims=True)
            ohigh = high(total)
            mixed = jnp.dot(p.astype(bf16), part, preferred_element_type=f32)
            olow = total - ohigh
            res = jnp.where(lane16 < PAIR, mixed[0:16], mixed[16:32])
            for i in range(2):
                for n, col in enumerate((thigh, tlow, ohigh, olow)):
                    res = jnp.where(lane16 == i * PAIR + n, col[i * 16 : (i + 1) * 16], res)
            for g in range(4):
                rsend[g * 32 + chunk] = res[g * 4 : (g + 1) * 4].astype(bf16)
            scatter(rsend, rin, rs, rr, chunk)
        return carry

    lax.fori_loop(0, 16, page_step, 0)
    rin[me] = rsend[me]

    m_swap.wait_recv()
    ysend[...] = (mp[c].astype(f32) + mrecv[...].astype(f32)).astype(bf16)
    y_out = [remote(ysend.at[y_at(s)], yrecv.at[y], ys.at[s], yr.at[s], y_at(s), b) for s in range(3)]
    for cp in y_out:
        cp.start()
    yrecv[y] = ysend[y]

    pltpu.make_async_copy(fin.at[others], fin.at[others], fr).wait()
    folded = jnp.dot(route_ref[...], fin[...].reshape(512, CHUNK), preferred_element_type=f32)
    for j in range(PPR):
        fold_ref[:, j, :] = folded[j * 32 : (j + 1) * 32].astype(bf16)
    f_score = []
    for j in range(PPR):
        fprod = folded[j * 32 : (j + 1) * 32] * query
        ok = drop_ref[j * 32 : (j + 1) * 32] > 0.5
        f_score.append([
            jnp.where(ok, jnp.sum(jnp.where(k_0, fprod, zero), axis=1, keepdims=True) * scale, -1e30),
            jnp.where(ok, jnp.sum(jnp.where(k_1, fprod, zero), axis=1, keepdims=True) * scale, -1e30),
        ])
    pltpu.make_async_copy(rin.at[others], rin.at[others], rr).wait()
    parts = jnp.dot(route_ref[...], rin[...].reshape(512, CHUNK), preferred_element_type=f32)
    tops = []
    for i in range(2):
        top = own_score[i]
        p_top = []
        for j in range(PPR):
            rows = parts[j * 32 : (j + 1) * 32]
            ok = kept_ref[j * 32 : (j + 1) * 32] > 0.5
            p_top.append(jnp.where(ok, rows[:, i * PAIR : i * PAIR + 1] + rows[:, i * PAIR + 1 : i * PAIR + 2], -1e30))
            top = jnp.maximum(top, jnp.maximum(p_top[j], f_score[j][i]))
        tops.append((top, p_top))
    is_first = lane < PAIR
    mixed = zero
    total = zero
    for j in range(PPR):
        rows = parts[j * 32 : (j + 1) * 32]
        ok = kept_ref[j * 32 : (j + 1) * 32] > 0.5
        w = [jnp.where(ok, jnp.exp(tops[i][1][j] - tops[i][0]), 0.0) for i in range(2)]
        e = [jnp.exp(f_score[j][i] - tops[i][0]) for i in range(2)]
        sums = [
            w[i] * (rows[:, i * PAIR + 2 : i * PAIR + 3] + rows[:, i * PAIR + 3 : i * PAIR + 4]) + e[i] for i in range(2)
        ]
        mixed = mixed + jnp.where(is_first, w[0], w[1]) * rows + jnp.where(is_first, e[0], e[1]) * folded[j * 32 : (j + 1) * 32]
        total = total + jnp.where(is_first, sums[0], sums[1])
    o = [jnp.exp(own_score[i] - tops[i][0]) for i in range(2)]
    own_exp = jnp.where(is_first, o[0], o[1])
    mixed = (mixed + own_exp * new_value) / (total + own_exp)
    attended = jnp.where(lane < HD, pltpu.roll(mixed, CHUNK - HD, 1), pltpu.roll(mixed, CHUNK - PAIR, 1))[:, 0:PAIR].astype(bf16)
    loads[9].wait()

    def dense_step(step, carry):
        lanes = pl.ds(pl.multiple_of(step * 1536, 128), 1536)
        out = jnp.dot(attended, dense[:, lanes], preferred_element_type=f32)
        apart[0, :, lanes] = out[0:16]
        apart[1, :, lanes] = out[16:32]
        return carry

    lax.fori_loop(0, 4, dense_step, 0)
    asend[...] = apart[1 - c].astype(bf16)
    a_swap = remote(asend, arecv, ats, atr, y, partner)
    a_swap.start()
    for cp in y_out:
        cp.wait_recv()
    summed = apart[c] + yrecv[0].astype(f32) + yrecv[1].astype(f32) + yrecv[2].astype(f32) + yrecv[3].astype(f32)
    a_swap.wait_recv()
    tsend[...] = (summed + arecv[...].astype(f32)).astype(bf16)

    def send_t(step, carry):
        other = lax.rem(chip + 1 + step, 16)
        remote(
            tsend.at[:, pl.ds(pl.multiple_of(other * CHUNK, 128), CHUNK)], trecv.at[chip], ts, tr, y, other * 2 + c
        ).start()
        return carry

    lax.fori_loop(0, 15, send_t, 0)
    trecv[chip] = tsend[:, pl.ds(pl.multiple_of(chip * CHUNK, 128), CHUNK)]
    fifteen = pl.ds(0, 15)
    pltpu.make_async_copy(trecv.at[fifteen], trecv.at[fifteen], tr).wait()
    oall[c] = jnp.sum(trecv[...].astype(f32), axis=0).astype(bf16)
    o_swap = remote(oall.at[c], oall.at[c], os, orr, y, partner)
    o_swap.start()
    o_swap.wait_recv()
    result = oall[...].astype(f32).reshape(32, CHUNK)
    sum_ref[...] = jnp.where(c == 0, result, pltpu.roll(result, PAIR, 1))[:, 0:PAIR].astype(bf16)

    for cp in a1 + b1 + a2 + b2 + swaps + w_sends + x2 + x3 + y_out + [m_swap, a_swap, o_swap]:
        cp.wait_send()
    pltpu.make_async_copy(xb.at[rest], xb.at[rest], xs).wait()
    for ref, sem in ((qsend, qs), (fsend, fs), (rsend, rs)):
        pltpu.make_async_copy(ref.at[others], ref.at[others], sem).wait()
    pltpu.make_async_copy(trecv.at[fifteen], trecv.at[fifteen], ts).wait()


def step_call(scale, blocks, arrays):
    f32, bf16 = jnp.float32, jnp.bfloat16
    one = pltpu.SemaphoreType.DMA
    sems = lambda n: pltpu.SemaphoreType.DMA((n,))
    rows4 = pltpu.VMEM((128, 4, CHUNK), bf16)
    scratch = [
        pltpu.VMEM((CHUNK, D), bf16), pltpu.VMEM((CHUNK, D), bf16), pltpu.VMEM((PAIR, D), bf16),
        pltpu.VMEM((PAIR, D), bf16), pltpu.VMEM((PAIR, D), bf16), pltpu.VMEM((PAIR, D), bf16),
        pltpu.VMEM((192, 2 * D), bf16), pltpu.VMEM((32, 32, PAIR), bf16), pltpu.VMEM((32, D), f32), pltpu.VMEM((32, D), bf16),
        pltpu.VMEM((4, 32, D), bf16), pltpu.VMEM((2, 4, 4, NREC, D), bf16), pltpu.VMEM((4, 8, 128), f32),
        pltpu.VMEM((48, 192), bf16), pltpu.VMEM((288, CHUNK), bf16), pltpu.VMEM((256, 256), f32),
        rows4, rows4, rows4, rows4, rows4, rows4,
        pltpu.VMEM((2, 4, 16, D), bf16), pltpu.VMEM((4, 16, D), bf16), pltpu.VMEM((4, 16, D), bf16), pltpu.VMEM((4, 16, D), bf16),
        pltpu.VMEM((2, 16, D), f32), pltpu.VMEM((16, D), bf16), pltpu.VMEM((16, D), bf16), pltpu.VMEM((16, D), bf16),
        pltpu.VMEM((16, 16, CHUNK), bf16), pltpu.VMEM((2, 16, CHUNK), bf16),
        sems(10), one, one, sems(3), sems(3), sems(3), sems(3),
        sems(3), sems(3), sems(3), sems(3), sems(3), sems(3), sems(3), sems(3), sems(4), sems(4), sems(4), sems(4), sems(3), sems(3),
        one, one, one, one, one, one, one, one, sems(3), sems(3), one, one, one, one, one, one, one,
    ]
    return pl.pallas_call(
        functools.partial(step_kernel, scale),
        out_shape=[jax.ShapeDtypeStruct((32, PAIR), bf16), jax.ShapeDtypeStruct((32, PPR, CHUNK), bf16)],
        in_specs=[VMEM_SPEC] * len(blocks) + [pl.BlockSpec(memory_space=pl.ANY)] * len(arrays),
        out_specs=[VMEM_SPEC] * 2,
        scratch_shapes=scratch,
        compiler_params=pltpu.CompilerParams(collective_id=0, has_side_effects=True, vmem_limit_bytes=58 << 20),
        name="decode_step",
    )(*blocks, *arrays)


def on_device(
    new_hidden,
    attn_gain,
    mlp_gain,
    qkv_weight,
    dense_weight,
    in_weight,
    out_weight,
    page_store,
    held_states,
    fold_weights,
    page_table,
    lengths,
    keep_slots,
    fold_index,
    recompute_list,
):
    n_pages = lax.axis_size("pages")
    n_blk = lax.axis_size("blk")
    group = lax.axis_index("pages")
    blk = lax.axis_index("blk")
    device = group * n_blk + blk
    n_devices = n_pages * n_blk
    rows = lengths.shape[0]
    pages_dev = page_store.shape[0]
    per_group = pages_dev // n_pages
    slots = rows * PPR
    scale = 1.0 / math.sqrt(HD)
    f32, bf16 = jnp.float32, jnp.bfloat16
    iota = lambda n: jnp.arange(n, dtype=jnp.int32)

    my_table = lax.dynamic_slice_in_dim(page_table, group * rows, rows, 0)
    ids = my_table.T.reshape(slots)
    rank = jnp.sum((ids[None, :] < ids[:, None]).astype(jnp.int32), axis=1)
    place = rank // per_group * 4 + rank % per_group
    route = (place[:, None] == iota(n_devices * 4)[None, :]).astype(bf16)
    owner = jnp.sum(
        jnp.where(page_table.reshape(1, -1) == (device * pages_dev + iota(16))[:, None], iota(n_devices * pages_dev)[None, :] // slots, 0),
        axis=1,
    )
    owner = jnp.where(iota(16) < pages_dev, owner, -1)
    earlier = jnp.sum(jnp.logical_and(owner[None, :] == owner[:, None], iota(16)[None, :] < iota(16)[:, None]).astype(jnp.int32), axis=1)
    local_place = jnp.where(owner >= 0, owner * 4 + earlier, -1)
    own = jnp.any(
        jnp.logical_and(
            local_place[None, None, :] == iota(16)[:, None, None], (iota(pages_dev * PAGE) // PAGE)[None, :, None] == iota(16)[None, None, :]
        ),
        axis=2,
    ).astype(f32)

    slot_ids = iota(PPR)[:, None]
    is_kept = jnp.any(keep_slots[None, :, :] == slot_ids[:, :, None], axis=2)
    dropped = jnp.logical_and(jnp.logical_not(is_kept), slot_ids * PAGE < lengths[None, :])
    live = slot_ids[:, :, None] * PAGE + iota(PAGE)[None, None, :] < lengths[None, :, None]
    choose = (fold_index.T[:, :, None] == iota(NF)[None, None, :]).astype(f32)
    weight_rows = jnp.sum(choose[:, :, :, None] * fold_weights[None, None], axis=2)
    weight_rows = jnp.where(jnp.logical_and(live, dropped[:, :, None]), weight_rows, 0.0).reshape(slots, PAGE)
    column = (iota(n_pages)[:, None] * n_blk + blk) * 4 + iota(4)[None, :]
    mine = (column.reshape(-1)[:, None] == place[None, :]).astype(f32)
    weight_out = jnp.einsum("cs,st->ct", mine, weight_rows, precision=lax.Precision.HIGHEST)
    weight_out = jnp.pad(weight_out.reshape(n_pages, 4, PAGE), ((0, 0), (0, 4), (0, 128 - PAGE)))

    by_core = lambda v: v.reshape(rows // 2, 2, NREC).transpose(1, 0, 2).reshape(rows * NREC)
    which = recompute_list // PAGE
    rec_slot = jnp.sum(jnp.where(which[:, :, None] == iota(KP)[None, None, :], keep_slots[:, None, :], 0), axis=2)
    rec_token = recompute_list % PAGE
    place2 = place.reshape(PPR, rows)
    rec_place = jnp.sum(jnp.where(rec_slot[None] == iota(PPR)[:, None, None], place2[:, :, None], 0), axis=0)
    at = iota(n_devices * 4)[:, None]
    to_place = jnp.concatenate(
        [jnp.any(place2[:, None, :] == at[None], axis=0), by_core(rec_place)[None, :] == at], axis=1
    ).astype(bf16)

    order = by_core(np.arange(rows)[:, None] + np.zeros((1, NREC), np.int32))
    repeat = (order[:, None] == np.arange(rows)[None, :]).astype(bf16)
    lane = np.arange(CHUNK)[:, None]
    tokens = np.arange(pages_dev * PAGE)[None, :] % PAGE
    spread = np.zeros((CHUNK, 4, 256), np.float32)
    for i in range(2):
        t = lane - (i * PAIR + HD)
        spread[:, i, : pages_dev * PAGE] = (t == tokens) | (t == tokens + PAGE)
        spread[:, 2 + i, : pages_dev * PAGE] = t == tokens + 2 * PAGE
    spread = jnp.asarray(spread.reshape(CHUNK, 1024), bf16)
    tile = jnp.asarray((np.arange(128)[:, None] == tokens).astype(np.float32), bf16)
    turn = jnp.asarray(rotary_rows(CHUNK, (0, PAIR)))
    fresh_turn = jnp.asarray(rotary_rows(256, (0, HD)))

    column_of = lambda v: v.reshape(-1, 1)
    blocks = (
        new_hidden, held_states.reshape(NREC, D), attn_gain.reshape(1, D), mlp_gain.reshape(1, D), weight_out, own, route, to_place,
        repeat, spread, tile, turn, fresh_turn, column_of(lengths.astype(f32)), column_of(by_core(rec_slot * PAGE + rec_token).astype(f32)),
        column_of(by_core(rec_token)), column_of(is_kept.astype(f32)), column_of(dropped.astype(f32)),
    )
    arrays = (qkv_weight.T, dense_weight, in_weight.T, out_weight, page_store.reshape(pages_dev * PAGE, 2 * D))
    return tuple(step_call(scale, blocks, arrays))


def solution(mesh):
    in_specs = (
        P("pages", "blk"),
        P(),
        P(),
        P(None, "blk"),
        P("blk", None),
        P(None, ("pages", "blk")),
        P(("pages", "blk"), None),
        P(("pages", "blk"), None, None),
        P(("pages", "blk"), None, None),
        P(),
        P(),
        P("pages"),
        P("pages", None),
        P("pages", None),
        P("pages", None),
    )
    out_specs = (P("pages", "blk"), P("pages", None, "blk"))
    return jax.shard_map(
        on_device, mesh=mesh, in_specs=in_specs, out_specs=out_specs, check_vma=False
    )
```

```python
import functools
import math

import jax
import jax.numpy as jnp
import numpy as np
from jax import lax
from jax.experimental import pallas as pl
from jax.experimental.pallas import tpu as pltpu
from jax.sharding import PartitionSpec as P

D = 6144
H = 64
HD = 96
ROT = 24
PAGE = 16
PPR = 12
KP = 5
NREC = 8
NF = 8
PAIR = 2 * HD
EPSILON = 1e-05
ROT_BASE = 10000.0
MESH = pl.DeviceIdType.MESH
VMEM_SPEC = pl.BlockSpec(memory_space=pltpu.VMEM)


CHUNK = 2 * PAIR


def rotary_rows(lanes, starts):
    out = np.zeros((8, lanes), np.float32)
    half = ROT // 2
    freq = (np.float32(ROT_BASE) ** (np.float32(-2.0) * np.arange(half, dtype=np.float32) / np.float32(ROT))).astype(np.float32)
    for start in starts:
        out[0, start : start + half] = freq
        out[0, start + half : start + ROT] = freq
        out[1, start + half : start + ROT] = 1.0
        out[2, start : start + half] = 1.0
    return out


def rotated(values, position, rows):
    lanes = values.shape[1]
    angle = position * rows[0:1]
    sine = jnp.sin(angle)
    return (
        values * jnp.cos(angle)
        + pltpu.roll(values, ROT // 2, 1) * (sine * rows[1:2])
        - pltpu.roll(values, lanes - ROT // 2, 1) * (sine * rows[2:3])
    )


def normed(values):
    centered = values - jnp.mean(values, axis=-1, keepdims=True)
    spread = jnp.mean(centered * centered, axis=-1, keepdims=True)
    return centered * lax.rsqrt(spread + EPSILON)


def times(left, right):
    return lax.dot_general(left, right, (((1,), (1,)), ((), ())), preferred_element_type=jnp.float32)


def over_rows(left, right):
    return lax.dot_general(left, right, (((0,), (0,)), ((), ())), preferred_element_type=jnp.float32)


def high(values):
    return values.astype(jnp.bfloat16).astype(jnp.float32)


def step_kernel(
    scale,
    x_ref, held_ref, again_ref, mgain_ref, fw_ref, table_ref, length_row, keep_rows, fold_rows, rec_rows, spread_ref, tile_ref,
    turn_ref, fturn_ref,
    qkv_hbm, dense_hbm, in_hbm, out_hbm, page_hbm,
    sum_ref, fold_ref,
    gt, route_ref, place_ref, fslot, fsel, w_ref, own8, wq, wkv, wk, dense, inw, outw, page, xb, xg, nattn, mall, hbuf, wall, wexp, qb, ks,
    qsend, qin, fsend, fin, rsend, rin, mp, mrecv, ysend, yrecv, apart, asend, arecv, tsend, trecv, oall,
    load, xs, xr, x2s, x2r, x3s, x3r, as1, ar1, bs1, br1, as2, ar2, bs2, br2, cs, cr, ds, dr, ws, wr,
    qs, qr, fs, fr, rs, rr, ms, mr, ys, yr, ats, atr, ts, tr, os, orr, owns,
):
    f32, bf16 = jnp.float32, jnp.bfloat16
    y = lax.axis_index("pages")
    b = lax.axis_index("blk")
    me = y * 32 + b
    z = lax.div(b, 8)
    x = lax.rem(lax.div(b, 2), 4)
    c = lax.rem(b, 2)
    chip = lax.div(b, 2)

    loads = [
        pltpu.make_async_copy(page_hbm, page, load.at[0]),
        pltpu.make_async_copy(qkv_hbm.at[pl.ds(0, PAIR)], wq.at[pl.ds(0, PAIR)], load.at[1]),
        pltpu.make_async_copy(qkv_hbm.at[pl.ds(288, PAIR)], wq.at[pl.ds(PAIR, PAIR)], load.at[5]),
        pltpu.make_async_copy(qkv_hbm.at[pl.ds(HD, PAIR)], wkv.at[pl.ds(0, PAIR)], load.at[6]),
        pltpu.make_async_copy(qkv_hbm.at[pl.ds(288 + HD, PAIR)], wkv.at[pl.ds(PAIR, PAIR)], load.at[7]),
        pltpu.make_async_copy(qkv_hbm.at[pl.ds(HD, HD)], wk.at[pl.ds(0, HD)], load.at[8]),
        pltpu.make_async_copy(qkv_hbm.at[pl.ds(288 + HD, HD)], wk.at[pl.ds(HD, HD)], load.at[9]),
        pltpu.make_async_copy(in_hbm, inw, load.at[2]),
        pltpu.make_async_copy(out_hbm, outw, load.at[3]),
        pltpu.make_async_copy(dense_hbm, dense, load.at[4]),
    ]
    for cp in loads:
        cp.start()

    barrier = pltpu.get_barrier_semaphore()

    def hello(step, carry):
        other = lax.rem(me + 1 + step, 128)
        pl.semaphore_signal(barrier, inc=1, device_id={"pages": lax.div(other, 32), "blk": lax.rem(other, 32)}, device_id_type=MESH)
        return carry

    lax.fori_loop(0, 127, hello, 0)
    hbuf[c, z, x] = (normed(held_ref[...].astype(f32)) * again_ref[...]).astype(bf16)
    xb[b] = x_ref[...]
    pl.semaphore_wait(barrier, 127)

    def remote(src, dst, s, r, pages_id, blk_id):
        return pltpu.make_async_remote_copy(
            src_ref=src, dst_ref=dst, send_sem=s, recv_sem=r, device_id={"pages": pages_id, "blk": blk_id}, device_id_type=MESH
        )

    def y_at(step):
        return lax.rem(y + 1 + step, 4)

    def x_blk(step):
        return z * 8 + lax.rem(x + 1 + step, 4) * 2 + c

    def z_blk(step):
        return lax.rem(z + 1 + step, 4) * 8 + x * 2 + c

    partner = b + 1 - 2 * c
    half = held_ref.shape[1] // 2
    la = pl.ds(0, half)
    lb = pl.ds(half, half)
    waits = []

    a1 = [remote(hbuf.at[c, z, x, :, la], hbuf.at[c, z, x, :, la], as1.at[s], ar1.at[s], y, x_blk(s)) for s in range(3)]
    b1 = [remote(hbuf.at[c, z, x, :, lb], hbuf.at[c, z, x, :, lb], bs1.at[s], br1.at[s], y, z_blk(s)) for s in range(3)]
    for s in range(3):
        a1[s].start()
        b1[s].start()

    def send_x(step, carry):
        remote(x_ref, xb.at[b], xs, xr, y, lax.rem(b + 1 + step, 32)).start()
        return carry

    lax.fori_loop(0, 31, send_x, 0)
    gt[...] = jnp.zeros_like(gt)
    gt[0:NREC, 0:32] = rec_rows[...].astype(f32)
    gt[8 : 8 + KP, 0:32] = keep_rows[...].astype(f32)
    gt[13:14, 0:32] = length_row[...].astype(f32)
    gt[16 : 16 + PPR, 0:32] = fold_rows[...].astype(f32)
    every = table_ref[...].astype(f32)
    mine = jnp.zeros((PPR, 32), f32)
    for g in range(4):
        mine = mine + jnp.where(y == g, every[:, g * 32 : (g + 1) * 32], 0.0)
    gt[32 : 32 + PPR, 0:32] = mine
    by_request = jnp.transpose(gt[...])[0:32]
    length_col = by_request[:, 13:14]
    lane512 = lax.broadcasted_iota(jnp.int32, (32, 512), 1)
    lane128 = lax.broadcasted_iota(jnp.int32, (32, 128), 1)
    token16 = lax.broadcasted_iota(jnp.int32, (32, PAGE), 1)
    target = (lax.shift_right_logical(token16, 2) * 32 + b) * 4 + jnp.bitwise_and(token16, 3)
    numbers = by_request
    any_slot = jnp.zeros((32, 512), f32)
    kept, dropped = [], []
    for j in range(PPR):
        column = by_request[:, 32 + j : 33 + j]
        below = jnp.zeros((32, 32), f32)
        for other in range(PPR):
            below = below + jnp.where(gt[32 + other : 33 + other, 0:32] < column, 1.0, 0.0)
        rank = jnp.sum(below, axis=1, keepdims=True).astype(jnp.int32)
        holder = lax.shift_right_logical(rank * 43691, 17)
        nth = rank - 3 * holder
        place = holder * 4 + nth
        hit = jnp.where(place == lane512, 1.0, 0.0)
        any_slot = any_slot + hit
        route_ref[j * 32 : (j + 1) * 32, :] = hit.astype(bf16)
        numbers = jnp.where(lane128 == 48 + j, holder.astype(f32), jnp.where(lane128 == 64 + j, nth.astype(f32), numbers))
        is_kept = by_request[:, 8:9] == j
        for m in range(1, KP):
            is_kept = jnp.logical_or(is_kept, by_request[:, 8 + m : 9 + m] == j)
        kept.append(jnp.where(is_kept, 1.0, 0.0))
        dropped.append(jnp.where(jnp.logical_and(jnp.logical_not(is_kept), length_col > j * PAGE), 1.0, 0.0))
        row = jnp.zeros((32, PAGE), f32)
        for f in range(NF):
            row = row + jnp.where(by_request[:, 16 + j : 17 + j] == f, fw_ref[f : f + 1, :], 0.0)
        live = jnp.logical_and(dropped[j] > 0.5, (token16 + j * PAGE).astype(f32) < length_col)
        fslot[j * 32 : (j + 1) * 32, :] = jnp.where(live, row, 0.0)
        fsel[j * 32 : (j + 1) * 32, :] = jnp.where(place == target, 1.0, 0.0).astype(bf16)
    place_ref[0:32, :] = any_slot.astype(bf16)
    wanted = fslot[...]
    wanted1 = high(wanted)
    wanted2 = high(wanted - wanted1)
    picked = jnp.zeros((16, PAGE), f32)
    for w in (wanted1, wanted2, wanted - wanted1 - wanted2):
        picked = picked + over_rows(fsel[...], w.astype(bf16))
    w_ref[...] = jnp.zeros_like(w_ref)
    for g in range(4):
        w_ref[g, 0:4, 0:PAGE] = picked[g * 4 : (g + 1) * 4]
    wall[y] = w_ref[y]
    w_sends = [remote(w_ref.at[y_at(s)], wall.at[y], ws.at[s], wr.at[s], y_at(s), b) for s in range(3)]
    for cp in w_sends:
        cp.start()

    row256 = lax.broadcasted_iota(jnp.int32, (256, 1), 0)
    request = jnp.bitwise_and(lax.shift_right_logical(row256, 3), 15) * 2 + lax.shift_right_logical(row256, 7)
    repeat = jnp.where(lax.broadcasted_iota(jnp.int32, (256, 32), 1) == request, 1.0, 0.0).astype(bf16)
    listed = jnp.dot(repeat, numbers.astype(bf16), preferred_element_type=f32)
    at256 = lax.broadcasted_iota(jnp.int32, (256, 128), 1)

    def entry(at):
        return jnp.sum(jnp.where(at256 == at, listed, 0.0), axis=1, keepdims=True).astype(jnp.int32)

    rec = entry(jnp.bitwise_and(row256, 7))
    rec_slot = entry(8 + lax.shift_right_logical(rec, 4))
    rec_token = jnp.bitwise_and(rec, 15)
    rec_place = entry(48 + rec_slot) * 4 + entry(64 + rec_slot)
    rec_pos = (rec_slot * PAGE + rec_token).astype(f32)
    place_ref[32:288, :] = jnp.where(lax.broadcasted_iota(jnp.int32, (256, 512), 1) == rec_place, 1.0, 0.0).astype(bf16)
    owner_lane = lax.shift_right_logical(lax.broadcasted_iota(jnp.int32, (PPR, 128), 1), 5).astype(f32)
    token_page = lax.shift_right_logical(lax.broadcasted_iota(jnp.int32, (16, 192), 1), 4)
    place_row = lax.broadcasted_iota(jnp.int32, (16, 192), 0).astype(f32)
    groups = []
    owned = jnp.zeros((16, 192), f32)
    for p in range(12):
        found = jnp.where(table_ref[...] == me * 12 + p, owner_lane, 0.0)
        group = jnp.sum(jnp.sum(found, axis=1, keepdims=True), axis=0, keepdims=True)
        nth = jnp.zeros((1, 1), f32)
        for g in groups:
            nth = nth + jnp.where(g == group, 1.0, 0.0)
        groups.append(group)
        owned = owned + jnp.where(jnp.logical_and(token_page == p, place_row == group * 4.0 + nth), 1.0, 0.0)
    for i in range(8):
        own8[i * 16 : (i + 1) * 16, :] = owned

    for cp in a1:
        cp.wait_recv()
    a2 = [remote(hbuf.at[c, z, :, :, la], hbuf.at[c, z, :, :, la], as2.at[s], ar2.at[s], y, z_blk(s)) for s in range(3)]
    for cp in a2:
        cp.start()
    for cp in b1:
        cp.wait_recv()
    b2 = [remote(hbuf.at[c, :, x, :, lb], hbuf.at[c, :, x, :, lb], bs2.at[s], br2.at[s], y, x_blk(s)) for s in range(3)]
    for cp in b2:
        cp.start()
    swaps = [
        remote(hbuf.at[c, z, :, :, la], hbuf.at[c, z, :, :, la], cs.at[3], cr.at[3], y, partner),
        remote(hbuf.at[c, :, x, :, lb], hbuf.at[c, :, x, :, lb], ds.at[3], dr.at[3], y, partner),
    ]
    for cp in swaps:
        cp.start()

    pltpu.make_async_copy(xb.at[pl.ds(0, 31)], xb.at[pl.ds(0, 31)], xr).wait()
    for m in range(16):
        both = jnp.concatenate([xb[2 * m].astype(f32), xb[2 * m + 1].astype(f32)], axis=1)
        xg[:, m * CHUNK : (m + 1) * CHUNK] = both
    unit = normed(xg[...])
    nattn[...] = (unit * again_ref[...]).astype(bf16)
    mall[y] = (unit * mgain_ref[...]).astype(bf16)
    lc = pl.ds(pl.multiple_of(c * half, 128), half)
    x2 = [remote(mall.at[y, :, lc], mall.at[y, :, lc], x2s.at[s], x2r.at[s], y_at(s), b) for s in range(3)]
    for cp in x2:
        cp.start()

    for cp in w_sends:
        cp.wait_recv()
    loads[0].wait()
    own = own8[0:16, :] > 0.5
    weights = wall[:, 0:4, :].reshape(16, 128)
    w1 = high(weights)
    w2 = high(weights - w1)
    w3 = weights - w1 - w2
    for i, w in enumerate((w1, w2, w3)):
        wide = jnp.dot(w.astype(bf16), tile_ref[...], preferred_element_type=f32)
        wexp[i * 16 : (i + 1) * 16, :] = jnp.where(own, wide, 0.0).astype(bf16)

    def scatter(src, dst, s, r, step):
        def one(n, carry):
            chunk = lax.rem(b + 1 + step * 4 + lax.div(n, 4), 32)
            g = lax.rem(y + 1 + lax.rem(n, 4), 4)
            remote(src.at[g * 32 + chunk], dst.at[me], s, r, g, chunk).start()
            return carry

        lax.fori_loop(0, 16 - lax.div(step, 7), one, 0)

    def chunk_at(step, u):
        chunk = lax.rem(b + 1 + step * 4 + u, 32)
        return chunk, page[:, pl.ds(pl.multiple_of(chunk * CHUNK, 128), CHUNK)]

    def fold_step(step, carry):
        for u in range(4):
            chunk, part = chunk_at(step, u)
            out = jnp.dot(wexp[...], part, preferred_element_type=f32)
            out = out[0:16] + out[16:32] + out[32:48]
            for g in range(4):
                fsend[g * 32 + chunk] = out[g * 4 : (g + 1) * 4].astype(bf16)
        scatter(fsend, fin, fs, fr, step)
        return carry

    lax.fori_loop(0, 8, fold_step, 0)
    fin[me] = fsend[me]

    for cp in loads[1:5]:
        cp.wait()
    lane = lax.broadcasted_iota(jnp.int32, (32, CHUNK), 1)
    zero = jnp.zeros((32, CHUNK), f32)
    k_0, k_1 = lane < HD, jnp.logical_and(lane >= PAIR, lane < PAIR + HD)
    is_key = jnp.logical_or(k_0, k_1)
    normal = nattn[...]
    query = jnp.where(is_key, high(rotated(times(normal, wq[...]), length_col, turn_ref[...])), zero)
    pairs = high(rotated(times(normal, wkv[...]), length_col, turn_ref[...]))
    new_key = jnp.where(is_key, pairs, zero)
    new_value = jnp.where(is_key, zero, pairs)
    q_fresh = jnp.where(lane < HD, query, pltpu.roll(query, CHUNK - HD, 1))[:, 0:PAIR].astype(bf16)
    qb[0:32, :] = query.astype(bf16)
    own_prod = query * new_key
    own_score = [jnp.sum(jnp.where(keep, own_prod, zero), axis=1, keepdims=True) * scale for keep in (k_0, k_1)]

    for s in range(3):
        a2[s].wait_recv()
        back = lax.rem(z + 3 - s, 4)
        swaps.append(remote(hbuf.at[c, back, :, :, la], hbuf.at[c, back, :, :, la], cs.at[s], cr.at[s], y, partner))
        swaps[-1].start()
        b2[s].wait_recv()
        back = lax.rem(x + 3 - s, 4)
        swaps.append(remote(hbuf.at[c, :, back, :, lb], hbuf.at[c, :, back, :, lb], ds.at[s], dr.at[s], y, partner))
        swaps[-1].start()

    loads[5].wait()
    loads[6].wait()

    def keys_of(core):
        ks[pl.ds(pl.multiple_of(core * 128, 128), 128), 0:PAIR] = times(hbuf[core].reshape(128, D), wk[...])

    ks[:, PAIR:] = jnp.zeros((256, 256 - PAIR), f32)
    keys_of(c)
    for cp in swaps:
        cp.wait_recv()
    keys_of(1 - c)
    fresh = high(rotated(ks[...], rec_pos, fturn_ref[...]))[:, 0:PAIR]
    prod = fresh * jnp.dot(repeat, q_fresh, preferred_element_type=f32)
    flane = lax.broadcasted_iota(jnp.int32, (256, PAIR), 1)
    score0 = jnp.sum(jnp.where(flane < HD, prod, 0.0), axis=1, keepdims=True) * scale
    score1 = jnp.sum(jnp.where(flane < HD, 0.0, prod), axis=1, keepdims=True) * scale
    wlane = lax.broadcasted_iota(jnp.int32, (256, CHUNK), 1)
    first = wlane < PAIR
    rel = jnp.where(first, wlane, wlane - PAIR) - HD
    score = jnp.where(first, score0, score1)
    shigh = high(score)
    kind = jnp.where(rel < PAGE, shigh, jnp.where(rel < 2 * PAGE, score - shigh, 1.0))
    token = jnp.where(rel < PAGE, rel, jnp.where(rel < 2 * PAGE, rel - PAGE, rel - 2 * PAGE))
    hit = jnp.logical_and(jnp.logical_and(rel >= 0, rel < 3 * PAGE), token == rec_token)
    qb[32:288, :] = jnp.where(hit, kind, 0.0).astype(bf16)
    message = over_rows(place_ref[...], qb[...])
    qsend[...] = message.reshape(128, 4, CHUNK).astype(bf16)

    def send_q(step, carry):
        other = lax.rem(me + 1 + step, 128)
        g, h = lax.div(other, 32), lax.rem(other, 32)
        remote(qsend.at[other], qin.at[me], qs, qr, g, h).start()
        return carry

    lax.fori_loop(0, 127, send_q, 0)
    qin[me] = qsend[me]

    x3 = []
    for s in range(3):
        x2[s].wait_recv()
        back = lax.rem(y + 3 - s, 4)
        x3.append(remote(mall.at[back, :, lc], mall.at[back, :, lc], x3s.at[s], x3r.at[s], y, partner))
        x3[-1].start()

    rest = pl.ds(0, 31)
    others = pl.ds(0, 127)
    pltpu.make_async_copy(qin.at[others], qin.at[others], qr).wait()
    lane16 = lax.broadcasted_iota(jnp.int32, (16, CHUNK), 1)
    key0 = lane16 < HD
    key1 = jnp.logical_and(lane16 >= PAIR, lane16 < PAIR + HD)

    def page_step(step, carry):
        chunks, parts, wides = [], [], []
        for u in range(4):
            chunk, part = chunk_at(step, u)
            chunks.append(chunk)
            parts.append(part)
            wides.append(jnp.concatenate([qin[g * 32 + chunk].astype(f32) for g in range(4)], axis=0))
        ex = jnp.dot(jnp.concatenate(wides, axis=0).astype(bf16), spread_ref[...], preferred_element_type=f32)
        scores, again, flags = [], [], []
        for u in range(4):
            q2 = jnp.concatenate([jnp.where(key0, wides[u], 0.0), jnp.where(key1, wides[u], 0.0)], axis=0).astype(bf16)
            scores.append(times(q2, parts[u]))
            again += [ex[u * 16 : (u + 1) * 16, 0:192], ex[u * 16 : (u + 1) * 16, 256:448]]
            flags += [ex[u * 16 : (u + 1) * 16, 512:704], ex[u * 16 : (u + 1) * 16, 768:960]]
        mask = own8[...] > 0.5
        s = jnp.where(jnp.concatenate(flags, axis=0) > 0.5, jnp.concatenate(again, axis=0), jnp.concatenate(scores, axis=0) * scale)
        s = jnp.where(mask, s, -1e30)
        top = jnp.max(s, axis=1, keepdims=True)
        thigh = high(top)
        tlow = high(top - thigh)
        p = jnp.where(mask, jnp.exp(s - (thigh + tlow)), 0.0)
        total = jnp.sum(p, axis=1, keepdims=True)
        ohigh = high(total)
        olow = total - ohigh
        p = p.astype(bf16)
        for u in range(4):
            mixed = jnp.dot(p[u * 32 : (u + 1) * 32], parts[u], preferred_element_type=f32)
            res = jnp.where(lane16 < PAIR, mixed[0:16], mixed[16:32])
            for i in range(2):
                rows = slice(u * 32 + i * 16, u * 32 + (i + 1) * 16)
                for n, col in enumerate((thigh, tlow, ohigh, olow)):
                    res = jnp.where(lane16 == i * PAIR + n, col[rows], res)
            for g in range(4):
                rsend[g * 32 + chunks[u]] = res[g * 4 : (g + 1) * 4].astype(bf16)
        scatter(rsend, rin, rs, rr, step)
        return carry

    lax.fori_loop(0, 8, page_step, 0)
    rin[me] = rsend[me]

    loads[7].wait()
    loads[8].wait()
    for cp in x3:
        cp.wait_recv()
    hidden = times(mall[...].reshape(128, D), inw[...])
    active = (0.5 * hidden * (1.0 + lax.erf(hidden * np.float32(math.sqrt(0.5))))).astype(bf16)

    def mlp_step(step, carry):
        lanes = pl.ds(pl.multiple_of(step * 768, 128), 768)
        out = jnp.dot(active, outw[:, lanes], preferred_element_type=f32).astype(bf16).reshape(4, 2, 16, 768)
        mp[0, :, :, lanes] = out[:, 0]
        mp[1, :, :, lanes] = out[:, 1]
        return carry

    lax.fori_loop(0, 8, mlp_step, 0)
    m_swap = remote(mp.at[1 - c], mrecv, ms, mr, y, partner)
    m_swap.start()

    m_swap.wait_recv()
    ysend[...] = (mp[c].astype(f32) + mrecv[...].astype(f32)).astype(bf16)
    y_out = [remote(ysend.at[y_at(s)], yrecv.at[y], ys.at[s], yr.at[s], y_at(s), b) for s in range(3)]
    for cp in y_out:
        cp.start()
    yrecv[y] = ysend[y]

    pltpu.make_async_copy(fin.at[others], fin.at[others], fr).wait()
    folded = jnp.dot(route_ref[...], fin[...].reshape(512, CHUNK), preferred_element_type=f32)
    for j in range(PPR):
        fold_ref[j] = folded[j * 32 : (j + 1) * 32].astype(bf16)
    f_score = []
    for j in range(PPR):
        fprod = folded[j * 32 : (j + 1) * 32] * query
        ok = dropped[j] > 0.5
        f_score.append([
            jnp.where(ok, jnp.sum(jnp.where(k_0, fprod, zero), axis=1, keepdims=True) * scale, -1e30),
            jnp.where(ok, jnp.sum(jnp.where(k_1, fprod, zero), axis=1, keepdims=True) * scale, -1e30),
        ])
    pltpu.make_async_copy(rin.at[others], rin.at[others], rr).wait()
    parts = jnp.dot(route_ref[...], rin[...].reshape(512, CHUNK), preferred_element_type=f32)
    tops = []
    for i in range(2):
        top = own_score[i]
        p_top = []
        for j in range(PPR):
            rows = parts[j * 32 : (j + 1) * 32]
            ok = kept[j] > 0.5
            p_top.append(jnp.where(ok, rows[:, i * PAIR : i * PAIR + 1] + rows[:, i * PAIR + 1 : i * PAIR + 2], -1e30))
            top = jnp.maximum(top, jnp.maximum(p_top[j], f_score[j][i]))
        tops.append((top, p_top))
    is_first = lane < PAIR
    mixed = zero
    total = zero
    for j in range(PPR):
        rows = parts[j * 32 : (j + 1) * 32]
        ok = kept[j] > 0.5
        w = [jnp.where(ok, jnp.exp(tops[i][1][j] - tops[i][0]), 0.0) for i in range(2)]
        e = [jnp.exp(f_score[j][i] - tops[i][0]) for i in range(2)]
        sums = [
            w[i] * (rows[:, i * PAIR + 2 : i * PAIR + 3] + rows[:, i * PAIR + 3 : i * PAIR + 4]) + e[i] for i in range(2)
        ]
        mixed = mixed + jnp.where(is_first, w[0], w[1]) * rows + jnp.where(is_first, e[0], e[1]) * folded[j * 32 : (j + 1) * 32]
        total = total + jnp.where(is_first, sums[0], sums[1])
    o = [jnp.exp(own_score[i] - tops[i][0]) for i in range(2)]
    own_exp = jnp.where(is_first, o[0], o[1])
    mixed = (mixed + own_exp * new_value) / (total + own_exp)
    attended = jnp.where(lane < HD, pltpu.roll(mixed, CHUNK - HD, 1), pltpu.roll(mixed, CHUNK - PAIR, 1))[:, 0:PAIR].astype(bf16)
    loads[9].wait()

    def dense_step(step, carry):
        lanes = pl.ds(pl.multiple_of(step * 1536, 128), 1536)
        out = jnp.dot(attended, dense[:, lanes], preferred_element_type=f32)
        apart[0, :, lanes] = out[0:16]
        apart[1, :, lanes] = out[16:32]
        return carry

    lax.fori_loop(0, 4, dense_step, 0)
    asend[...] = apart[1 - c].astype(bf16)
    a_swap = remote(asend, arecv, ats, atr, y, partner)
    a_swap.start()
    for cp in y_out:
        cp.wait_recv()
    summed = apart[c] + yrecv[0].astype(f32) + yrecv[1].astype(f32) + yrecv[2].astype(f32) + yrecv[3].astype(f32)
    a_swap.wait_recv()
    tsend[...] = (summed + arecv[...].astype(f32)).astype(bf16)

    def send_t(step, carry):
        other = lax.rem(chip + 1 + step, 16)
        remote(
            tsend.at[:, pl.ds(pl.multiple_of(other * CHUNK, 128), CHUNK)], trecv.at[chip], ts, tr, y, other * 2 + c
        ).start()
        return carry

    lax.fori_loop(0, 15, send_t, 0)
    trecv[chip] = tsend[:, pl.ds(pl.multiple_of(chip * CHUNK, 128), CHUNK)]
    fifteen = pl.ds(0, 15)
    pltpu.make_async_copy(trecv.at[fifteen], trecv.at[fifteen], tr).wait()
    oall[c] = jnp.sum(trecv[...].astype(f32), axis=0).astype(bf16)
    o_swap = remote(oall.at[c], oall.at[c], os, orr, y, partner)
    o_swap.start()
    o_swap.wait_recv()
    result = oall[...].astype(f32).reshape(32, CHUNK)
    sum_ref[...] = jnp.where(c == 0, result, pltpu.roll(result, PAIR, 1))[:, 0:PAIR].astype(bf16)

    for cp in a1 + b1 + a2 + b2 + swaps + w_sends + x2 + x3 + y_out + [m_swap, a_swap, o_swap]:
        cp.wait_send()
    pltpu.make_async_copy(xb.at[rest], xb.at[rest], xs).wait()
    for ref, sem in ((qsend, qs), (fsend, fs), (rsend, rs)):
        pltpu.make_async_copy(ref.at[others], ref.at[others], sem).wait()
    pltpu.make_async_copy(trecv.at[fifteen], trecv.at[fifteen], ts).wait()


def step_call(scale, blocks, arrays):
    f32, bf16 = jnp.float32, jnp.bfloat16
    one = pltpu.SemaphoreType.DMA
    sems = lambda n: pltpu.SemaphoreType.DMA((n,))
    rows4 = pltpu.VMEM((128, 4, CHUNK), bf16)
    scratch = [
        pltpu.VMEM((128, 128), f32), pltpu.VMEM((384, 512), bf16), pltpu.VMEM((288, 512), bf16), pltpu.VMEM((384, PAGE), f32),
        pltpu.VMEM((384, PAGE), bf16), pltpu.VMEM((4, 8, 128), f32), pltpu.VMEM((128, 192), f32),
        pltpu.VMEM((CHUNK, D), bf16), pltpu.VMEM((CHUNK, D), bf16), pltpu.VMEM((PAIR, D), bf16),
        pltpu.VMEM((PAIR, D), bf16), pltpu.VMEM((PAIR, D), bf16), pltpu.VMEM((PAIR, D), bf16),
        pltpu.VMEM((192, 2 * D), bf16), pltpu.VMEM((32, 32, PAIR), bf16), pltpu.VMEM((32, D), f32), pltpu.VMEM((32, D), bf16),
        pltpu.VMEM((4, 32, D), bf16), pltpu.VMEM((2, 4, 4, NREC, D), bf16), pltpu.VMEM((4, 8, 128), f32),
        pltpu.VMEM((48, 192), bf16), pltpu.VMEM((288, CHUNK), bf16), pltpu.VMEM((256, 256), f32),
        rows4, rows4, rows4, rows4, rows4, rows4,
        pltpu.VMEM((2, 4, 16, D), bf16), pltpu.VMEM((4, 16, D), bf16), pltpu.VMEM((4, 16, D), bf16), pltpu.VMEM((4, 16, D), bf16),
        pltpu.VMEM((2, 16, D), f32), pltpu.VMEM((16, D), bf16), pltpu.VMEM((16, D), bf16), pltpu.VMEM((16, D), bf16),
        pltpu.VMEM((16, 16, CHUNK), bf16), pltpu.VMEM((2, 16, CHUNK), bf16),
        sems(10), one, one, sems(3), sems(3), sems(3), sems(3),
        sems(3), sems(3), sems(3), sems(3), sems(3), sems(3), sems(3), sems(3), sems(4), sems(4), sems(4), sems(4), sems(3), sems(3),
        one, one, one, one, one, one, one, one, sems(3), sems(3), one, one, one, one, one, one, one,
    ]
    return pl.pallas_call(
        functools.partial(step_kernel, scale),
        out_shape=[jax.ShapeDtypeStruct((32, PAIR), bf16), jax.ShapeDtypeStruct((PPR, 32, CHUNK), bf16)],
        in_specs=[VMEM_SPEC] * len(blocks) + [pl.BlockSpec(memory_space=pl.ANY)] * len(arrays),
        out_specs=[VMEM_SPEC] * 2,
        scratch_shapes=scratch,
        compiler_params=pltpu.CompilerParams(collective_id=0, has_side_effects=True, vmem_limit_bytes=58 << 20),
        name="decode_step",
    )(*blocks, *arrays)


def on_device(
    new_hidden,
    attn_gain,
    mlp_gain,
    qkv_weight,
    dense_weight,
    in_weight,
    out_weight,
    page_store,
    held_states,
    fold_weights,
    page_table,
    lengths,
    keep_slots,
    fold_index,
    recompute_list,
):
    rows = lengths.shape[0]
    pages_dev = page_store.shape[0]
    scale = 1.0 / math.sqrt(HD)
    bf16 = jnp.bfloat16
    lane = np.arange(CHUNK)[:, None]
    tokens = np.arange(pages_dev * PAGE)[None, :] % PAGE
    spread = np.zeros((CHUNK, 4, 256), np.float32)
    for i in range(2):
        t = lane - (i * PAIR + HD)
        spread[:, i, : pages_dev * PAGE] = (t == tokens) | (t == tokens + PAGE)
        spread[:, 2 + i, : pages_dev * PAGE] = t == tokens + 2 * PAGE
    spread = jnp.asarray(spread.reshape(CHUNK, 1024), bf16)
    tile = jnp.asarray((np.arange(128)[:, None] == tokens).astype(np.float32), bf16)
    turn = jnp.asarray(rotary_rows(CHUNK, (0, PAIR)))
    fresh_turn = jnp.asarray(rotary_rows(256, (0, HD)))

    blocks = (
        new_hidden, held_states.reshape(NREC, D), attn_gain.reshape(1, D), mlp_gain.reshape(1, D), fold_weights, page_table.T,
        lengths.reshape(1, rows), keep_slots.T, fold_index.T, recompute_list.T, spread, tile, turn, fresh_turn,
    )
    arrays = (qkv_weight.T, dense_weight, in_weight.T, out_weight, page_store.reshape(pages_dev * PAGE, 2 * D))
    update, folded = step_call(scale, blocks, arrays)
    return (update, folded.transpose(1, 0, 2))


def solution(mesh):
    in_specs = (
        P("pages", "blk"),
        P(),
        P(),
        P(None, "blk"),
        P("blk", None),
        P(None, ("pages", "blk")),
        P(("pages", "blk"), None),
        P(("pages", "blk"), None, None),
        P(("pages", "blk"), None, None),
        P(),
        P(),
        P("pages"),
        P("pages", None),
        P("pages", None),
        P("pages", None),
    )
    out_specs = (P("pages", "blk"), P("pages", None, "blk"))
    return jax.shard_map(
        on_device, mesh=mesh, in_specs=in_specs, out_specs=out_specs, check_vma=False
    )
```

```python
import functools
import math

import jax
import jax.numpy as jnp
import numpy as np
from jax import lax
from jax.experimental import pallas as pl
from jax.experimental.pallas import tpu as pltpu
from jax.sharding import PartitionSpec as P

D = 6144
H = 64
HD = 96
ROT = 24
PAGE = 16
PPR = 12
KP = 5
NREC = 8
NF = 8
PAIR = 2 * HD
EPSILON = 1e-05
ROT_BASE = 10000.0
MESH = pl.DeviceIdType.MESH
VMEM_SPEC = pl.BlockSpec(memory_space=pltpu.VMEM)


CHUNK = 2 * PAIR


def rotary_rows(lanes, starts):
    out = np.zeros((8, lanes), np.float32)
    half = ROT // 2
    freq = (np.float32(ROT_BASE) ** (np.float32(-2.0) * np.arange(half, dtype=np.float32) / np.float32(ROT))).astype(np.float32)
    for start in starts:
        out[0, start : start + half] = freq
        out[0, start + half : start + ROT] = freq
        out[1, start + half : start + ROT] = 1.0
        out[2, start : start + half] = 1.0
    return out


def rotated(values, position, rows):
    lanes = values.shape[1]
    angle = position * rows[0:1]
    sine = jnp.sin(angle)
    return (
        values * jnp.cos(angle)
        + pltpu.roll(values, ROT // 2, 1) * (sine * rows[1:2])
        - pltpu.roll(values, lanes - ROT // 2, 1) * (sine * rows[2:3])
    )


def normed(values):
    centered = values - jnp.mean(values, axis=-1, keepdims=True)
    spread = jnp.mean(centered * centered, axis=-1, keepdims=True)
    return centered * lax.rsqrt(spread + EPSILON)


def times(left, right):
    return lax.dot_general(left, right, (((1,), (1,)), ((), ())), preferred_element_type=jnp.float32)


def over_rows(left, right):
    return lax.dot_general(left, right, (((0,), (0,)), ((), ())), preferred_element_type=jnp.float32)


def high(values):
    return values.astype(jnp.bfloat16).astype(jnp.float32)


def step_kernel(
    scale,
    x_ref, held_ref, again_ref, mgain_ref, fw_ref, table_ref, length_row, keep_rows, fold_rows, rec_rows, spread_ref, tile_ref,
    turn_ref, fturn_ref, regroup_ref,
    qkv_hbm, dense_hbm, in_hbm, out_hbm, page_hbm,
    sum_ref, fold_ref,
    exp_ref, gt, route_ref, place_ref, fslot, fsel, w_ref, own8, wq, wkv, wk, dense, inw, outw, page, xb, xg, nattn, mall, hbuf, wall, wexp, qb, ks,
    q1send, q1in, q2send, q2in, f1send, f1in, f2send, f2in, r1send, r1in, r2send, r2in, mp, mrecv, ysend, yrecv, apart, asend, arecv, tsend, trecv, oall,
    load, xs, xr, x2s, x2r, x3s, x3r, as1, ar1, bs1, br1, as2, ar2, bs2, br2, cs, cr, ds, dr, ws, wr,
    q1s, q1r, q2s, q2r, f1s, f1r, f2s, f2r, r1s, r1r, r2s, r2r, ms, mr, ys, yr, ats, atr, ts, tr, os, orr, owns,
):
    f32, bf16 = jnp.float32, jnp.bfloat16
    y = lax.axis_index("pages")
    b = lax.axis_index("blk")
    me = y * 32 + b
    z = lax.div(b, 8)
    x = lax.rem(lax.div(b, 2), 4)
    c = lax.rem(b, 2)
    chip = lax.div(b, 2)

    loads = [
        pltpu.make_async_copy(page_hbm, page, load.at[0]),
        pltpu.make_async_copy(qkv_hbm.at[pl.ds(0, PAIR)], wq.at[pl.ds(0, PAIR)], load.at[1]),
        pltpu.make_async_copy(qkv_hbm.at[pl.ds(288, PAIR)], wq.at[pl.ds(PAIR, PAIR)], load.at[5]),
        pltpu.make_async_copy(qkv_hbm.at[pl.ds(HD, PAIR)], wkv.at[pl.ds(0, PAIR)], load.at[6]),
        pltpu.make_async_copy(qkv_hbm.at[pl.ds(288 + HD, PAIR)], wkv.at[pl.ds(PAIR, PAIR)], load.at[7]),
        pltpu.make_async_copy(qkv_hbm.at[pl.ds(HD, HD)], wk.at[pl.ds(0, HD)], load.at[8]),
        pltpu.make_async_copy(qkv_hbm.at[pl.ds(288 + HD, HD)], wk.at[pl.ds(HD, HD)], load.at[9]),
        pltpu.make_async_copy(in_hbm, inw, load.at[2]),
        pltpu.make_async_copy(out_hbm, outw, load.at[3]),
        pltpu.make_async_copy(dense_hbm, dense, load.at[4]),
    ]
    for cp in loads:
        cp.start()

    barrier = pltpu.get_barrier_semaphore()

    def hello_plane(step, carry):
        pl.semaphore_signal(barrier, inc=1, device_id={"pages": y, "blk": lax.rem(b + 1 + step, 32)}, device_id_type=MESH)
        return carry

    def hello_y(step, carry):
        pl.semaphore_signal(barrier, inc=1, device_id={"pages": lax.rem(y + 1 + step, 4), "blk": b}, device_id_type=MESH)
        return carry

    lax.fori_loop(0, 3, hello_y, 0)
    lax.fori_loop(0, 31, hello_plane, 0)
    hbuf[c, z, x] = (normed(held_ref[...].astype(f32)) * again_ref[...]).astype(bf16)
    xb[b] = x_ref[...]
    pl.semaphore_wait(barrier, 34)

    def remote(src, dst, s, r, pages_id, blk_id):
        return pltpu.make_async_remote_copy(
            src_ref=src, dst_ref=dst, send_sem=s, recv_sem=r, device_id={"pages": pages_id, "blk": blk_id}, device_id_type=MESH
        )

    def y_at(step):
        return lax.rem(y + 1 + step, 4)

    def x_blk(step):
        return z * 8 + lax.rem(x + 1 + step, 4) * 2 + c

    def z_blk(step):
        return lax.rem(z + 1 + step, 4) * 8 + x * 2 + c

    partner = b + 1 - 2 * c
    half = held_ref.shape[1] // 2
    la = pl.ds(0, half)
    lb = pl.ds(half, half)
    waits = []

    a1 = [remote(hbuf.at[c, z, x, :, la], hbuf.at[c, z, x, :, la], as1.at[s], ar1.at[s], y, x_blk(s)) for s in range(3)]
    b1 = [remote(hbuf.at[c, z, x, :, lb], hbuf.at[c, z, x, :, lb], bs1.at[s], br1.at[s], y, z_blk(s)) for s in range(3)]
    for s in range(3):
        a1[s].start()
        b1[s].start()

    def send_x(step, carry):
        remote(x_ref, xb.at[b], xs, xr, y, lax.rem(b + 1 + step, 32)).start()
        return carry

    lax.fori_loop(0, 31, send_x, 0)
    def scatter(src, dst, s, r, step):
        def one(n, carry):
            chunk = lax.rem(b + 1 + step * 4 + n, 32)
            remote(src.at[chunk], dst.at[b], s, r, y, chunk).start()
            return carry

        lax.fori_loop(0, 4 - lax.div(step, 7), one, 0)

    def send_y(src, dst, s, r):
        copies = [remote(src.at[y_at(i)], dst.at[y], s.at[i], r.at[i], y_at(i), b) for i in range(3)]
        for cp in copies:
            cp.start()
        return copies

    rest = pl.ds(0, 31)

    def arrived(ref, sem):
        pltpu.make_async_copy(ref.at[rest], ref.at[rest], sem).wait()

    def chunk_at(step, u):
        chunk = lax.rem(b + 1 + step * 4 + u, 32)
        return chunk, page[:, pl.ds(pl.multiple_of(chunk * CHUNK, 128), CHUNK)]

    gt[...] = jnp.zeros_like(gt)
    gt[0:NREC, 0:32] = rec_rows[...].astype(f32)
    gt[8 : 8 + KP, 0:32] = keep_rows[...].astype(f32)
    gt[13:14, 0:32] = length_row[...].astype(f32)
    gt[16 : 16 + PPR, 0:32] = fold_rows[...].astype(f32)
    every = table_ref[...].astype(f32)
    mine = jnp.zeros((PPR, 32), f32)
    for g in range(4):
        mine = mine + jnp.where(y == g, every[:, g * 32 : (g + 1) * 32], 0.0)
    gt[32 : 32 + PPR, 0:32] = mine
    by_request = jnp.transpose(gt[...])[0:32]
    length_col = by_request[:, 13:14]
    lane384 = lax.broadcasted_iota(jnp.int32, (32, 384), 1)
    lane128 = lax.broadcasted_iota(jnp.int32, (32, 128), 1)
    token16 = lax.broadcasted_iota(jnp.int32, (32, PAGE), 1)
    nth_page = jnp.bitwise_and(token16, 3)
    target = jnp.where(nth_page < 3, (lax.shift_right_logical(token16, 2) * 32 + b) * 3 + nth_page, -1)
    numbers = by_request
    any_slot = jnp.zeros((32, 384), f32)
    kept, dropped = [], []
    for j in range(PPR):
        column = by_request[:, 32 + j : 33 + j]
        below = jnp.zeros((32, 32), f32)
        for other in range(PPR):
            below = below + jnp.where(gt[32 + other : 33 + other, 0:32] < column, 1.0, 0.0)
        place = jnp.sum(below, axis=1, keepdims=True).astype(jnp.int32)
        hit = jnp.where(place == lane384, 1.0, 0.0)
        any_slot = any_slot + hit
        route_ref[j * 32 : (j + 1) * 32, :] = hit.astype(bf16)
        coarse = lax.shift_right_logical(place, 4).astype(f32)
        fine = jnp.bitwise_and(place, 15).astype(f32)
        numbers = jnp.where(lane128 == 48 + j, coarse, jnp.where(lane128 == 64 + j, fine, numbers))
        is_kept = by_request[:, 8:9] == j
        for m in range(1, KP):
            is_kept = jnp.logical_or(is_kept, by_request[:, 8 + m : 9 + m] == j)
        kept.append(jnp.where(is_kept, 1.0, 0.0))
        dropped.append(jnp.where(jnp.logical_and(jnp.logical_not(is_kept), length_col > j * PAGE), 1.0, 0.0))
        row = jnp.zeros((32, PAGE), f32)
        for f in range(NF):
            row = row + jnp.where(by_request[:, 16 + j : 17 + j] == f, fw_ref[f : f + 1, :], 0.0)
        live = jnp.logical_and(dropped[j] > 0.5, (token16 + j * PAGE).astype(f32) < length_col)
        fslot[j * 32 : (j + 1) * 32, :] = jnp.where(live, row, 0.0)
        fsel[j * 32 : (j + 1) * 32, :] = jnp.where(place == target, 1.0, 0.0).astype(bf16)
    for cp in a1:
        cp.wait_recv()
    a2 = [remote(hbuf.at[c, z, :, :, la], hbuf.at[c, z, :, :, la], as2.at[s], ar2.at[s], y, z_blk(s)) for s in range(3)]
    for cp in a2:
        cp.start()
    for cp in b1:
        cp.wait_recv()
    b2 = [remote(hbuf.at[c, :, x, :, lb], hbuf.at[c, :, x, :, lb], bs2.at[s], br2.at[s], y, x_blk(s)) for s in range(3)]
    for cp in b2:
        cp.start()
    swaps = [
        remote(hbuf.at[c, z, :, :, la], hbuf.at[c, z, :, :, la], cs.at[3], cr.at[3], y, partner),
        remote(hbuf.at[c, :, x, :, lb], hbuf.at[c, :, x, :, lb], ds.at[3], dr.at[3], y, partner),
    ]
    for cp in swaps:
        cp.start()

    place_ref[0:32, :] = any_slot.astype(bf16)
    wanted = fslot[...]
    wanted1 = high(wanted)
    wanted2 = high(wanted - wanted1)
    picked = jnp.zeros((16, PAGE), f32)
    for w in (wanted1, wanted2, wanted - wanted1 - wanted2):
        picked = picked + over_rows(fsel[...], w.astype(bf16))
    w_ref[...] = jnp.zeros_like(w_ref)
    for g in range(4):
        w_ref[g, 0:4, 0:PAGE] = picked[g * 4 : (g + 1) * 4]
    wall[y] = w_ref[y]
    w_sends = [remote(w_ref.at[y_at(s)], wall.at[y], ws.at[s], wr.at[s], y_at(s), b) for s in range(3)]
    for cp in w_sends:
        cp.start()

    row256 = lax.broadcasted_iota(jnp.int32, (256, 1), 0)
    request = jnp.bitwise_and(lax.shift_right_logical(row256, 3), 15) * 2 + lax.shift_right_logical(row256, 7)
    repeat = jnp.where(lax.broadcasted_iota(jnp.int32, (256, 32), 1) == request, 1.0, 0.0).astype(bf16)
    listed = jnp.dot(repeat, numbers.astype(bf16), preferred_element_type=f32)
    at256 = lax.broadcasted_iota(jnp.int32, (256, 128), 1)

    def entry(at):
        return jnp.sum(jnp.where(at256 == at, listed, 0.0), axis=1, keepdims=True).astype(jnp.int32)

    rec = entry(jnp.bitwise_and(row256, 7))
    rec_slot = entry(8 + lax.shift_right_logical(rec, 4))
    rec_token = jnp.bitwise_and(rec, 15)
    rec_place = entry(48 + rec_slot) * 16 + entry(64 + rec_slot)
    rec_pos = (rec_slot * PAGE + rec_token).astype(f32)
    place_ref[32:288, :] = jnp.where(lax.broadcasted_iota(jnp.int32, (256, 384), 1) == rec_place, 1.0, 0.0).astype(bf16)
    owner_lane = lax.shift_right_logical(lax.broadcasted_iota(jnp.int32, (PPR, 128), 1), 5).astype(f32)
    token_page = lax.shift_right_logical(lax.broadcasted_iota(jnp.int32, (16, 192), 1), 4)
    place_row = lax.broadcasted_iota(jnp.int32, (16, 192), 0).astype(f32)
    groups = []
    owned = jnp.zeros((16, 192), f32)
    for p in range(12):
        found = jnp.where(table_ref[...] == me * 12 + p, owner_lane, 0.0)
        group = jnp.sum(jnp.sum(found, axis=1, keepdims=True), axis=0, keepdims=True)
        nth = jnp.zeros((1, 1), f32)
        for g in groups:
            nth = nth + jnp.where(g == group, 1.0, 0.0)
        groups.append(group)
        owned = owned + jnp.where(jnp.logical_and(token_page == p, place_row == group * 4.0 + nth), 1.0, 0.0)
    for i in range(8):
        own8[i * 16 : (i + 1) * 16, :] = owned

    pltpu.make_async_copy(xb.at[pl.ds(0, 31)], xb.at[pl.ds(0, 31)], xr).wait()
    for m in range(16):
        both = jnp.concatenate([xb[2 * m].astype(f32), xb[2 * m + 1].astype(f32)], axis=1)
        xg[:, m * CHUNK : (m + 1) * CHUNK] = both
    unit = normed(xg[...])
    nattn[...] = (unit * again_ref[...]).astype(bf16)
    mall[y] = (unit * mgain_ref[...]).astype(bf16)
    lc = pl.ds(pl.multiple_of(c * half, 128), half)
    x2 = [remote(mall.at[y, :, lc], mall.at[y, :, lc], x2s.at[s], x2r.at[s], y_at(s), b) for s in range(3)]
    for cp in x2:
        cp.start()

    for cp in loads[1:5]:
        cp.wait()
    lane = lax.broadcasted_iota(jnp.int32, (32, CHUNK), 1)
    zero = jnp.zeros((32, CHUNK), f32)
    k_0, k_1 = lane < HD, jnp.logical_and(lane >= PAIR, lane < PAIR + HD)
    is_key = jnp.logical_or(k_0, k_1)
    normal = nattn[...]
    query = jnp.where(is_key, high(rotated(times(normal, wq[...]), length_col, turn_ref[...])), zero)
    pairs = high(rotated(times(normal, wkv[...]), length_col, turn_ref[...]))
    new_key = jnp.where(is_key, pairs, zero)
    new_value = jnp.where(is_key, zero, pairs)
    q_fresh = jnp.where(lane < HD, query, pltpu.roll(query, CHUNK - HD, 1))[:, 0:PAIR].astype(bf16)
    qb[0:32, :] = query.astype(bf16)
    own_prod = query * new_key
    own_score = [jnp.sum(jnp.where(keep, own_prod, zero), axis=1, keepdims=True) * scale for keep in (k_0, k_1)]

    for s in range(3):
        a2[s].wait_recv()
        back = lax.rem(z + 3 - s, 4)
        swaps.append(remote(hbuf.at[c, back, :, :, la], hbuf.at[c, back, :, :, la], cs.at[s], cr.at[s], y, partner))
        swaps[-1].start()
        b2[s].wait_recv()
        back = lax.rem(x + 3 - s, 4)
        swaps.append(remote(hbuf.at[c, :, back, :, lb], hbuf.at[c, :, back, :, lb], ds.at[s], dr.at[s], y, partner))
        swaps[-1].start()

    x3 = []
    for s in range(3):
        x2[s].wait_recv()
        back = lax.rem(y + 3 - s, 4)
        x3.append(remote(mall.at[back, :, lc], mall.at[back, :, lc], x3s.at[s], x3r.at[s], y, partner))
        x3[-1].start()

    loads[5].wait()
    loads[6].wait()

    def keys_of(core):
        ks[pl.ds(pl.multiple_of(core * 128, 128), 128), 0:PAIR] = times(hbuf[core].reshape(128, D), wk[...])

    ks[:, PAIR:] = jnp.zeros((256, 256 - PAIR), f32)
    keys_of(c)
    for cp in swaps:
        cp.wait_recv()
    keys_of(1 - c)
    fresh = high(rotated(ks[...], rec_pos, fturn_ref[...]))[:, 0:PAIR]
    prod = fresh * jnp.dot(repeat, q_fresh, preferred_element_type=f32)
    flane = lax.broadcasted_iota(jnp.int32, (256, PAIR), 1)
    score0 = jnp.sum(jnp.where(flane < HD, prod, 0.0), axis=1, keepdims=True) * scale
    score1 = jnp.sum(jnp.where(flane < HD, 0.0, prod), axis=1, keepdims=True) * scale
    wlane = lax.broadcasted_iota(jnp.int32, (256, CHUNK), 1)
    first = wlane < PAIR
    rel = jnp.where(first, wlane, wlane - PAIR) - HD
    score = jnp.where(first, score0, score1)
    shigh = high(score)
    kind = jnp.where(rel < PAGE, shigh, jnp.where(rel < 2 * PAGE, score - shigh, 1.0))
    token = jnp.where(rel < PAGE, rel, jnp.where(rel < 2 * PAGE, rel - PAGE, rel - 2 * PAGE))
    hit = jnp.logical_and(jnp.logical_and(rel >= 0, rel < 3 * PAGE), token == rec_token)
    qb[32:288, :] = jnp.where(hit, kind, 0.0).astype(bf16)
    message = over_rows(place_ref[...], qb[...]).astype(bf16)
    q1send[...] = message.reshape(4, 96, CHUNK)
    q_out = send_y(q1send, q1in, q1s, q1r)
    q1in[y] = q1send[y]

    loads[7].wait()
    loads[8].wait()
    for cp in x3:
        cp.wait_recv()
    hidden = times(mall[...].reshape(128, D), inw[...])
    active = (0.5 * hidden * (1.0 + lax.erf(hidden * np.float32(math.sqrt(0.5))))).astype(bf16)

    def mlp_step(step, carry):
        lanes = pl.ds(pl.multiple_of(step * 768, 128), 768)
        out = jnp.dot(active, outw[:, lanes], preferred_element_type=f32).astype(bf16).reshape(4, 2, 16, 768)
        mp[0, :, :, lanes] = out[:, 0]
        mp[1, :, :, lanes] = out[:, 1]
        return carry

    lax.fori_loop(0, 8, mlp_step, 0)
    m_swap = remote(mp.at[1 - c], mrecv, ms, mr, y, partner)
    m_swap.start()

    for cp in q_out:
        cp.wait_recv()
    message = jnp.dot(regroup_ref[...], q1in[...].reshape(384, CHUNK), preferred_element_type=f32).astype(bf16)
    q2send[...] = message.reshape(32, 16, CHUNK)

    def send_q(step, carry):
        other = lax.rem(b + 1 + step, 32)
        remote(q2send.at[other], q2in.at[b], q2s, q2r, y, other).start()
        return carry

    lax.fori_loop(0, 31, send_q, 0)
    q2in[b] = q2send[b]

    for cp in w_sends:
        cp.wait_recv()
    loads[0].wait()
    own = own8[0:16, :] > 0.5
    weights = wall[:, 0:4, :].reshape(16, 128)
    w1 = high(weights)
    w2 = high(weights - w1)
    w3 = weights - w1 - w2
    for i, w in enumerate((w1, w2, w3)):
        wide = jnp.dot(w.astype(bf16), tile_ref[...], preferred_element_type=f32)
        wexp[i * 16 : (i + 1) * 16, :] = jnp.where(own, wide, 0.0).astype(bf16)

    def fold_step(step, carry):
        for u in range(4):
            chunk, part = chunk_at(step, u)
            out = jnp.dot(wexp[...], part, preferred_element_type=f32)
            out = out[0:16] + out[16:32] + out[32:48]
            f1send[chunk] = out.astype(bf16)
        scatter(f1send, f1in, f1s, f1r, step)
        return carry

    lax.fori_loop(0, 8, fold_step, 0)
    f1in[b] = f1send[b]

    arrived(q2in, q2r)
    lane16 = lax.broadcasted_iota(jnp.int32, (16, CHUNK), 1)
    key0 = lane16 < HD
    key1 = jnp.logical_and(lane16 >= PAIR, lane16 < PAIR + HD)

    def page_step(step, carry):
        chunks, parts, wides = [], [], []
        for u in range(4):
            chunk, part = chunk_at(step, u)
            chunks.append(chunk)
            parts.append(part)
            wides.append(q2in[chunk].astype(f32))
        scores, again, flags = [], [], []
        for u in range(4):
            q2 = jnp.concatenate([jnp.where(key0, wides[u], 0.0), jnp.where(key1, wides[u], 0.0)], axis=0).astype(bf16)
            scores.append(times(q2, parts[u]))
            ex = [exp_ref[chunks[u], :, n * 256 : n * 256 + 192] for n in range(3)]
            again += [ex[0], ex[1]]
            flags += [ex[2], ex[2]]
        mask = own8[...] > 0.5
        s = jnp.where(jnp.concatenate(flags, axis=0) > 0.5, jnp.concatenate(again, axis=0), jnp.concatenate(scores, axis=0) * scale)
        s = jnp.where(mask, s, -1e30)
        top = jnp.max(s, axis=1, keepdims=True)
        thigh = high(top)
        tlow = high(top - thigh)
        p = jnp.where(mask, jnp.exp(s - (thigh + tlow)), 0.0)
        total = jnp.sum(p, axis=1, keepdims=True)
        ohigh = high(total)
        olow = total - ohigh
        p = p.astype(bf16)
        for u in range(4):
            mixed = jnp.dot(p[u * 32 : (u + 1) * 32], parts[u], preferred_element_type=f32)
            res = jnp.where(lane16 < PAIR, mixed[0:16], mixed[16:32])
            for i in range(2):
                rows = slice(u * 32 + i * 16, u * 32 + (i + 1) * 16)
                for n, col in enumerate((thigh, tlow, ohigh, olow)):
                    res = jnp.where(lane16 == i * PAIR + n, col[rows], res)
            r1send[chunks[u]] = res.astype(bf16)
        scatter(r1send, r1in, r1s, r1r, step)
        return carry

    exp_ref[...] = jnp.dot(q2in[...].reshape(512, CHUNK), spread_ref[...], preferred_element_type=f32).reshape(32, 16, 768)
    lax.fori_loop(0, 4, page_step, 0)

    m_swap.wait_recv()
    ysend[...] = (mp[c].astype(f32) + mrecv[...].astype(f32)).astype(bf16)
    y_out = [remote(ysend.at[y_at(s)], yrecv.at[y], ys.at[s], yr.at[s], y_at(s), b) for s in range(3)]
    for cp in y_out:
        cp.start()
    yrecv[y] = ysend[y]

    arrived(f1in, f1r)
    f2send[...] = over_rows(regroup_ref[...], f1in[...].reshape(512, CHUNK)).astype(bf16).reshape(4, 96, CHUNK)
    f_out = send_y(f2send, f2in, f2s, f2r)
    f2in[y] = f2send[y]
    lax.fori_loop(4, 8, page_step, 0)
    r1in[b] = r1send[b]
    arrived(r1in, r1r)
    r2send[...] = over_rows(regroup_ref[...], r1in[...].reshape(512, CHUNK)).astype(bf16).reshape(4, 96, CHUNK)
    r_out = send_y(r2send, r2in, r2s, r2r)
    r2in[y] = r2send[y]


    for cp in f_out:
        cp.wait_recv()
    folded = jnp.dot(route_ref[...], f2in[...].reshape(384, CHUNK), preferred_element_type=f32)
    for j in range(PPR):
        fold_ref[j] = folded[j * 32 : (j + 1) * 32].astype(bf16)
    f_score = []
    for j in range(PPR):
        fprod = folded[j * 32 : (j + 1) * 32] * query
        ok = dropped[j] > 0.5
        f_score.append([
            jnp.where(ok, jnp.sum(jnp.where(k_0, fprod, zero), axis=1, keepdims=True) * scale, -1e30),
            jnp.where(ok, jnp.sum(jnp.where(k_1, fprod, zero), axis=1, keepdims=True) * scale, -1e30),
        ])
    for cp in r_out:
        cp.wait_recv()
    parts = jnp.dot(route_ref[...], r2in[...].reshape(384, CHUNK), preferred_element_type=f32)
    tops = []
    for i in range(2):
        top = own_score[i]
        p_top = []
        for j in range(PPR):
            rows = parts[j * 32 : (j + 1) * 32]
            ok = kept[j] > 0.5
            p_top.append(jnp.where(ok, rows[:, i * PAIR : i * PAIR + 1] + rows[:, i * PAIR + 1 : i * PAIR + 2], -1e30))
            top = jnp.maximum(top, jnp.maximum(p_top[j], f_score[j][i]))
        tops.append((top, p_top))
    is_first = lane < PAIR
    mixed = zero
    total = zero
    for j in range(PPR):
        rows = parts[j * 32 : (j + 1) * 32]
        ok = kept[j] > 0.5
        w = [jnp.where(ok, jnp.exp(tops[i][1][j] - tops[i][0]), 0.0) for i in range(2)]
        e = [jnp.exp(f_score[j][i] - tops[i][0]) for i in range(2)]
        sums = [
            w[i] * (rows[:, i * PAIR + 2 : i * PAIR + 3] + rows[:, i * PAIR + 3 : i * PAIR + 4]) + e[i] for i in range(2)
        ]
        mixed = mixed + jnp.where(is_first, w[0], w[1]) * rows + jnp.where(is_first, e[0], e[1]) * folded[j * 32 : (j + 1) * 32]
        total = total + jnp.where(is_first, sums[0], sums[1])
    o = [jnp.exp(own_score[i] - tops[i][0]) for i in range(2)]
    own_exp = jnp.where(is_first, o[0], o[1])
    mixed = (mixed + own_exp * new_value) / (total + own_exp)
    attended = jnp.where(lane < HD, pltpu.roll(mixed, CHUNK - HD, 1), pltpu.roll(mixed, CHUNK - PAIR, 1))[:, 0:PAIR].astype(bf16)
    loads[9].wait()

    def dense_step(step, carry):
        lanes = pl.ds(pl.multiple_of(step * 1536, 128), 1536)
        out = jnp.dot(attended, dense[:, lanes], preferred_element_type=f32)
        apart[0, :, lanes] = out[0:16]
        apart[1, :, lanes] = out[16:32]
        return carry

    lax.fori_loop(0, 4, dense_step, 0)
    asend[...] = apart[1 - c].astype(bf16)
    a_swap = remote(asend, arecv, ats, atr, y, partner)
    a_swap.start()
    for cp in y_out:
        cp.wait_recv()
    summed = apart[c] + yrecv[0].astype(f32) + yrecv[1].astype(f32) + yrecv[2].astype(f32) + yrecv[3].astype(f32)
    a_swap.wait_recv()
    tsend[...] = (summed + arecv[...].astype(f32)).astype(bf16)

    def send_t(step, carry):
        other = lax.rem(chip + 1 + step, 16)
        remote(
            tsend.at[:, pl.ds(pl.multiple_of(other * CHUNK, 128), CHUNK)], trecv.at[chip], ts, tr, y, other * 2 + c
        ).start()
        return carry

    lax.fori_loop(0, 15, send_t, 0)
    trecv[chip] = tsend[:, pl.ds(pl.multiple_of(chip * CHUNK, 128), CHUNK)]
    fifteen = pl.ds(0, 15)
    pltpu.make_async_copy(trecv.at[fifteen], trecv.at[fifteen], tr).wait()
    oall[c] = jnp.sum(trecv[...].astype(f32), axis=0).astype(bf16)
    o_swap = remote(oall.at[c], oall.at[c], os, orr, y, partner)
    o_swap.start()
    o_swap.wait_recv()
    result = oall[...].astype(f32).reshape(32, CHUNK)
    sum_ref[...] = jnp.where(c == 0, result, pltpu.roll(result, PAIR, 1))[:, 0:PAIR].astype(bf16)

    for cp in a1 + b1 + a2 + b2 + swaps + w_sends + x2 + x3 + y_out + q_out + f_out + r_out + [m_swap, a_swap, o_swap]:
        cp.wait_send()
    pltpu.make_async_copy(xb.at[rest], xb.at[rest], xs).wait()
    for ref, sem in ((q2send, q2s), (f1send, f1s), (r1send, r1s)):
        pltpu.make_async_copy(ref.at[rest], ref.at[rest], sem).wait()
    pltpu.make_async_copy(trecv.at[fifteen], trecv.at[fifteen], ts).wait()


def step_call(scale, blocks, arrays):
    f32, bf16 = jnp.float32, jnp.bfloat16
    one = pltpu.SemaphoreType.DMA
    sems = lambda n: pltpu.SemaphoreType.DMA((n,))
    by_y = pltpu.VMEM((4, 96, CHUNK), bf16)
    by_blk = pltpu.VMEM((32, 16, CHUNK), bf16)
    scratch = [
        pltpu.VMEM((32, 16, 768), f32), pltpu.VMEM((128, 128), f32), pltpu.VMEM((384, 384), bf16), pltpu.VMEM((288, 384), bf16), pltpu.VMEM((384, PAGE), f32),
        pltpu.VMEM((384, PAGE), bf16), pltpu.VMEM((4, 8, 128), f32), pltpu.VMEM((128, 192), f32),
        pltpu.VMEM((CHUNK, D), bf16), pltpu.VMEM((CHUNK, D), bf16), pltpu.VMEM((PAIR, D), bf16),
        pltpu.VMEM((PAIR, D), bf16), pltpu.VMEM((PAIR, D), bf16), pltpu.VMEM((PAIR, D), bf16),
        pltpu.VMEM((192, 2 * D), bf16), pltpu.VMEM((32, 32, PAIR), bf16), pltpu.VMEM((32, D), f32), pltpu.VMEM((32, D), bf16),
        pltpu.VMEM((4, 32, D), bf16), pltpu.VMEM((2, 4, 4, NREC, D), bf16), pltpu.VMEM((4, 8, 128), f32),
        pltpu.VMEM((48, 192), bf16), pltpu.VMEM((288, CHUNK), bf16), pltpu.VMEM((256, 256), f32),
        by_y, by_y, by_blk, by_blk, by_blk, by_blk, by_y, by_y, by_blk, by_blk, by_y, by_y,
        pltpu.VMEM((2, 4, 16, D), bf16), pltpu.VMEM((4, 16, D), bf16), pltpu.VMEM((4, 16, D), bf16), pltpu.VMEM((4, 16, D), bf16),
        pltpu.VMEM((2, 16, D), f32), pltpu.VMEM((16, D), bf16), pltpu.VMEM((16, D), bf16), pltpu.VMEM((16, D), bf16),
        pltpu.VMEM((16, 16, CHUNK), bf16), pltpu.VMEM((2, 16, CHUNK), bf16),
        sems(10), one, one, sems(3), sems(3), sems(3), sems(3),
        sems(3), sems(3), sems(3), sems(3), sems(3), sems(3), sems(3), sems(3), sems(4), sems(4), sems(4), sems(4), sems(3), sems(3),
        sems(3), sems(3), one, one, one, one, sems(3), sems(3), one, one, sems(3), sems(3), one, one, sems(3), sems(3), one, one, one, one, one, one, one,
    ]
    return pl.pallas_call(
        functools.partial(step_kernel, scale),
        out_shape=[jax.ShapeDtypeStruct((32, PAIR), bf16), jax.ShapeDtypeStruct((PPR, 32, CHUNK), bf16)],
        in_specs=[VMEM_SPEC] * len(blocks) + [pl.BlockSpec(memory_space=pl.ANY)] * len(arrays),
        out_specs=[VMEM_SPEC] * 2,
        scratch_shapes=scratch,
        compiler_params=pltpu.CompilerParams(collective_id=0, has_side_effects=True, vmem_limit_bytes=58 << 20),
        name="decode_step",
    )(*blocks, *arrays)


def on_device(
    new_hidden,
    attn_gain,
    mlp_gain,
    qkv_weight,
    dense_weight,
    in_weight,
    out_weight,
    page_store,
    held_states,
    fold_weights,
    page_table,
    lengths,
    keep_slots,
    fold_index,
    recompute_list,
):
    rows = lengths.shape[0]
    pages_dev = page_store.shape[0]
    scale = 1.0 / math.sqrt(HD)
    bf16 = jnp.bfloat16
    lane = np.arange(CHUNK)[:, None]
    tokens = np.arange(pages_dev * PAGE)[None, :] % PAGE
    spread = np.zeros((CHUNK, 3, 256), np.float32)
    for i in range(2):
        t = lane - (i * PAIR + HD)
        spread[:, i, : pages_dev * PAGE] = (t == tokens) | (t == tokens + PAGE)
    spread[:, 2, : pages_dev * PAGE] = lane - HD == tokens + 2 * PAGE
    spread = jnp.asarray(spread.reshape(CHUNK, 768), bf16)
    tile = jnp.asarray((np.arange(128)[:, None] == tokens).astype(np.float32), bf16)
    regroup = np.zeros((32, 4, 4, 4, 32, 3), np.float32)
    for d in range(32):
        for g in range(4):
            for k in range(3):
                regroup[d, g, k, g, d, k] = 1.0
    regroup = jnp.asarray(regroup.reshape(512, 384), bf16)
    turn = jnp.asarray(rotary_rows(CHUNK, (0, PAIR)))
    fresh_turn = jnp.asarray(rotary_rows(256, (0, HD)))

    blocks = (
        new_hidden, held_states.reshape(NREC, D), attn_gain.reshape(1, D), mlp_gain.reshape(1, D), fold_weights, page_table.T,
        lengths.reshape(1, rows), keep_slots.T, fold_index.T, recompute_list.T, spread, tile, turn, fresh_turn, regroup,
    )
    arrays = (qkv_weight.T, dense_weight, in_weight.T, out_weight, page_store.reshape(pages_dev * PAGE, 2 * D))
    update, folded = step_call(scale, blocks, arrays)
    return (update, folded.transpose(1, 0, 2))


def solution(mesh):
    in_specs = (
        P("pages", "blk"),
        P(),
        P(),
        P(None, "blk"),
        P("blk", None),
        P(None, ("pages", "blk")),
        P(("pages", "blk"), None),
        P(("pages", "blk"), None, None),
        P(("pages", "blk"), None, None),
        P(),
        P(),
        P("pages"),
        P("pages", None),
        P("pages", None),
        P("pages", None),
    )
    out_specs = (P("pages", "blk"), P("pages", None, "blk"))
    return jax.shard_map(
        on_device, mesh=mesh, in_specs=in_specs, out_specs=out_specs, check_vma=False
    )
```

```python
import functools
import math

import jax
import jax.numpy as jnp
import numpy as np
from jax import lax
from jax.experimental import pallas as pl
from jax.experimental.pallas import tpu as pltpu
from jax.sharding import PartitionSpec as P

D = 6144
H = 64
HD = 96
ROT = 24
PAGE = 16
PPR = 12
KP = 5
NREC = 8
NF = 8
PAIR = 2 * HD
EPSILON = 1e-05
ROT_BASE = 10000.0
MESH = pl.DeviceIdType.MESH
VMEM_SPEC = pl.BlockSpec(memory_space=pltpu.VMEM)


CHUNK = 2 * PAIR


def rotary_rows(lanes, starts):
    out = np.zeros((8, lanes), np.float32)
    half = ROT // 2
    freq = (np.float32(ROT_BASE) ** (np.float32(-2.0) * np.arange(half, dtype=np.float32) / np.float32(ROT))).astype(np.float32)
    for start in starts:
        out[0, start : start + half] = freq
        out[0, start + half : start + ROT] = freq
        out[1, start + half : start + ROT] = 1.0
        out[2, start : start + half] = 1.0
    return out


def rotated(values, position, rows):
    lanes = values.shape[1]
    angle = position * rows[0:1]
    sine = jnp.sin(angle)
    return (
        values * jnp.cos(angle)
        + pltpu.roll(values, ROT // 2, 1) * (sine * rows[1:2])
        - pltpu.roll(values, lanes - ROT // 2, 1) * (sine * rows[2:3])
    )


def normed(values):
    centered = values - jnp.mean(values, axis=-1, keepdims=True)
    spread = jnp.mean(centered * centered, axis=-1, keepdims=True)
    return centered * lax.rsqrt(spread + EPSILON)


def times(left, right):
    return lax.dot_general(left, right, (((1,), (1,)), ((), ())), preferred_element_type=jnp.float32)


def over_rows(left, right):
    return lax.dot_general(left, right, (((0,), (0,)), ((), ())), preferred_element_type=jnp.float32)


def high(values):
    return values.astype(jnp.bfloat16).astype(jnp.float32)


def step_kernel(
    scale,
    x_ref, held_ref, again_ref, mgain_ref, fw_ref, table_ref, length_row, keep_rows, fold_rows, rec_rows, spread_ref, tile_ref,
    turn_ref, fturn_ref,
    qkv_hbm, dense_hbm, in_hbm, out_hbm, page_hbm,
    sum_ref, fold_ref,
    exp_ref, gt, route_ref, place_ref, fslot, fsel, w_ref, own8, wq, wkv, wk, dense, inw, outw, page, xb, xg, nattn, mall, hbuf, wall, wexp, qb, ks,
    qsend, qin, fsend, fin, rsend, rin, mp, mrecv, ysend, yrecv, apart, asend, arecv, tsend, trecv, oall,
    load, xs, xr, x2s, x2r, x3s, x3r, as1, ar1, bs1, br1, as2, ar2, bs2, br2, cs, cr, ds, dr, ws, wr,
    qs, qr, fs, fr, rs, rr, ms, mr, ys, yr, ats, atr, ts, tr, os, orr, xps, xpr,
):
    f32, bf16 = jnp.float32, jnp.bfloat16
    y = lax.axis_index("pages")
    b = lax.axis_index("blk")
    me = y * 32 + b
    z = lax.div(b, 8)
    x = lax.rem(lax.div(b, 2), 4)
    c = lax.rem(b, 2)
    chip = lax.div(b, 2)

    loads = [
        pltpu.make_async_copy(page_hbm, page, load.at[0]),
        pltpu.make_async_copy(qkv_hbm.at[pl.ds(0, PAIR)], wq.at[pl.ds(0, PAIR)], load.at[1]),
        pltpu.make_async_copy(qkv_hbm.at[pl.ds(288, PAIR)], wq.at[pl.ds(PAIR, PAIR)], load.at[5]),
        pltpu.make_async_copy(qkv_hbm.at[pl.ds(HD, PAIR)], wkv.at[pl.ds(0, PAIR)], load.at[6]),
        pltpu.make_async_copy(qkv_hbm.at[pl.ds(288 + HD, PAIR)], wkv.at[pl.ds(PAIR, PAIR)], load.at[7]),
        pltpu.make_async_copy(qkv_hbm.at[pl.ds(HD, HD)], wk.at[pl.ds(0, HD)], load.at[8]),
        pltpu.make_async_copy(qkv_hbm.at[pl.ds(288 + HD, HD)], wk.at[pl.ds(HD, HD)], load.at[9]),
        pltpu.make_async_copy(in_hbm, inw, load.at[2]),
        pltpu.make_async_copy(out_hbm, outw, load.at[3]),
        pltpu.make_async_copy(dense_hbm, dense, load.at[4]),
    ]
    for cp in loads:
        cp.start()

    barrier = pltpu.get_barrier_semaphore()

    def hello(step, carry):
        other = lax.rem(me + 1 + step, 128)
        pl.semaphore_signal(barrier, inc=1, device_id={"pages": lax.div(other, 32), "blk": lax.rem(other, 32)}, device_id_type=MESH)
        return carry

    lax.fori_loop(0, 127, hello, 0)
    hbuf[c, z, x] = (normed(held_ref[...].astype(f32)) * again_ref[...]).astype(bf16)
    xb[c, chip] = x_ref[...]
    pl.semaphore_wait(barrier, 127)

    def remote(src, dst, s, r, pages_id, blk_id):
        return pltpu.make_async_remote_copy(
            src_ref=src, dst_ref=dst, send_sem=s, recv_sem=r, device_id={"pages": pages_id, "blk": blk_id}, device_id_type=MESH
        )

    def y_at(step):
        return lax.rem(y + 1 + step, 4)

    def x_blk(step):
        return z * 8 + lax.rem(x + 1 + step, 4) * 2 + c

    def z_blk(step):
        return lax.rem(z + 1 + step, 4) * 8 + x * 2 + c

    partner = b + 1 - 2 * c
    half = held_ref.shape[1] // 2
    la = pl.ds(0, half)
    lb = pl.ds(half, half)
    waits = []

    a1 = [remote(hbuf.at[c, z, x, :, la], hbuf.at[c, z, x, :, la], as1.at[s], ar1.at[s], y, x_blk(s)) for s in range(3)]
    b1 = [remote(hbuf.at[c, z, x, :, lb], hbuf.at[c, z, x, :, lb], bs1.at[s], br1.at[s], y, z_blk(s)) for s in range(3)]
    for s in range(3):
        a1[s].start()
        b1[s].start()

    def send_x(step, carry):
        remote(x_ref, xb.at[c, chip], xs, xr, y, lax.rem(chip + 1 + step, 16) * 2 + c).start()
        return carry

    lax.fori_loop(0, 15, send_x, 0)
    def scatter(src, dst, s, r, step):
        def one(n, carry):
            chunk = lax.rem(b + 1 + step * 4 + lax.div(n, 4), 32)
            g = lax.rem(y + 1 + lax.rem(n, 4), 4)
            remote(src.at[g * 32 + chunk], dst.at[me], s, r, g, chunk).start()
            return carry

        lax.fori_loop(0, 16 - lax.div(step, 7), one, 0)

    def chunk_at(step, u):
        chunk = lax.rem(b + 1 + step * 4 + u, 32)
        return chunk, page[:, pl.ds(pl.multiple_of(chunk * CHUNK, 128), CHUNK)]

    gt[...] = jnp.zeros_like(gt)
    gt[0:NREC, 0:32] = rec_rows[...].astype(f32)
    gt[8 : 8 + KP, 0:32] = keep_rows[...].astype(f32)
    gt[13:14, 0:32] = length_row[...].astype(f32)
    gt[16 : 16 + PPR, 0:32] = fold_rows[...].astype(f32)
    every = table_ref[...].astype(f32)
    mine = jnp.zeros((PPR, 32), f32)
    for g in range(4):
        mine = mine + jnp.where(y == g, every[:, g * 32 : (g + 1) * 32], 0.0)
    gt[32 : 32 + PPR, 0:32] = mine
    by_request = jnp.transpose(gt[...])[0:32]
    length_col = by_request[:, 13:14]
    lane512 = lax.broadcasted_iota(jnp.int32, (32, 512), 1)
    lane128 = lax.broadcasted_iota(jnp.int32, (32, 128), 1)
    token16 = lax.broadcasted_iota(jnp.int32, (32, PAGE), 1)
    target = (lax.shift_right_logical(token16, 2) * 32 + b) * 4 + jnp.bitwise_and(token16, 3)
    numbers = by_request
    any_slot = jnp.zeros((32, 512), f32)
    kept, dropped = [], []
    for j in range(PPR):
        column = by_request[:, 32 + j : 33 + j]
        below = jnp.zeros((32, 32), f32)
        for other in range(PPR):
            below = below + jnp.where(gt[32 + other : 33 + other, 0:32] < column, 1.0, 0.0)
        rank = jnp.sum(below, axis=1, keepdims=True).astype(jnp.int32)
        holder = lax.shift_right_logical(rank * 43691, 17)
        nth = rank - 3 * holder
        place = holder * 4 + nth
        hit = jnp.where(place == lane512, 1.0, 0.0)
        any_slot = any_slot + hit
        route_ref[j * 32 : (j + 1) * 32, :] = hit.astype(bf16)
        numbers = jnp.where(lane128 == 48 + j, holder.astype(f32), jnp.where(lane128 == 64 + j, nth.astype(f32), numbers))
        is_kept = by_request[:, 8:9] == j
        for m in range(1, KP):
            is_kept = jnp.logical_or(is_kept, by_request[:, 8 + m : 9 + m] == j)
        kept.append(jnp.where(is_kept, 1.0, 0.0))
        dropped.append(jnp.where(jnp.logical_and(jnp.logical_not(is_kept), length_col > j * PAGE), 1.0, 0.0))
        row = jnp.zeros((32, PAGE), f32)
        for f in range(NF):
            row = row + jnp.where(by_request[:, 16 + j : 17 + j] == f, fw_ref[f : f + 1, :], 0.0)
        live = jnp.logical_and(dropped[j] > 0.5, (token16 + j * PAGE).astype(f32) < length_col)
        fslot[j * 32 : (j + 1) * 32, :] = jnp.where(live, row, 0.0)
        fsel[j * 32 : (j + 1) * 32, :] = jnp.where(place == target, 1.0, 0.0).astype(bf16)
    for cp in a1:
        cp.wait_recv()
    a2 = [remote(hbuf.at[c, z, :, :, la], hbuf.at[c, z, :, :, la], as2.at[s], ar2.at[s], y, z_blk(s)) for s in range(3)]
    for cp in a2:
        cp.start()
    for cp in b1:
        cp.wait_recv()
    b2 = [remote(hbuf.at[c, :, x, :, lb], hbuf.at[c, :, x, :, lb], bs2.at[s], br2.at[s], y, x_blk(s)) for s in range(3)]
    for cp in b2:
        cp.start()
    swaps = [
        remote(hbuf.at[c, z, :, :, la], hbuf.at[c, z, :, :, la], cs.at[3], cr.at[3], y, partner),
        remote(hbuf.at[c, :, x, :, lb], hbuf.at[c, :, x, :, lb], ds.at[3], dr.at[3], y, partner),
    ]
    for cp in swaps:
        cp.start()

    fifteen = pl.ds(0, 15)
    pltpu.make_async_copy(xb.at[0, fifteen], xb.at[0, fifteen], xr).wait()
    x_swap = remote(xb.at[c], xb.at[c], xps, xpr, y, partner)
    x_swap.start()

    place_ref[0:32, :] = any_slot.astype(bf16)
    wanted = fslot[...]
    wanted1 = high(wanted)
    wanted2 = high(wanted - wanted1)
    picked = jnp.zeros((16, PAGE), f32)
    for w in (wanted1, wanted2, wanted - wanted1 - wanted2):
        picked = picked + over_rows(fsel[...], w.astype(bf16))
    w_ref[...] = jnp.zeros_like(w_ref)
    for g in range(4):
        w_ref[g, 0:4, 0:PAGE] = picked[g * 4 : (g + 1) * 4]
    wall[y] = w_ref[y]
    w_sends = [remote(w_ref.at[y_at(s)], wall.at[y], ws.at[s], wr.at[s], y_at(s), b) for s in range(3)]
    for cp in w_sends:
        cp.start()

    row256 = lax.broadcasted_iota(jnp.int32, (256, 1), 0)
    request = jnp.bitwise_and(lax.shift_right_logical(row256, 3), 15) * 2 + lax.shift_right_logical(row256, 7)
    repeat = jnp.where(lax.broadcasted_iota(jnp.int32, (256, 32), 1) == request, 1.0, 0.0).astype(bf16)
    listed = jnp.dot(repeat, numbers.astype(bf16), preferred_element_type=f32)
    at256 = lax.broadcasted_iota(jnp.int32, (256, 128), 1)

    def entry(at):
        return jnp.sum(jnp.where(at256 == at, listed, 0.0), axis=1, keepdims=True).astype(jnp.int32)

    rec = entry(jnp.bitwise_and(row256, 7))
    rec_slot = entry(8 + lax.shift_right_logical(rec, 4))
    rec_token = jnp.bitwise_and(rec, 15)
    rec_place = entry(48 + rec_slot) * 4 + entry(64 + rec_slot)
    rec_pos = (rec_slot * PAGE + rec_token).astype(f32)
    place_ref[32:288, :] = jnp.where(lax.broadcasted_iota(jnp.int32, (256, 512), 1) == rec_place, 1.0, 0.0).astype(bf16)
    owner_lane = lax.shift_right_logical(lax.broadcasted_iota(jnp.int32, (PPR, 128), 1), 5).astype(f32)
    token_page = lax.shift_right_logical(lax.broadcasted_iota(jnp.int32, (16, 192), 1), 4)
    place_row = lax.broadcasted_iota(jnp.int32, (16, 192), 0).astype(f32)
    groups = []
    owned = jnp.zeros((16, 192), f32)
    for p in range(12):
        found = jnp.where(table_ref[...] == me * 12 + p, owner_lane, 0.0)
        group = jnp.sum(jnp.sum(found, axis=1, keepdims=True), axis=0, keepdims=True)
        nth = jnp.zeros((1, 1), f32)
        for g in groups:
            nth = nth + jnp.where(g == group, 1.0, 0.0)
        groups.append(group)
        owned = owned + jnp.where(jnp.logical_and(token_page == p, place_row == group * 4.0 + nth), 1.0, 0.0)
    for i in range(8):
        own8[i * 16 : (i + 1) * 16, :] = owned

    x_swap.wait_recv()
    for m in range(16):
        both = jnp.concatenate([xb[0, m].astype(f32), xb[1, m].astype(f32)], axis=1)
        xg[:, m * CHUNK : (m + 1) * CHUNK] = both
    unit = normed(xg[...])
    nattn[...] = (unit * again_ref[...]).astype(bf16)
    mall[y] = (unit * mgain_ref[...]).astype(bf16)
    lc = pl.ds(pl.multiple_of(c * half, 128), half)
    x2 = [remote(mall.at[y, :, lc], mall.at[y, :, lc], x2s.at[s], x2r.at[s], y_at(s), b) for s in range(3)]
    for cp in x2:
        cp.start()

    for cp in loads[1:5]:
        cp.wait()
    lane = lax.broadcasted_iota(jnp.int32, (32, CHUNK), 1)
    zero = jnp.zeros((32, CHUNK), f32)
    k_0, k_1 = lane < HD, jnp.logical_and(lane >= PAIR, lane < PAIR + HD)
    is_key = jnp.logical_or(k_0, k_1)
    normal = nattn[...]
    query = jnp.where(is_key, high(rotated(times(normal, wq[...]), length_col, turn_ref[...])), zero)
    pairs = high(rotated(times(normal, wkv[...]), length_col, turn_ref[...]))
    new_key = jnp.where(is_key, pairs, zero)
    new_value = jnp.where(is_key, zero, pairs)
    q_fresh = jnp.where(lane < HD, query, pltpu.roll(query, CHUNK - HD, 1))[:, 0:PAIR].astype(bf16)
    qb[0:32, :] = query.astype(bf16)
    own_prod = query * new_key
    own_score = [jnp.sum(jnp.where(keep, own_prod, zero), axis=1, keepdims=True) * scale for keep in (k_0, k_1)]

    for s in range(3):
        a2[s].wait_recv()
        back = lax.rem(z + 3 - s, 4)
        swaps.append(remote(hbuf.at[c, back, :, :, la], hbuf.at[c, back, :, :, la], cs.at[s], cr.at[s], y, partner))
        swaps[-1].start()
        b2[s].wait_recv()
        back = lax.rem(x + 3 - s, 4)
        swaps.append(remote(hbuf.at[c, :, back, :, lb], hbuf.at[c, :, back, :, lb], ds.at[s], dr.at[s], y, partner))
        swaps[-1].start()

    loads[5].wait()
    loads[6].wait()

    def keys_of(core):
        ks[pl.ds(pl.multiple_of(core * 128, 128), 128), 0:PAIR] = times(hbuf[core].reshape(128, D), wk[...])

    ks[:, PAIR:] = jnp.zeros((256, 256 - PAIR), f32)
    keys_of(c)
    for cp in swaps:
        cp.wait_recv()
    keys_of(1 - c)
    fresh = high(rotated(ks[...], rec_pos, fturn_ref[...]))[:, 0:PAIR]
    prod = fresh * jnp.dot(repeat, q_fresh, preferred_element_type=f32)
    flane = lax.broadcasted_iota(jnp.int32, (256, PAIR), 1)
    score0 = jnp.sum(jnp.where(flane < HD, prod, 0.0), axis=1, keepdims=True) * scale
    score1 = jnp.sum(jnp.where(flane < HD, 0.0, prod), axis=1, keepdims=True) * scale
    wlane = lax.broadcasted_iota(jnp.int32, (256, CHUNK), 1)
    first = wlane < PAIR
    rel = jnp.where(first, wlane, wlane - PAIR) - HD
    score = jnp.where(first, score0, score1)
    shigh = high(score)
    kind = jnp.where(rel < PAGE, shigh, jnp.where(rel < 2 * PAGE, score - shigh, 1.0))
    token = jnp.where(rel < PAGE, rel, jnp.where(rel < 2 * PAGE, rel - PAGE, rel - 2 * PAGE))
    hit = jnp.logical_and(jnp.logical_and(rel >= 0, rel < 3 * PAGE), token == rec_token)
    qb[32:288, :] = jnp.where(hit, kind, 0.0).astype(bf16)
    message = over_rows(place_ref[...], qb[...])
    qsend[...] = message.reshape(128, 4, CHUNK).astype(bf16)

    def send_q(step, carry):
        other = lax.rem(me + 1 + step, 128)
        g, h = lax.div(other, 32), lax.rem(other, 32)
        remote(qsend.at[other], qin.at[me], qs, qr, g, h).start()
        return carry

    lax.fori_loop(0, 127, send_q, 0)
    qin[me] = qsend[me]

    x3 = []
    for s in range(3):
        x2[s].wait_recv()
        back = lax.rem(y + 3 - s, 4)
        x3.append(remote(mall.at[back, :, lc], mall.at[back, :, lc], x3s.at[s], x3r.at[s], y, partner))
        x3[-1].start()

    for cp in w_sends:
        cp.wait_recv()
    loads[0].wait()
    own = own8[0:16, :] > 0.5
    weights = wall[:, 0:4, :].reshape(16, 128)
    w1 = high(weights)
    w2 = high(weights - w1)
    w3 = weights - w1 - w2
    for i, w in enumerate((w1, w2, w3)):
        wide = jnp.dot(w.astype(bf16), tile_ref[...], preferred_element_type=f32)
        wexp[i * 16 : (i + 1) * 16, :] = jnp.where(own, wide, 0.0).astype(bf16)

    def fold_step(step, carry):
        for u in range(4):
            chunk, part = chunk_at(step, u)
            out = jnp.dot(wexp[...], part, preferred_element_type=f32)
            out = out[0:16] + out[16:32] + out[32:48]
            for g in range(4):
                fsend[g * 32 + chunk] = out[g * 4 : (g + 1) * 4].astype(bf16)
        scatter(fsend, fin, fs, fr, step)
        return carry

    lax.fori_loop(0, 8, fold_step, 0)
    fin[me] = fsend[me]

    loads[7].wait()
    loads[8].wait()
    for cp in x3:
        cp.wait_recv()
    hidden = times(mall[...].reshape(128, D), inw[...])
    active = (0.5 * hidden * (1.0 + lax.erf(hidden * np.float32(math.sqrt(0.5))))).astype(bf16)

    def mlp_step(step, carry):
        lanes = pl.ds(pl.multiple_of(step * 768, 128), 768)
        out = jnp.dot(active, outw[:, lanes], preferred_element_type=f32).astype(bf16).reshape(4, 2, 16, 768)
        mp[0, :, :, lanes] = out[:, 0]
        mp[1, :, :, lanes] = out[:, 1]
        return carry

    lax.fori_loop(0, 8, mlp_step, 0)
    m_swap = remote(mp.at[1 - c], mrecv, ms, mr, y, partner)
    m_swap.start()

    rest = pl.ds(0, 31)
    others = pl.ds(0, 127)
    pltpu.make_async_copy(qin.at[others], qin.at[others], qr).wait()
    lane16 = lax.broadcasted_iota(jnp.int32, (16, CHUNK), 1)
    lane_tile = lax.broadcasted_iota(jnp.int32, (16, 128), 1)
    key0 = lane16 < HD
    key1 = jnp.logical_and(lane16 >= PAIR, lane16 < PAIR + HD)

    def page_step(step, carry):
        chunks, parts, wides = [], [], []
        for u in range(4):
            chunk, part = chunk_at(step, u)
            chunks.append(chunk)
            parts.append(part)
            wides.append(jnp.concatenate([qin[g * 32 + chunk].astype(f32) for g in range(4)], axis=0))
        scores, again, flags = [], [], []
        for u in range(4):
            q2 = jnp.concatenate([jnp.where(key0, wides[u], 0.0), jnp.where(key1, wides[u], 0.0)], axis=0).astype(bf16)
            scores.append(times(q2, parts[u]))
            ex = [jnp.concatenate([exp_ref[g * 32 + chunks[u], :, n * 256 : n * 256 + 192] for g in range(4)], axis=0) for n in range(3)]
            again += [ex[0], ex[1]]
            flags += [ex[2], ex[2]]
        mask = own8[...] > 0.5
        s = jnp.where(jnp.concatenate(flags, axis=0) > 0.5, jnp.concatenate(again, axis=0), jnp.concatenate(scores, axis=0) * scale)
        s = jnp.where(mask, s, -1e30)
        top = jnp.max(s, axis=1, keepdims=True)
        thigh = high(top)
        tlow = high(top - thigh)
        p = jnp.where(mask, jnp.exp(s - (thigh + tlow)), 0.0)
        total = jnp.sum(p, axis=1, keepdims=True)
        ohigh = high(total)
        olow = total - ohigh
        p = p.astype(bf16)
        for u in range(4):
            mixed = jnp.dot(p[u * 32 : (u + 1) * 32], parts[u], preferred_element_type=f32)
            res = jnp.where(lane16 < PAIR, mixed[0:16], mixed[16:32])
            tiles = [res[:, 0:128], res[:, 128:256]]
            for i in range(2):
                rows = slice(u * 32 + i * 16, u * 32 + (i + 1) * 16)
                for n, col in enumerate((thigh, tlow, ohigh, olow)):
                    tiles[i] = jnp.where(lane_tile == i * (PAIR - 128) + n, col[rows], tiles[i])
            res = jnp.concatenate(tiles + [res[:, 256:CHUNK]], axis=1)
            for g in range(4):
                rsend[g * 32 + chunks[u]] = res[g * 4 : (g + 1) * 4].astype(bf16)
        scatter(rsend, rin, rs, rr, step)
        return carry

    exp_ref[...] = jnp.dot(qin[...].reshape(512, CHUNK), spread_ref[...], preferred_element_type=f32).reshape(128, 4, 768)
    lax.fori_loop(0, 4, page_step, 0)

    m_swap.wait_recv()
    ysend[...] = (mp[c].astype(f32) + mrecv[...].astype(f32)).astype(bf16)
    y_out = [remote(ysend.at[y_at(s)], yrecv.at[y], ys.at[s], yr.at[s], y_at(s), b) for s in range(3)]
    for cp in y_out:
        cp.start()
    yrecv[y] = ysend[y]

    lax.fori_loop(4, 8, page_step, 0)
    rin[me] = rsend[me]

    pltpu.make_async_copy(fin.at[others], fin.at[others], fr).wait()
    folded = jnp.dot(route_ref[...], fin[...].reshape(512, CHUNK), preferred_element_type=f32)
    for j in range(PPR):
        fold_ref[j] = folded[j * 32 : (j + 1) * 32].astype(bf16)
    f_score = []
    for j in range(PPR):
        fprod = folded[j * 32 : (j + 1) * 32] * query
        ok = dropped[j] > 0.5
        f_score.append([
            jnp.where(ok, jnp.sum(jnp.where(k_0, fprod, zero), axis=1, keepdims=True) * scale, -1e30),
            jnp.where(ok, jnp.sum(jnp.where(k_1, fprod, zero), axis=1, keepdims=True) * scale, -1e30),
        ])
    pltpu.make_async_copy(rin.at[others], rin.at[others], rr).wait()
    parts = jnp.dot(route_ref[...], rin[...].reshape(512, CHUNK), preferred_element_type=f32)
    tops = []
    for i in range(2):
        top = own_score[i]
        p_top = []
        for j in range(PPR):
            rows = parts[j * 32 : (j + 1) * 32]
            ok = kept[j] > 0.5
            p_top.append(jnp.where(ok, rows[:, i * PAIR : i * PAIR + 1] + rows[:, i * PAIR + 1 : i * PAIR + 2], -1e30))
            top = jnp.maximum(top, jnp.maximum(p_top[j], f_score[j][i]))
        tops.append((top, p_top))
    is_first = lane < PAIR
    mixed = zero
    total = zero
    for j in range(PPR):
        rows = parts[j * 32 : (j + 1) * 32]
        ok = kept[j] > 0.5
        w = [jnp.where(ok, jnp.exp(tops[i][1][j] - tops[i][0]), 0.0) for i in range(2)]
        e = [jnp.exp(f_score[j][i] - tops[i][0]) for i in range(2)]
        sums = [
            w[i] * (rows[:, i * PAIR + 2 : i * PAIR + 3] + rows[:, i * PAIR + 3 : i * PAIR + 4]) + e[i] for i in range(2)
        ]
        mixed = mixed + jnp.where(is_first, w[0], w[1]) * rows + jnp.where(is_first, e[0], e[1]) * folded[j * 32 : (j + 1) * 32]
        total = total + jnp.where(is_first, sums[0], sums[1])
    o = [jnp.exp(own_score[i] - tops[i][0]) for i in range(2)]
    own_exp = jnp.where(is_first, o[0], o[1])
    mixed = (mixed + own_exp * new_value) / (total + own_exp)
    attended = jnp.where(lane < HD, pltpu.roll(mixed, CHUNK - HD, 1), pltpu.roll(mixed, CHUNK - PAIR, 1))[:, 0:PAIR].astype(bf16)
    loads[9].wait()

    def dense_step(step, carry):
        lanes = pl.ds(pl.multiple_of(step * 1536, 128), 1536)
        out = jnp.dot(attended, dense[:, lanes], preferred_element_type=f32)
        apart[0, :, lanes] = out[0:16]
        apart[1, :, lanes] = out[16:32]
        return carry

    lax.fori_loop(0, 4, dense_step, 0)
    asend[...] = apart[1 - c].astype(bf16)
    a_swap = remote(asend, arecv, ats, atr, y, partner)
    a_swap.start()
    for cp in y_out:
        cp.wait_recv()
    summed = apart[c] + yrecv[0].astype(f32) + yrecv[1].astype(f32) + yrecv[2].astype(f32) + yrecv[3].astype(f32)
    a_swap.wait_recv()
    tsend[...] = (summed + arecv[...].astype(f32)).astype(bf16)

    def send_t(step, carry):
        other = lax.rem(chip + 1 + step, 16)
        remote(
            tsend.at[:, pl.ds(pl.multiple_of(other * CHUNK, 128), CHUNK)], trecv.at[chip], ts, tr, y, other * 2 + c
        ).start()
        return carry

    lax.fori_loop(0, 15, send_t, 0)
    trecv[chip] = tsend[:, pl.ds(pl.multiple_of(chip * CHUNK, 128), CHUNK)]
    pltpu.make_async_copy(trecv.at[fifteen], trecv.at[fifteen], tr).wait()
    oall[c] = jnp.sum(trecv[...].astype(f32), axis=0).astype(bf16)
    o_swap = remote(oall.at[c], oall.at[c], os, orr, y, partner)
    o_swap.start()
    o_swap.wait_recv()
    result = oall[...].astype(f32).reshape(32, CHUNK)
    sum_ref[...] = jnp.where(c == 0, result, pltpu.roll(result, PAIR, 1))[:, 0:PAIR].astype(bf16)

    for cp in a1 + b1 + a2 + b2 + swaps + w_sends + x2 + x3 + y_out + [x_swap, m_swap, a_swap, o_swap]:
        cp.wait_send()
    pltpu.make_async_copy(xb.at[0, fifteen], xb.at[0, fifteen], xs).wait()
    for ref, sem in ((qsend, qs), (fsend, fs), (rsend, rs)):
        pltpu.make_async_copy(ref.at[others], ref.at[others], sem).wait()
    pltpu.make_async_copy(trecv.at[fifteen], trecv.at[fifteen], ts).wait()


def step_call(scale, blocks, arrays):
    f32, bf16 = jnp.float32, jnp.bfloat16
    one = pltpu.SemaphoreType.DMA
    sems = lambda n: pltpu.SemaphoreType.DMA((n,))
    rows4 = pltpu.VMEM((128, 4, CHUNK), bf16)
    scratch = [
        pltpu.VMEM((128, 4, 768), f32), pltpu.VMEM((128, 128), f32), pltpu.VMEM((384, 512), bf16), pltpu.VMEM((288, 512), bf16), pltpu.VMEM((384, PAGE), f32),
        pltpu.VMEM((384, PAGE), bf16), pltpu.VMEM((4, 8, 128), f32), pltpu.VMEM((128, 192), f32),
        pltpu.VMEM((CHUNK, D), bf16), pltpu.VMEM((CHUNK, D), bf16), pltpu.VMEM((PAIR, D), bf16),
        pltpu.VMEM((PAIR, D), bf16), pltpu.VMEM((PAIR, D), bf16), pltpu.VMEM((PAIR, D), bf16),
        pltpu.VMEM((192, 2 * D), bf16), pltpu.VMEM((2, 16, 32, PAIR), bf16), pltpu.VMEM((32, D), f32), pltpu.VMEM((32, D), bf16),
        pltpu.VMEM((4, 32, D), bf16), pltpu.VMEM((2, 4, 4, NREC, D), bf16), pltpu.VMEM((4, 8, 128), f32),
        pltpu.VMEM((48, 192), bf16), pltpu.VMEM((288, CHUNK), bf16), pltpu.VMEM((256, 256), f32),
        rows4, rows4, rows4, rows4, rows4, rows4,
        pltpu.VMEM((2, 4, 16, D), bf16), pltpu.VMEM((4, 16, D), bf16), pltpu.VMEM((4, 16, D), bf16), pltpu.VMEM((4, 16, D), bf16),
        pltpu.VMEM((2, 16, D), f32), pltpu.VMEM((16, D), bf16), pltpu.VMEM((16, D), bf16), pltpu.VMEM((16, D), bf16),
        pltpu.VMEM((16, 16, CHUNK), bf16), pltpu.VMEM((2, 16, CHUNK), bf16),
        sems(10), one, one, sems(3), sems(3), sems(3), sems(3),
        sems(3), sems(3), sems(3), sems(3), sems(3), sems(3), sems(3), sems(3), sems(4), sems(4), sems(4), sems(4), sems(3), sems(3),
        one, one, one, one, one, one, one, one, sems(3), sems(3), one, one, one, one, one, one, one, one,
    ]
    return pl.pallas_call(
        functools.partial(step_kernel, scale),
        out_shape=[jax.ShapeDtypeStruct((32, PAIR), bf16), jax.ShapeDtypeStruct((PPR, 32, CHUNK), bf16)],
        in_specs=[VMEM_SPEC] * len(blocks) + [pl.BlockSpec(memory_space=pl.ANY)] * len(arrays),
        out_specs=[VMEM_SPEC] * 2,
        scratch_shapes=scratch,
        compiler_params=pltpu.CompilerParams(collective_id=0, has_side_effects=True, vmem_limit_bytes=58 << 20),
        name="decode_step",
    )(*blocks, *arrays)


def on_device(
    new_hidden,
    attn_gain,
    mlp_gain,
    qkv_weight,
    dense_weight,
    in_weight,
    out_weight,
    page_store,
    held_states,
    fold_weights,
    page_table,
    lengths,
    keep_slots,
    fold_index,
    recompute_list,
):
    rows = lengths.shape[0]
    pages_dev = page_store.shape[0]
    scale = 1.0 / math.sqrt(HD)
    bf16 = jnp.bfloat16
    lane = np.arange(CHUNK)[:, None]
    tokens = np.arange(pages_dev * PAGE)[None, :] % PAGE
    spread = np.zeros((CHUNK, 3, 256), np.float32)
    for i in range(2):
        t = lane - (i * PAIR + HD)
        spread[:, i, : pages_dev * PAGE] = (t == tokens) | (t == tokens + PAGE)
    spread[:, 2, : pages_dev * PAGE] = lane - HD == tokens + 2 * PAGE
    spread = jnp.asarray(spread.reshape(CHUNK, 768), bf16)
    tile = jnp.asarray((np.arange(128)[:, None] == tokens).astype(np.float32), bf16)
    turn = jnp.asarray(rotary_rows(CHUNK, (0, PAIR)))
    fresh_turn = jnp.asarray(rotary_rows(256, (0, HD)))

    blocks = (
        new_hidden, held_states.reshape(NREC, D), attn_gain.reshape(1, D), mlp_gain.reshape(1, D), fold_weights, page_table.T,
        lengths.reshape(1, rows), keep_slots.T, fold_index.T, recompute_list.T, spread, tile, turn, fresh_turn,
    )
    arrays = (qkv_weight.T, dense_weight, in_weight.T, out_weight, page_store.reshape(pages_dev * PAGE, 2 * D))
    update, folded = step_call(scale, blocks, arrays)
    return (update, folded.transpose(1, 0, 2))


def solution(mesh):
    in_specs = (
        P("pages", "blk"),
        P(),
        P(),
        P(None, "blk"),
        P("blk", None),
        P(None, ("pages", "blk")),
        P(("pages", "blk"), None),
        P(("pages", "blk"), None, None),
        P(("pages", "blk"), None, None),
        P(),
        P(),
        P("pages"),
        P("pages", None),
        P("pages", None),
        P("pages", None),
    )
    out_specs = (P("pages", "blk"), P("pages", None, "blk"))
    return jax.shard_map(
        on_device, mesh=mesh, in_specs=in_specs, out_specs=out_specs, check_vma=False
    )
```

```python
import functools
import math

import jax
import jax.numpy as jnp
import numpy as np
from jax import lax
from jax.experimental import pallas as pl
from jax.experimental.pallas import tpu as pltpu
from jax.sharding import PartitionSpec as P

D = 6144
H = 64
HD = 96
ROT = 24
PAGE = 16
PPR = 12
KP = 5
NREC = 8
NF = 8
PAIR = 2 * HD
EPSILON = 1e-05
ROT_BASE = 10000.0
MESH = pl.DeviceIdType.MESH
VMEM_SPEC = pl.BlockSpec(memory_space=pltpu.VMEM)


CHUNK = 2 * PAIR


def rotary_rows(lanes, starts):
    out = np.zeros((8, lanes), np.float32)
    half = ROT // 2
    freq = (np.float32(ROT_BASE) ** (np.float32(-2.0) * np.arange(half, dtype=np.float32) / np.float32(ROT))).astype(np.float32)
    for start in starts:
        out[0, start : start + half] = freq
        out[0, start + half : start + ROT] = freq
        out[1, start + half : start + ROT] = 1.0
        out[2, start : start + half] = 1.0
    return out


def rotated(values, position, rows):
    lanes = values.shape[1]
    angle = position * rows[0:1]
    sine = jnp.sin(angle)
    return (
        values * jnp.cos(angle)
        + pltpu.roll(values, ROT // 2, 1) * (sine * rows[1:2])
        - pltpu.roll(values, lanes - ROT // 2, 1) * (sine * rows[2:3])
    )


def normed(values):
    centered = values - jnp.mean(values, axis=-1, keepdims=True)
    spread = jnp.mean(centered * centered, axis=-1, keepdims=True)
    return centered * lax.rsqrt(spread + EPSILON)


def times(left, right):
    return lax.dot_general(left, right, (((1,), (1,)), ((), ())), preferred_element_type=jnp.float32)


def over_rows(left, right):
    return lax.dot_general(left, right, (((0,), (0,)), ((), ())), preferred_element_type=jnp.float32)


def high(values):
    return values.astype(jnp.bfloat16).astype(jnp.float32)


def step_kernel(
    scale,
    x_ref, held_ref, again_ref, mgain_ref, fw_ref, table_ref, length_row, keep_rows, fold_rows, rec_rows, spread_ref, tile_ref,
    turn_ref, fturn_ref,
    qkv_hbm, dense_hbm, in_hbm, out_hbm, page_hbm,
    sum_ref, fold_ref,
    exp_ref, gt, route_ref, place_ref, fslot, fsel, w_ref, own8, wq, wkv, wk, dense, inw, outw, page, xb, xg, nattn, mall, hbuf, wall, wexp, qb, ks,
    qsend, qin, fsend, fin, rsend, rin, mp, mrecv, ysend, yrecv, apart, asend, arecv, tsend, trecv, oall,
    load, xs, xr, x2s, x2r, x3s, x3r, as1, ar1, bs1, br1, as2, ar2, bs2, br2, cs, cr, ds, dr, ws, wr,
    qs, qr, fs, fr, rs, rr, ms, mr, ys, yr, ats, atr, ts, tr, os, orr, xps, xpr,
):
    f32, bf16 = jnp.float32, jnp.bfloat16
    y = lax.axis_index("pages")
    b = lax.axis_index("blk")
    me = y * 32 + b
    z = lax.div(b, 8)
    x = lax.rem(lax.div(b, 2), 4)
    c = lax.rem(b, 2)
    chip = lax.div(b, 2)

    loads = [
        pltpu.make_async_copy(page_hbm, page, load.at[0]),
        pltpu.make_async_copy(qkv_hbm.at[pl.ds(0, PAIR)], wq.at[pl.ds(0, PAIR)], load.at[1]),
        pltpu.make_async_copy(qkv_hbm.at[pl.ds(288, PAIR)], wq.at[pl.ds(PAIR, PAIR)], load.at[5]),
        pltpu.make_async_copy(qkv_hbm.at[pl.ds(HD, PAIR)], wkv.at[pl.ds(0, PAIR)], load.at[6]),
        pltpu.make_async_copy(qkv_hbm.at[pl.ds(288 + HD, PAIR)], wkv.at[pl.ds(PAIR, PAIR)], load.at[7]),
        pltpu.make_async_copy(qkv_hbm.at[pl.ds(HD, HD)], wk.at[pl.ds(0, HD)], load.at[8]),
        pltpu.make_async_copy(qkv_hbm.at[pl.ds(288 + HD, HD)], wk.at[pl.ds(HD, HD)], load.at[9]),
        pltpu.make_async_copy(in_hbm, inw, load.at[2]),
        pltpu.make_async_copy(out_hbm, outw, load.at[3]),
        pltpu.make_async_copy(dense_hbm, dense, load.at[4]),
    ]
    for cp in loads:
        cp.start()

    barrier = pltpu.get_barrier_semaphore()

    def hello(step, carry):
        other = lax.rem(me + 1 + step, 128)
        pl.semaphore_signal(barrier, inc=1, device_id={"pages": lax.div(other, 32), "blk": lax.rem(other, 32)}, device_id_type=MESH)
        return carry

    lax.fori_loop(0, 127, hello, 0)
    hbuf[c, z, x] = (normed(held_ref[...].astype(f32)) * again_ref[...]).astype(bf16)
    xb[c, chip] = x_ref[...]
    pl.semaphore_wait(barrier, 127)

    def remote(src, dst, s, r, pages_id, blk_id):
        return pltpu.make_async_remote_copy(
            src_ref=src, dst_ref=dst, send_sem=s, recv_sem=r, device_id={"pages": pages_id, "blk": blk_id}, device_id_type=MESH
        )

    def y_at(step):
        return lax.rem(y + 1 + step, 4)

    def x_blk(step):
        return z * 8 + lax.rem(x + 1 + step, 4) * 2 + c

    def z_blk(step):
        return lax.rem(z + 1 + step, 4) * 8 + x * 2 + c

    partner = b + 1 - 2 * c
    half = held_ref.shape[1] // 2
    la = pl.ds(0, half)
    lb = pl.ds(half, half)
    waits = []

    a1 = [remote(hbuf.at[c, z, x, :, la], hbuf.at[c, z, x, :, la], as1.at[s], ar1.at[s], y, x_blk(s)) for s in range(3)]
    b1 = [remote(hbuf.at[c, z, x, :, lb], hbuf.at[c, z, x, :, lb], bs1.at[s], br1.at[s], y, z_blk(s)) for s in range(3)]
    for s in range(3):
        a1[s].start()
        b1[s].start()

    def send_x(step, carry):
        remote(x_ref, xb.at[c, chip], xs, xr, y, lax.rem(chip + 1 + step, 16) * 2 + c).start()
        return carry

    lax.fori_loop(0, 15, send_x, 0)
    def scatter(src, dst, s, r, step):
        def one(n, carry):
            chunk = lax.rem(b + 1 + step * 4 + lax.div(n, 4), 32)
            g = lax.rem(y + 1 + lax.rem(n, 4), 4)
            remote(src.at[g * 32 + chunk], dst.at[me], s, r, g, chunk).start()
            return carry

        lax.fori_loop(0, 16 - lax.div(step, 7), one, 0)

    def chunk_at(step, u):
        chunk = lax.rem(b + 1 + step * 4 + u, 32)
        return chunk, page[:, pl.ds(pl.multiple_of(chunk * CHUNK, 128), CHUNK)]

    gt[...] = jnp.zeros_like(gt)
    gt[0:NREC, 0:32] = rec_rows[...].astype(f32)
    gt[8 : 8 + KP, 0:32] = keep_rows[...].astype(f32)
    gt[13:14, 0:32] = length_row[...].astype(f32)
    gt[16 : 16 + PPR, 0:32] = fold_rows[...].astype(f32)
    every = table_ref[...].astype(f32)
    mine = jnp.zeros((PPR, 32), f32)
    for g in range(4):
        mine = mine + jnp.where(y == g, every[:, g * 32 : (g + 1) * 32], 0.0)
    gt[32 : 32 + PPR, 0:32] = mine
    by_request = jnp.transpose(gt[...])[0:32]
    length_col = by_request[:, 13:14]
    lane512 = lax.broadcasted_iota(jnp.int32, (32, 512), 1)
    lane128 = lax.broadcasted_iota(jnp.int32, (32, 128), 1)
    token16 = lax.broadcasted_iota(jnp.int32, (32, PAGE), 1)
    target = (lax.shift_right_logical(token16, 2) * 32 + b) * 4 + jnp.bitwise_and(token16, 3)
    numbers = by_request
    any_slot = jnp.zeros((32, 512), f32)
    kept, dropped = [], []
    for j in range(PPR):
        column = by_request[:, 32 + j : 33 + j]
        below = jnp.zeros((32, 32), f32)
        for other in range(PPR):
            below = below + jnp.where(gt[32 + other : 33 + other, 0:32] < column, 1.0, 0.0)
        rank = jnp.sum(below, axis=1, keepdims=True).astype(jnp.int32)
        holder = lax.shift_right_logical(rank * 43691, 17)
        nth = rank - 3 * holder
        place = holder * 4 + nth
        hit = jnp.where(place == lane512, 1.0, 0.0)
        any_slot = any_slot + hit
        route_ref[j * 32 : (j + 1) * 32, :] = hit.astype(bf16)
        numbers = jnp.where(lane128 == 48 + j, holder.astype(f32), jnp.where(lane128 == 64 + j, nth.astype(f32), numbers))
        is_kept = by_request[:, 8:9] == j
        for m in range(1, KP):
            is_kept = jnp.logical_or(is_kept, by_request[:, 8 + m : 9 + m] == j)
        kept.append(jnp.where(is_kept, 1.0, 0.0))
        dropped.append(jnp.where(jnp.logical_and(jnp.logical_not(is_kept), length_col > j * PAGE), 1.0, 0.0))
        row = jnp.zeros((32, PAGE), f32)
        for f in range(NF):
            row = row + jnp.where(by_request[:, 16 + j : 17 + j] == f, fw_ref[f : f + 1, :], 0.0)
        live = jnp.logical_and(dropped[j] > 0.5, (token16 + j * PAGE).astype(f32) < length_col)
        fslot[j * 32 : (j + 1) * 32, :] = jnp.where(live, row, 0.0)
        fsel[j * 32 : (j + 1) * 32, :] = jnp.where(place == target, 1.0, 0.0).astype(bf16)
    for cp in a1:
        cp.wait_recv()
    a2 = [remote(hbuf.at[c, z, :, :, la], hbuf.at[c, z, :, :, la], as2.at[s], ar2.at[s], y, z_blk(s)) for s in range(3)]
    for cp in a2:
        cp.start()
    for cp in b1:
        cp.wait_recv()
    b2 = [remote(hbuf.at[c, :, x, :, lb], hbuf.at[c, :, x, :, lb], bs2.at[s], br2.at[s], y, x_blk(s)) for s in range(3)]
    for cp in b2:
        cp.start()
    swaps = [
        remote(hbuf.at[c, z, :, :, la], hbuf.at[c, z, :, :, la], cs.at[3], cr.at[3], y, partner),
        remote(hbuf.at[c, :, x, :, lb], hbuf.at[c, :, x, :, lb], ds.at[3], dr.at[3], y, partner),
    ]
    for cp in swaps:
        cp.start()

    fifteen = pl.ds(0, 15)
    pltpu.make_async_copy(xb.at[0, fifteen], xb.at[0, fifteen], xr).wait()
    x_swap = remote(xb.at[c], xb.at[c], xps, xpr, y, partner)
    x_swap.start()

    place_ref[0:32, :] = any_slot.astype(bf16)
    wanted = fslot[...]
    wanted1 = high(wanted)
    wanted2 = high(wanted - wanted1)
    picked = jnp.zeros((16, PAGE), f32)
    for w in (wanted1, wanted2, wanted - wanted1 - wanted2):
        picked = picked + over_rows(fsel[...], w.astype(bf16))
    w_ref[...] = jnp.zeros_like(w_ref)
    for g in range(4):
        w_ref[g, 0:4, 0:PAGE] = picked[g * 4 : (g + 1) * 4]
    wall[y] = w_ref[y]
    w_sends = [remote(w_ref.at[y_at(s)], wall.at[y], ws.at[s], wr.at[s], y_at(s), b) for s in range(3)]
    for cp in w_sends:
        cp.start()

    row256 = lax.broadcasted_iota(jnp.int32, (256, 1), 0)
    request = jnp.bitwise_and(lax.shift_right_logical(row256, 3), 15) * 2 + lax.shift_right_logical(row256, 7)
    repeat = jnp.where(lax.broadcasted_iota(jnp.int32, (256, 32), 1) == request, 1.0, 0.0).astype(bf16)
    listed = jnp.dot(repeat, numbers.astype(bf16), preferred_element_type=f32)
    at256 = lax.broadcasted_iota(jnp.int32, (256, 128), 1)

    def entry(at):
        return jnp.sum(jnp.where(at256 == at, listed, 0.0), axis=1, keepdims=True).astype(jnp.int32)

    rec = entry(jnp.bitwise_and(row256, 7))
    rec_slot = entry(8 + lax.shift_right_logical(rec, 4))
    rec_token = jnp.bitwise_and(rec, 15)
    rec_place = entry(48 + rec_slot) * 4 + entry(64 + rec_slot)
    rec_pos = (rec_slot * PAGE + rec_token).astype(f32)
    place_ref[32:288, :] = jnp.where(lax.broadcasted_iota(jnp.int32, (256, 512), 1) == rec_place, 1.0, 0.0).astype(bf16)
    owner_lane = lax.shift_right_logical(lax.broadcasted_iota(jnp.int32, (PPR, 128), 1), 5).astype(f32)
    token_page = lax.shift_right_logical(lax.broadcasted_iota(jnp.int32, (16, 192), 1), 4)
    place_row = lax.broadcasted_iota(jnp.int32, (16, 192), 0).astype(f32)
    groups = []
    owned = jnp.zeros((16, 192), f32)
    for p in range(12):
        found = jnp.where(table_ref[...] == me * 12 + p, owner_lane, 0.0)
        group = jnp.sum(jnp.sum(found, axis=1, keepdims=True), axis=0, keepdims=True)
        nth = jnp.zeros((1, 1), f32)
        for g in groups:
            nth = nth + jnp.where(g == group, 1.0, 0.0)
        groups.append(group)
        owned = owned + jnp.where(jnp.logical_and(token_page == p, place_row == group * 4.0 + nth), 1.0, 0.0)
    for i in range(8):
        own8[i * 16 : (i + 1) * 16, :] = owned

    x_swap.wait_recv()
    for m in range(16):
        both = jnp.concatenate([xb[0, m].astype(f32), xb[1, m].astype(f32)], axis=1)
        xg[:, m * CHUNK : (m + 1) * CHUNK] = both
    unit = normed(xg[...])
    nattn[...] = (unit * again_ref[...]).astype(bf16)
    mall[y] = (unit * mgain_ref[...]).astype(bf16)
    lc = pl.ds(pl.multiple_of(c * half, 128), half)
    x2 = [remote(mall.at[y, :, lc], mall.at[y, :, lc], x2s.at[s], x2r.at[s], y_at(s), b) for s in range(3)]
    for cp in x2:
        cp.start()

    for cp in loads[1:5]:
        cp.wait()
    lane = lax.broadcasted_iota(jnp.int32, (32, CHUNK), 1)
    zero = jnp.zeros((32, CHUNK), f32)
    k_0, k_1 = lane < HD, jnp.logical_and(lane >= PAIR, lane < PAIR + HD)
    is_key = jnp.logical_or(k_0, k_1)
    normal = nattn[...]
    query = jnp.where(is_key, high(rotated(times(normal, wq[...]), length_col, turn_ref[...])), zero)
    pairs = high(rotated(times(normal, wkv[...]), length_col, turn_ref[...]))
    new_key = jnp.where(is_key, pairs, zero)
    new_value = jnp.where(is_key, zero, pairs)
    q_fresh = jnp.where(lane < HD, query, pltpu.roll(query, CHUNK - HD, 1))[:, 0:PAIR].astype(bf16)
    qb[0:32, :] = query.astype(bf16)
    own_prod = query * new_key
    own_score = [jnp.sum(jnp.where(keep, own_prod, zero), axis=1, keepdims=True) * scale for keep in (k_0, k_1)]

    for s in range(3):
        a2[s].wait_recv()
        back = lax.rem(z + 3 - s, 4)
        swaps.append(remote(hbuf.at[c, back, :, :, la], hbuf.at[c, back, :, :, la], cs.at[s], cr.at[s], y, partner))
        swaps[-1].start()
        b2[s].wait_recv()
        back = lax.rem(x + 3 - s, 4)
        swaps.append(remote(hbuf.at[c, :, back, :, lb], hbuf.at[c, :, back, :, lb], ds.at[s], dr.at[s], y, partner))
        swaps[-1].start()

    loads[5].wait()
    loads[6].wait()

    def keys_of(core):
        ks[pl.ds(pl.multiple_of(core * 128, 128), 128), 0:PAIR] = times(hbuf[core].reshape(128, D), wk[...])

    ks[:, PAIR:] = jnp.zeros((256, 256 - PAIR), f32)
    keys_of(c)
    for cp in swaps:
        cp.wait_recv()
    keys_of(1 - c)
    fresh = high(rotated(ks[...], rec_pos, fturn_ref[...]))[:, 0:PAIR]
    prod = fresh * jnp.dot(repeat, q_fresh, preferred_element_type=f32)
    flane = lax.broadcasted_iota(jnp.int32, (256, PAIR), 1)
    score0 = jnp.sum(jnp.where(flane < HD, prod, 0.0), axis=1, keepdims=True) * scale
    score1 = jnp.sum(jnp.where(flane < HD, 0.0, prod), axis=1, keepdims=True) * scale
    wlane = lax.broadcasted_iota(jnp.int32, (256, CHUNK), 1)
    first = wlane < PAIR
    rel = jnp.where(first, wlane, wlane - PAIR) - HD
    score = jnp.where(first, score0, score1)
    shigh = high(score)
    kind = jnp.where(rel < PAGE, shigh, jnp.where(rel < 2 * PAGE, score - shigh, 1.0))
    token = jnp.where(rel < PAGE, rel, jnp.where(rel < 2 * PAGE, rel - PAGE, rel - 2 * PAGE))
    hit = jnp.logical_and(jnp.logical_and(rel >= 0, rel < 3 * PAGE), token == rec_token)
    qb[32:288, :] = jnp.where(hit, kind, 0.0).astype(bf16)
    message = over_rows(place_ref[...], qb[...])
    qsend[...] = message.reshape(128, 4, CHUNK).astype(bf16)

    def send_q(step, carry):
        other = lax.rem(me + 1 + step, 128)
        g, h = lax.div(other, 32), lax.rem(other, 32)
        remote(qsend.at[other], qin.at[me], qs, qr, g, h).start()
        return carry

    lax.fori_loop(0, 127, send_q, 0)
    qin[me] = qsend[me]

    x3 = []
    for s in range(3):
        x2[s].wait_recv()
        back = lax.rem(y + 3 - s, 4)
        x3.append(remote(mall.at[back, :, lc], mall.at[back, :, lc], x3s.at[s], x3r.at[s], y, partner))
        x3[-1].start()

    loads[7].wait()
    loads[8].wait()
    for cp in x3:
        cp.wait_recv()
    hidden = times(mall[...].reshape(128, D), inw[...])
    active = (0.5 * hidden * (1.0 + lax.erf(hidden * np.float32(math.sqrt(0.5))))).astype(bf16)

    def mlp_step(step, carry):
        lanes = pl.ds(pl.multiple_of(step * 768, 128), 768)
        out = jnp.dot(active, outw[:, lanes], preferred_element_type=f32).astype(bf16).reshape(4, 2, 16, 768)
        mp[0, :, :, lanes] = out[:, 0]
        mp[1, :, :, lanes] = out[:, 1]
        return carry

    lax.fori_loop(0, 8, mlp_step, 0)
    m_swap = remote(mp.at[1 - c], mrecv, ms, mr, y, partner)
    m_swap.start()

    for cp in w_sends:
        cp.wait_recv()
    loads[0].wait()
    own = own8[0:16, :] > 0.5
    weights = wall[:, 0:4, :].reshape(16, 128)
    w1 = high(weights)
    w2 = high(weights - w1)
    w3 = weights - w1 - w2
    for i, w in enumerate((w1, w2, w3)):
        wide = jnp.dot(w.astype(bf16), tile_ref[...], preferred_element_type=f32)
        wexp[i * 16 : (i + 1) * 16, :] = jnp.where(own, wide, 0.0).astype(bf16)

    def fold_step(step, carry):
        for u in range(4):
            chunk, part = chunk_at(step, u)
            out = jnp.dot(wexp[...], part, preferred_element_type=f32)
            out = out[0:16] + out[16:32] + out[32:48]
            for g in range(4):
                fsend[g * 32 + chunk] = out[g * 4 : (g + 1) * 4].astype(bf16)
        scatter(fsend, fin, fs, fr, step)
        return carry

    lax.fori_loop(0, 8, fold_step, 0)
    fin[me] = fsend[me]

    rest = pl.ds(0, 31)
    others = pl.ds(0, 127)
    pltpu.make_async_copy(qin.at[others], qin.at[others], qr).wait()
    lane16 = lax.broadcasted_iota(jnp.int32, (16, CHUNK), 1)
    lane_tile = lax.broadcasted_iota(jnp.int32, (16, 128), 1)
    key0 = lane16 < HD
    key1 = jnp.logical_and(lane16 >= PAIR, lane16 < PAIR + HD)

    def page_step(step, carry):
        chunks, parts, wides = [], [], []
        for u in range(4):
            chunk, part = chunk_at(step, u)
            chunks.append(chunk)
            parts.append(part)
            wides.append(jnp.concatenate([qin[g * 32 + chunk].astype(f32) for g in range(4)], axis=0))
        scores, again, flags = [], [], []
        for u in range(4):
            q2 = jnp.concatenate([jnp.where(key0, wides[u], 0.0), jnp.where(key1, wides[u], 0.0)], axis=0).astype(bf16)
            scores.append(times(q2, parts[u]))
            ex = [jnp.concatenate([exp_ref[g * 32 + chunks[u], :, n * 256 : n * 256 + 192] for g in range(4)], axis=0) for n in range(3)]
            again += [ex[0], ex[1]]
            flags += [ex[2], ex[2]]
        mask = own8[...] > 0.5
        s = jnp.where(jnp.concatenate(flags, axis=0) > 0.5, jnp.concatenate(again, axis=0), jnp.concatenate(scores, axis=0) * scale)
        s = jnp.where(mask, s, -1e30)
        top = jnp.max(s, axis=1, keepdims=True)
        thigh = high(top)
        tlow = high(top - thigh)
        p = jnp.where(mask, jnp.exp(s - (thigh + tlow)), 0.0)
        total = jnp.sum(p, axis=1, keepdims=True)
        ohigh = high(total)
        olow = total - ohigh
        p = p.astype(bf16)
        for u in range(4):
            mixed = jnp.dot(p[u * 32 : (u + 1) * 32], parts[u], preferred_element_type=f32)
            res = jnp.where(lane16 < PAIR, mixed[0:16], mixed[16:32])
            tiles = [res[:, 0:128], res[:, 128:256]]
            for i in range(2):
                rows = slice(u * 32 + i * 16, u * 32 + (i + 1) * 16)
                for n, col in enumerate((thigh, tlow, ohigh, olow)):
                    tiles[i] = jnp.where(lane_tile == i * (PAIR - 128) + n, col[rows], tiles[i])
            res = jnp.concatenate(tiles + [res[:, 256:CHUNK]], axis=1)
            for g in range(4):
                rsend[g * 32 + chunks[u]] = res[g * 4 : (g + 1) * 4].astype(bf16)
        scatter(rsend, rin, rs, rr, step)
        return carry

    exp_ref[...] = jnp.dot(qin[...].reshape(512, CHUNK), spread_ref[...], preferred_element_type=f32).reshape(128, 4, 768)
    lax.fori_loop(0, 2, page_step, 0)

    m_swap.wait_recv()
    ysend[...] = (mp[c].astype(f32) + mrecv[...].astype(f32)).astype(bf16)
    y_out = [remote(ysend.at[y_at(s)], yrecv.at[y], ys.at[s], yr.at[s], y_at(s), b) for s in range(3)]
    for cp in y_out:
        cp.start()
    yrecv[y] = ysend[y]

    lax.fori_loop(2, 8, page_step, 0)
    rin[me] = rsend[me]

    pltpu.make_async_copy(fin.at[others], fin.at[others], fr).wait()
    folded = jnp.dot(route_ref[...], fin[...].reshape(512, CHUNK), preferred_element_type=f32)
    for j in range(PPR):
        fold_ref[j] = folded[j * 32 : (j + 1) * 32].astype(bf16)
    f_score = []
    for j in range(PPR):
        fprod = folded[j * 32 : (j + 1) * 32] * query
        ok = dropped[j] > 0.5
        f_score.append([
            jnp.where(ok, jnp.sum(jnp.where(k_0, fprod, zero), axis=1, keepdims=True) * scale, -1e30),
            jnp.where(ok, jnp.sum(jnp.where(k_1, fprod, zero), axis=1, keepdims=True) * scale, -1e30),
        ])
    pltpu.make_async_copy(rin.at[others], rin.at[others], rr).wait()
    parts = jnp.dot(route_ref[...], rin[...].reshape(512, CHUNK), preferred_element_type=f32)
    tops = []
    for i in range(2):
        top = own_score[i]
        p_top = []
        for j in range(PPR):
            rows = parts[j * 32 : (j + 1) * 32]
            ok = kept[j] > 0.5
            p_top.append(jnp.where(ok, rows[:, i * PAIR : i * PAIR + 1] + rows[:, i * PAIR + 1 : i * PAIR + 2], -1e30))
            top = jnp.maximum(top, jnp.maximum(p_top[j], f_score[j][i]))
        tops.append((top, p_top))
    is_first = lane < PAIR
    mixed = zero
    total = zero
    for j in range(PPR):
        rows = parts[j * 32 : (j + 1) * 32]
        ok = kept[j] > 0.5
        w = [jnp.where(ok, jnp.exp(tops[i][1][j] - tops[i][0]), 0.0) for i in range(2)]
        e = [jnp.exp(f_score[j][i] - tops[i][0]) for i in range(2)]
        sums = [
            w[i] * (rows[:, i * PAIR + 2 : i * PAIR + 3] + rows[:, i * PAIR + 3 : i * PAIR + 4]) + e[i] for i in range(2)
        ]
        mixed = mixed + jnp.where(is_first, w[0], w[1]) * rows + jnp.where(is_first, e[0], e[1]) * folded[j * 32 : (j + 1) * 32]
        total = total + jnp.where(is_first, sums[0], sums[1])
    o = [jnp.exp(own_score[i] - tops[i][0]) for i in range(2)]
    own_exp = jnp.where(is_first, o[0], o[1])
    mixed = (mixed + own_exp * new_value) / (total + own_exp)
    attended = jnp.where(lane < HD, pltpu.roll(mixed, CHUNK - HD, 1), pltpu.roll(mixed, CHUNK - PAIR, 1))[:, 0:PAIR].astype(bf16)
    loads[9].wait()

    def dense_step(step, carry):
        lanes = pl.ds(pl.multiple_of(step * 1536, 128), 1536)
        out = jnp.dot(attended, dense[:, lanes], preferred_element_type=f32)
        apart[0, :, lanes] = out[0:16]
        apart[1, :, lanes] = out[16:32]
        return carry

    lax.fori_loop(0, 4, dense_step, 0)
    asend[...] = apart[1 - c].astype(bf16)
    a_swap = remote(asend, arecv, ats, atr, y, partner)
    a_swap.start()
    for cp in y_out:
        cp.wait_recv()
    summed = apart[c] + yrecv[0].astype(f32) + yrecv[1].astype(f32) + yrecv[2].astype(f32) + yrecv[3].astype(f32)
    a_swap.wait_recv()
    tsend[...] = (summed + arecv[...].astype(f32)).astype(bf16)

    def send_t(step, carry):
        other = lax.rem(chip + 1 + step, 16)
        remote(
            tsend.at[:, pl.ds(pl.multiple_of(other * CHUNK, 128), CHUNK)], trecv.at[chip], ts, tr, y, other * 2 + c
        ).start()
        return carry

    lax.fori_loop(0, 15, send_t, 0)
    trecv[chip] = tsend[:, pl.ds(pl.multiple_of(chip * CHUNK, 128), CHUNK)]
    pltpu.make_async_copy(trecv.at[fifteen], trecv.at[fifteen], tr).wait()
    oall[c] = jnp.sum(trecv[...].astype(f32), axis=0).astype(bf16)
    o_swap = remote(oall.at[c], oall.at[c], os, orr, y, partner)
    o_swap.start()
    o_swap.wait_recv()
    result = oall[...].astype(f32).reshape(32, CHUNK)
    sum_ref[...] = jnp.where(c == 0, result, pltpu.roll(result, PAIR, 1))[:, 0:PAIR].astype(bf16)

    for cp in a1 + b1 + a2 + b2 + swaps + w_sends + x2 + x3 + y_out + [x_swap, m_swap, a_swap, o_swap]:
        cp.wait_send()
    pltpu.make_async_copy(xb.at[0, fifteen], xb.at[0, fifteen], xs).wait()
    for ref, sem in ((qsend, qs), (fsend, fs), (rsend, rs)):
        pltpu.make_async_copy(ref.at[others], ref.at[others], sem).wait()
    pltpu.make_async_copy(trecv.at[fifteen], trecv.at[fifteen], ts).wait()


def step_call(scale, blocks, arrays):
    f32, bf16 = jnp.float32, jnp.bfloat16
    one = pltpu.SemaphoreType.DMA
    sems = lambda n: pltpu.SemaphoreType.DMA((n,))
    rows4 = pltpu.VMEM((128, 4, CHUNK), bf16)
    scratch = [
        pltpu.VMEM((128, 4, 768), f32), pltpu.VMEM((128, 128), f32), pltpu.VMEM((384, 512), bf16), pltpu.VMEM((288, 512), bf16), pltpu.VMEM((384, PAGE), f32),
        pltpu.VMEM((384, PAGE), bf16), pltpu.VMEM((4, 8, 128), f32), pltpu.VMEM((128, 192), f32),
        pltpu.VMEM((CHUNK, D), bf16), pltpu.VMEM((CHUNK, D), bf16), pltpu.VMEM((PAIR, D), bf16),
        pltpu.VMEM((PAIR, D), bf16), pltpu.VMEM((PAIR, D), bf16), pltpu.VMEM((PAIR, D), bf16),
        pltpu.VMEM((192, 2 * D), bf16), pltpu.VMEM((2, 16, 32, PAIR), bf16), pltpu.VMEM((32, D), f32), pltpu.VMEM((32, D), bf16),
        pltpu.VMEM((4, 32, D), bf16), pltpu.VMEM((2, 4, 4, NREC, D), bf16), pltpu.VMEM((4, 8, 128), f32),
        pltpu.VMEM((48, 192), bf16), pltpu.VMEM((288, CHUNK), bf16), pltpu.VMEM((256, 256), f32),
        rows4, rows4, rows4, rows4, rows4, rows4,
        pltpu.VMEM((2, 4, 16, D), bf16), pltpu.VMEM((4, 16, D), bf16), pltpu.VMEM((4, 16, D), bf16), pltpu.VMEM((4, 16, D), bf16),
        pltpu.VMEM((2, 16, D), f32), pltpu.VMEM((16, D), bf16), pltpu.VMEM((16, D), bf16), pltpu.VMEM((16, D), bf16),
        pltpu.VMEM((16, 16, CHUNK), bf16), pltpu.VMEM((2, 16, CHUNK), bf16),
        sems(10), one, one, sems(3), sems(3), sems(3), sems(3),
        sems(3), sems(3), sems(3), sems(3), sems(3), sems(3), sems(3), sems(3), sems(4), sems(4), sems(4), sems(4), sems(3), sems(3),
        one, one, one, one, one, one, one, one, sems(3), sems(3), one, one, one, one, one, one, one, one,
    ]
    return pl.pallas_call(
        functools.partial(step_kernel, scale),
        out_shape=[jax.ShapeDtypeStruct((32, PAIR), bf16), jax.ShapeDtypeStruct((PPR, 32, CHUNK), bf16)],
        in_specs=[VMEM_SPEC] * len(blocks) + [pl.BlockSpec(memory_space=pl.ANY)] * len(arrays),
        out_specs=[VMEM_SPEC] * 2,
        scratch_shapes=scratch,
        compiler_params=pltpu.CompilerParams(collective_id=0, has_side_effects=True, vmem_limit_bytes=58 << 20),
        name="decode_step",
    )(*blocks, *arrays)


def on_device(
    new_hidden,
    attn_gain,
    mlp_gain,
    qkv_weight,
    dense_weight,
    in_weight,
    out_weight,
    page_store,
    held_states,
    fold_weights,
    page_table,
    lengths,
    keep_slots,
    fold_index,
    recompute_list,
):
    rows = lengths.shape[0]
    pages_dev = page_store.shape[0]
    scale = 1.0 / math.sqrt(HD)
    bf16 = jnp.bfloat16
    lane = np.arange(CHUNK)[:, None]
    tokens = np.arange(pages_dev * PAGE)[None, :] % PAGE
    spread = np.zeros((CHUNK, 3, 256), np.float32)
    for i in range(2):
        t = lane - (i * PAIR + HD)
        spread[:, i, : pages_dev * PAGE] = (t == tokens) | (t == tokens + PAGE)
    spread[:, 2, : pages_dev * PAGE] = lane - HD == tokens + 2 * PAGE
    spread = jnp.asarray(spread.reshape(CHUNK, 768), bf16)
    tile = jnp.asarray((np.arange(128)[:, None] == tokens).astype(np.float32), bf16)
    turn = jnp.asarray(rotary_rows(CHUNK, (0, PAIR)))
    fresh_turn = jnp.asarray(rotary_rows(256, (0, HD)))

    blocks = (
        new_hidden, held_states.reshape(NREC, D), attn_gain.reshape(1, D), mlp_gain.reshape(1, D), fold_weights, page_table.T,
        lengths.reshape(1, rows), keep_slots.T, fold_index.T, recompute_list.T, spread, tile, turn, fresh_turn,
    )
    arrays = (qkv_weight.T, dense_weight, in_weight.T, out_weight, page_store.reshape(pages_dev * PAGE, 2 * D))
    update, folded = step_call(scale, blocks, arrays)
    return (update, folded.transpose(1, 0, 2))


def solution(mesh):
    in_specs = (
        P("pages", "blk"),
        P(),
        P(),
        P(None, "blk"),
        P("blk", None),
        P(None, ("pages", "blk")),
        P(("pages", "blk"), None),
        P(("pages", "blk"), None, None),
        P(("pages", "blk"), None, None),
        P(),
        P(),
        P("pages"),
        P("pages", None),
        P("pages", None),
        P("pages", None),
    )
    out_specs = (P("pages", "blk"), P("pages", None, "blk"))
    return jax.shard_map(
        on_device, mesh=mesh, in_specs=in_specs, out_specs=out_specs, check_vma=False
    )
```
